32 devices in a mesh: dp: 16 (over z, y, x), tensor: 2 (over core).
Axes of the slice: x: 2, y: 2, z: 4, core: 2. Of those that a mesh axis runs over, the one named last changes fastest.
Arguments:
- tokens: bfloat16 [4096, 1024], P(('dp', 'tensor'))
- cotangent: bfloat16 [4096, 1024], P(('dp', 'tensor')), may hold values from -6 to 6
- route: int32 [4096], P(('dp', 'tensor')), may hold values from 0 to 4095, as said below
- lengths: int32 [16, 4], P('dp'), may hold values from 1 to 128, 224 in all within a row
- clip_tau: int32 [1], replicated, may hold values from 2 to 11
- attn_norm_gain: bfloat16 [1024], replicated, may hold values from 0.5 to 1.5
- attn_norm_bias: bfloat16 [1024], replicated, may hold values from -4 to 4
- qkv_weight: bfloat16 [1024, 3, 1024], P(None, None, 'tensor')
- qv_bias: bfloat16 [2, 1024], P(None, 'tensor'), may hold values from -6 to 6
- out_weight: bfloat16 [1024, 1024], P('tensor'), may hold values from -1.5 to 1.5
- out_bias: bfloat16 [1024], replicated, may hold values from -4 to 4
- mlp_norm_gain: bfloat16 [1024], replicated, may hold values from 0.5 to 1.5
- mlp_norm_bias: bfloat16 [1024], replicated, may hold values from -4 to 4
- up_weight: bfloat16 [1024, 4096], P(None, 'tensor'), may hold values from -0.1875 to 0.1875
- up_bias: bfloat16 [4096], P('tensor'), may hold values from -6 to 6
- down_weight: bfloat16 [4096, 1024], P('tensor'), may hold values from -0.09375 to 0.09375
- down_bias: bfloat16 [1024], replicated, may hold values from -4 to 4
Outputs:
- out_tokens: bfloat16 [4096, 1024], P(('dp', 'tensor'))
- grad_tokens: bfloat16 [4096, 1024], P(('dp', 'tensor'))
- grad_qkv: float32 [1024, 3, 1024], P('dp', None, 'tensor')
- grad_out_weight: float32 [1024, 1024], P('tensor', 'dp')
- grad_up_weight: float32 [1024, 4096], P('dp', 'tensor')
- grad_down_weight: float32 [4096, 1024], P('tensor', 'dp')
- grad_qv_bias: float32 [2, 1024], replicated
- grad_up_bias: float32 [4096], replicated
- grad_vectors: float32 [6, 1024], replicated
- head_factor: float32 [16], P('tensor')
- clipped_qk: bfloat16 [1024, 2, 1024], P(None, None, 'tensor')
- clipped_q_bias: bfloat16 [1024], P('tensor')
The draws below stay inside these ranges and needn't reach their ends.
Inputs may be any that keep to these rules, and one draw needn't show every extreme that they name: `route`: every packed position is named once. A token stored on device (d, t) of the dp and tensor axes goes to a position held by some device (d', t), and each such pair of devices gets exactly 8 tokens. Each group's lengths add up to 224; the longest of each group is exactly 128.
All inputs are finite; a program needn't handle non-finite values.
Results may differ from the reference program's by a relative error of at most 0.015.
Values may be sent and summed in bfloat16 or wider, within the bound.
No kernel may reach another device: no remote copies, remote signals or barrier semaphores. Data moves between devices by JAX's collectives and lax.ppermute only.
A program may use at most 128 MiB of HBM per device.

```python
import math
import jax
import jax.numpy as jnp
import numpy as np
from jax import lax

D = 1024
HEADS = 16
HD = 64
FF = 4096
TOK_DEV = 128
SEGS = 4
SPLIT = 2
GROUPS = 16
GROUP = 256
LIVE = 224
TOKENS = 4096


def destinations(key):
    base_key = jax.random.fold_in(key, 101)
    first_key = jax.random.fold_in(base_key, 1)
    second_key = jax.random.fold_in(base_key, 2)
    device_count = GROUPS * SPLIT
    per_peer = TOK_DEV // GROUPS
    spread_order = jax.vmap(lambda sub_key: jax.random.permutation(sub_key, TOK_DEV))(jax.random.split(first_key, device_count))
    landing_order = jax.vmap(lambda sub_key: jax.random.permutation(sub_key, TOK_DEV))(jax.random.split(second_key, device_count))
    source_dev = jnp.arange(device_count, dtype=jnp.int32)[:, None]
    target_group = spread_order // per_peer
    target_dev = target_group * SPLIT + source_dev % SPLIT
    slot_index = source_dev // SPLIT * per_peer + spread_order % per_peer
    row_index = landing_order[target_dev, slot_index]
    return (target_dev * TOK_DEV + row_index).reshape(-1).astype(jnp.int32)


def common_direction(key):
    return jax.random.normal(jax.random.fold_in(key, 13), (D,), jnp.float32)


def draw_route(key, part):
    return destinations(key)


def draw_tokens(key, part):
    group_index = destinations(key) // GROUP
    noise_key = jax.random.fold_in(key, 11)
    noise = jax.random.normal(noise_key, (TOKENS, D), jnp.float32)
    common_dir = common_direction(key)
    amplitude = 3.0 * group_index.astype(jnp.float32) / max(GROUPS - 1, 1)
    return (noise + amplitude[:, None] * common_dir[None, :]).astype(jnp.bfloat16)


def draw_qkv_weight(key, part):
    entry_key = jax.random.fold_in(key, 17)
    entries = jax.random.normal(entry_key, (D, 3, D), jnp.float32)
    ladder_rank = jax.random.permutation(jax.random.fold_in(key, 19), HEADS).astype(jnp.float32)
    head_scale = 1.0 + ladder_rank / max(HEADS - 1, 1)
    query_scale = jnp.repeat(head_scale, HD)
    column_scale = jnp.stack([query_scale, jnp.ones((D,), jnp.float32), jnp.ones((D,), jnp.float32)])
    base = entries * D ** (-0.5) * column_scale[None, :, :]
    common_dir = common_direction(key)
    shared_cols = jax.random.normal(jax.random.fold_in(key, 23), (D,), jnp.float32)
    bump_scale = (200.0 / HD) ** 0.5 / D
    bump = bump_scale * common_dir[:, None] * shared_cols[None, :]
    return base.at[:, 0, :].add(bump).at[:, 1, :].add(bump).astype(jnp.bfloat16)


def block_levels(stream_key, shape, pieces, least, top_value):
    def one(axis_at, blocks):
        heights = jax.random.uniform(jax.random.fold_in(jax.random.fold_in(stream_key, 6), axis_at), (blocks,), jnp.float32, least / len(pieces), top_value / len(pieces))
        return jnp.repeat(jnp.exp(heights), shape[axis_at] // blocks).reshape((-1,) + (1,) * (len(shape) - axis_at - 1))

    loudness = one(*pieces[0])
    for cut in pieces[1:]:
        loudness = loudness * one(*cut)
    return loudness


def length_profile(number_of, total, bound, lean):
    loads = [(1 << 20) // math.isqrt(standing ** lean) + 1 for standing in range(2, number_of + 1)]
    spare, given = total - bound - (number_of - 1), [1] * (number_of - 1)
    while spare > 0:
        movable = [i for i in range(number_of - 1) if given[i] < bound]
        mass, remaining = sum([loads[i] for i in movable]), spare
        for i in movable:
            extra = min(bound - given[i], max(1, remaining * loads[i] // mass), spare)
            given[i] = given[i] + extra
            spare = spare - extra
    return np.array([bound] + given)


def uneven(own_key, number_of, total, limit, skew):
    if number_of == 2:
        one = jax.random.randint(own_key, (), max(1, total - limit), min(limit, total - 1) + 1)
        return jnp.stack([one, total - one])
    sizes = jnp.asarray(length_profile(number_of, total, limit, skew), jnp.int32)
    couples = (number_of - 1) // 2
    donor, receiver = sizes[1:1 + 2 * couples:2], sizes[2:2 + 2 * couples:2]
    room = jnp.minimum(donor - 1, limit - receiver)
    moved = jax.random.randint(jax.random.fold_in(own_key, 1), (couples,), 0, 1 << 20) % (room + 1)
    sizes = sizes.at[1:1 + 2 * couples:2].set(donor - moved).at[2:2 + 2 * couples:2].set(receiver + moved)
    return sizes[jax.random.permutation(jax.random.fold_in(own_key, 2), number_of)]


def gaussian(rng, extent, width, most, shards=(), kind=jnp.bfloat16):
    factor_of = block_levels(rng, extent, shards, -0.22, 0.18) if shards else 1.0
    array = jax.random.normal(rng, extent, jnp.float32) * width * factor_of
    return jnp.minimum(jnp.maximum(array, -most), most).astype(kind)


def setup_inputs(seed: int = 0) -> dict:
    arg_keys = jax.random.split(jax.random.key(seed), 18)
    return {
        "tokens": draw_tokens(jax.random.fold_in(arg_keys[17], 71), 0),
        "cotangent": gaussian(arg_keys[1], (TOKENS, D), 1.0, 6.0, ((0, 32),)),
        "route": draw_route(jax.random.fold_in(arg_keys[17], 71), 0),
        "lengths": jax.vmap(lambda own: uneven(own, SEGS, LIVE, TOK_DEV, 2))(jax.random.split(arg_keys[3], GROUPS)).reshape((GROUPS, SEGS)).astype(jnp.int32),
        "clip_tau": jax.random.randint(arg_keys[4], (1,), 2, 12).astype(jnp.int32),
        "attn_norm_gain": jnp.clip(1.0 + 0.1 * jax.random.normal(arg_keys[5], (D,), jnp.float32), 0.5, 1.5).astype(jnp.bfloat16),
        "attn_norm_bias": gaussian(arg_keys[6], (D,), 0.3, 4.0),
        "qkv_weight": draw_qkv_weight(jax.random.fold_in(arg_keys[17], 71), 0),
        "qv_bias": gaussian(arg_keys[8], (2, D), 0.5, 6.0, ((1, 2),)),
        "out_weight": gaussian(arg_keys[9], (D, D), (D // 64) ** -0.5, 1.5, ((0, 2),)),
        "out_bias": gaussian(arg_keys[10], (D,), 0.3, 4.0),
        "mlp_norm_gain": jnp.clip(1.0 + 0.1 * jax.random.normal(arg_keys[11], (D,), jnp.float32), 0.5, 1.5).astype(jnp.bfloat16),
        "mlp_norm_bias": gaussian(arg_keys[12], (D,), 0.3, 4.0),
        "up_weight": gaussian(arg_keys[13], (D, FF), D ** -0.5, 0.1875, ((1, 2),)),
        "up_bias": gaussian(arg_keys[14], (FF,), 0.5, 6.0, ((0, 2),)),
        "down_weight": gaussian(arg_keys[15], (FF, D), FF ** -0.5, 0.09375, ((0, 2),)),
        "down_bias": gaussian(arg_keys[16], (D,), 0.3, 4.0),
    }


@jax.custom_vjp
def low(v):
    return lax.optimization_barrier(v.astype(jnp.bfloat16)).astype(jnp.float32)

@jax.custom_vjp
def low_back(v):
    return v

def low_keep(v):
    return (low(v), None)

def low_pass(kept, grad):
    return (grad,)

def back_keep(v):
    return (v, None)

def back_low(kept, grad):
    return (low(grad),)
low.defvjp(low_keep, low_pass)
low_back.defvjp(back_keep, back_low)
epsilon = 1e-05
masked_value = -1e+30
highest = lax.Precision.HIGHEST
gelu_coef = 0.7978845608028654

def layer_norm(values, scale_vec, shift_vec):
    row_mean = lax.optimization_barrier(jnp.mean(values, axis=-1, keepdims=True))
    centered = values - row_mean
    variance = lax.optimization_barrier(jnp.mean(centered * centered, axis=-1, keepdims=True))
    return centered * lax.rsqrt(variance + epsilon) * scale_vec + shift_vec

def gelu_tanh(values):
    return 0.5 * values * (1.0 + jnp.tanh(gelu_coef * (values + 0.044715 * values * values * values)))

def allowed_pairs(seq_lengths, row_start, row_stop):
    seq_ends = jnp.cumsum(seq_lengths, dtype=jnp.int32)
    key_pos = jnp.arange(row_stop, dtype=jnp.int32)
    sequence_id = lax.optimization_barrier(jnp.sum((key_pos[:, None] >= seq_ends[None, :]).astype(jnp.int32), axis=1, dtype=jnp.int32))
    live_rows = key_pos < seq_ends[-1]
    query_pos = key_pos[row_start:]
    same_seq = sequence_id[row_start:, None] == sequence_id[None, :]
    causal = key_pos[None, :] <= query_pos[:, None]
    diagonal = key_pos[None, :] == query_pos[:, None]
    allowed = causal & same_seq & live_rows[row_start:, None] | diagonal
    return (allowed, live_rows[row_start:])

def group_forward(group_rows, seq_lengths, params):
    attn_gain, attn_shift, qkv_mat, qv_vec, out_mat, out_vec, mlp_gain, mlp_shift, up_mat, up_vec, down_mat, down_vec = params
    allowed, live_query = allowed_pairs(seq_lengths, 0, GROUP)
    normed = low(layer_norm(group_rows, attn_gain, attn_shift))
    bias_rows = jnp.stack([qv_vec[0], jnp.zeros_like(qv_vec[0]), qv_vec[1]])
    projected = jnp.einsum('td,dce->tce', normed, qkv_mat, precision=highest) + bias_rows
    projected = low_back(low(projected)).reshape(GROUP, 3, HEADS, HD)
    queries = projected[:, 0]
    keys_all = projected[:, 1]
    values_all = projected[:, 2]
    scores = low_back(jnp.einsum('qhd,khd->hqk', queries, keys_all, precision=highest) * 0.125)
    masked = jnp.where(allowed[None], scores, masked_value)
    row_max = lax.optimization_barrier(jnp.max(masked, axis=-1, keepdims=True))
    exp_scores = jnp.exp(masked - row_max)
    probabilities = exp_scores / lax.optimization_barrier(jnp.sum(exp_scores, axis=-1, keepdims=True))
    live_pairs = allowed & live_query[:, None]
    head_top = lax.optimization_barrier(jnp.max(jnp.where(live_pairs[None], scores, masked_value), axis=(1, 2)))
    context = jnp.einsum('hqk,khd->qhd', low(probabilities), values_all, precision=highest).reshape(GROUP, D)
    context = low_back(low(context))
    attended = low_back(jnp.dot(context, out_mat, precision=highest))
    middle = group_rows + attended + out_vec
    normed_mid = low(layer_norm(middle, mlp_gain, mlp_shift))
    pre_act = low_back(jnp.dot(normed_mid, up_mat, precision=highest) + up_vec)
    activated = low(gelu_tanh(pre_act))
    result = middle + jnp.dot(activated, down_mat, precision=highest) + down_vec
    return (result, head_top)

def reference(tokens, cotangent, route, lengths, clip_tau, attn_norm_gain, attn_norm_bias, qkv_weight, qv_bias, out_weight, out_bias, mlp_norm_gain, mlp_norm_bias, up_weight, up_bias, down_weight, down_bias):
    arrival = jnp.argsort(route).astype(jnp.int32)
    packed = tokens.astype(jnp.float32)[arrival]
    packed_grad = cotangent.astype(jnp.float32)[arrival]
    params = tuple((member.astype(jnp.float32) for member in (attn_norm_gain, attn_norm_bias, qkv_weight, qv_bias, out_weight, out_bias, mlp_norm_gain, mlp_norm_bias, up_weight, up_bias, down_weight, down_bias)))

    def forward(rows_all, weights):
        grouped = rows_all.reshape(GROUPS, GROUP, D)

        def one_group(group_pair):
            return group_forward(group_pair[0], group_pair[1], weights)
        results, group_tops = lax.map(jax.checkpoint(one_group), (grouped, lengths))
        return (results.reshape(TOKENS, D), lax.optimization_barrier(jnp.max(group_tops, axis=0)))
    result, pullback, head_top = jax.vjp(forward, packed, params, has_aux=True)
    grad_rows, weight_grads = pullback(packed_grad)
    grad_attn_gain, grad_attn_shift, grad_qkv, grad_qv, grad_out, grad_out_vec, grad_mlp_gain, grad_mlp_shift, grad_up, grad_up_vec, grad_down, grad_down_vec = weight_grads
    out_tokens = result[route].astype(jnp.bfloat16)
    grad_tokens = grad_rows[route].astype(jnp.bfloat16)
    grad_vectors = jnp.stack([grad_attn_gain, grad_attn_shift, grad_out_vec, grad_mlp_gain, grad_mlp_shift, grad_down_vec])
    threshold = clip_tau[0].astype(jnp.float32)
    head_factor = jnp.sqrt(threshold / jnp.maximum(head_top, threshold))
    column_factor = jnp.repeat(head_factor, HD)
    clipped_qk = (qkv_weight[:, 0:2].astype(jnp.float32) * column_factor).astype(jnp.bfloat16)
    clipped_q_bias = (qv_bias[0].astype(jnp.float32) * column_factor).astype(jnp.bfloat16)
    return (out_tokens, grad_tokens, grad_qkv, grad_out, grad_up, grad_down, grad_qv, grad_up_vec, grad_vectors, head_factor, clipped_qk, clipped_q_bias)
```

```python
import jax
import jax.numpy as jnp
from jax import lax
from jax.sharding import PartitionSpec as P

HD = 64
AG_BITS = (0, 2)

epsilon = 1e-05
masked_value = -1e30
gelu_coef = 0.7978845608028654
F32 = jnp.float32
BF16 = jnp.bfloat16


def norm_stats(values):
    row_mean = jnp.mean(values, axis=-1, keepdims=True)
    centered = values - row_mean
    variance = jnp.mean(centered * centered, axis=-1, keepdims=True)
    inv = lax.rsqrt(variance + epsilon)
    return centered * inv, inv


def norm_grad(xhat, inv, gain, grad):
    scaled = grad * gain
    a = jnp.mean(scaled, axis=-1, keepdims=True)
    b = jnp.mean(scaled * xhat, axis=-1, keepdims=True)
    return inv * (scaled - a - xhat * b)


def gelu_parts(p):
    th = jnp.tanh(gelu_coef * (p + 0.044715 * p * p * p))
    act = 0.5 * p * (1.0 + th)
    slope = 0.5 * (1.0 + th) + 0.5 * p * (1.0 - th * th) * (
        gelu_coef * (1.0 + 3.0 * 0.044715 * p * p)
    )
    return act, slope


def allowed_pairs(seq_lengths, pos):
    seq_ends = jnp.cumsum(seq_lengths, dtype=jnp.int32)
    seq_id = jnp.sum(
        (pos[:, None] >= seq_ends[None, :]).astype(jnp.int32), axis=1, dtype=jnp.int32
    )
    live = pos < seq_ends[-1]
    same = seq_id[:, None] == seq_id[None, :]
    causal = pos[None, :] <= pos[:, None]
    diagonal = pos[None, :] == pos[:, None]
    return causal & same & live[:, None] | diagonal, live


def dot(a, b, ca, cb):
    return lax.dot_general(a, b, (((ca,), (cb,)), ((), ())), preferred_element_type=F32)


def heads_of(x):
    return x.reshape(x.shape[0], x.shape[1] // HD, HD)


def attention(q, k, v, allowed, live):
    scores = jnp.einsum("qhd,khd->hqk", q, k, preferred_element_type=F32) * 0.125
    masked = jnp.where(allowed[None], scores, masked_value)
    row_max = jnp.max(masked, axis=-1, keepdims=True)
    e = jnp.exp(masked - row_max)
    probs = e / jnp.sum(e, axis=-1, keepdims=True)
    context = jnp.einsum(
        "hqk,khd->qhd", probs.astype(BF16), v, preferred_element_type=F32
    ).reshape(q.shape[0], -1).astype(BF16)
    top = jnp.max(jnp.where((allowed & live[:, None])[None], scores, masked_value), axis=(1, 2))
    return probs, context, top


def attention_grad(q, k, v, probs, grad_context):
    g = jnp.einsum("qhd,khd->hqk", grad_context, v, preferred_element_type=F32)
    row_dot = jnp.sum(probs * g, axis=-1, keepdims=True)
    ds = (probs * (g - row_dot)).astype(BF16)
    gq = jnp.einsum("hqk,khd->qhd", ds, k, preferred_element_type=F32) * 0.125
    gk = jnp.einsum("hqk,qhd->khd", ds, q, preferred_element_type=F32) * 0.125
    gv = jnp.einsum("hqk,qhd->khd", probs.astype(BF16), grad_context, preferred_element_type=F32)
    rows = q.shape[0]
    return [x.astype(BF16).reshape(rows, -1) for x in (gq, gk, gv)]


def local(
    tokens,
    cotangent,
    route,
    lengths,
    clip_tau,
    attn_norm_gain,
    attn_norm_bias,
    qkv_weight,
    qv_bias,
    out_weight,
    out_bias,
    mlp_norm_gain,
    mlp_norm_bias,
    up_weight,
    up_bias,
    down_weight,
    down_bias,
):
    n_dp = lax.axis_size("dp")
    n_bits = n_dp.bit_length() - 1
    rs_bits = [b for b in range(n_bits) if b not in AG_BITS]
    masks = [1 << AG_BITS[0], 1 << AG_BITS[1], (1 << AG_BITS[0]) | (1 << AG_BITS[1])]
    me = lax.axis_index("dp")
    core = lax.axis_index("tensor")
    rows = tokens.shape[0]
    width = tokens.shape[1]
    cols = qkv_weight.shape[2]
    hidden = up_weight.shape[1]
    quarter_cols = cols // 4
    quarter_hidden = hidden // 4
    bit0 = (me >> AG_BITS[0]) & 1
    bit1 = (me >> AG_BITS[1]) & 1
    quarter = bit0 + 2 * bit1

    def swap(x):
        return lax.ppermute(x, "tensor", [(0, 1), (1, 0)])

    def hop(x, mask):
        return lax.ppermute(x, "dp", [(i, i ^ mask) for i in range(n_dp)])

    def both(x):
        return jnp.concatenate([x, swap(x)], axis=0)

    def share(own):
        got = jnp.stack([hop(own[:rows], m) for m in masks])
        other = swap(got)
        rest = jnp.concatenate([got, other], axis=1).reshape(-1, own.shape[1])
        return jnp.concatenate([own, rest], axis=0)

    def flip(x):
        return jnp.concatenate([x[rows:], x[:rows]], axis=0)

    f = lambda x: x.astype(F32)
    w_qkv = jnp.transpose(qkv_weight, (1, 0, 2))

    dest_dev = route // (2 * rows)
    dest_row = route % rows
    earlier = jnp.arange(rows)[None, :] < jnp.arange(rows)[:, None]
    same_dest = dest_dev[None, :] == dest_dev[:, None]
    rank = dest_dev * (rows // n_dp) + jnp.sum((earlier & same_dest).astype(jnp.int32), axis=1)
    pick = (rank[None, :] == jnp.arange(rows)[:, None]).astype(BF16)
    send_tok = dot(pick, tokens, 1, 0).astype(BF16)
    send_cot = dot(pick, cotangent, 1, 0).astype(BF16)
    send_row = dot(pick, dest_row.astype(BF16)[:, None] * jnp.ones((1, 128), BF16), 1, 0).astype(BF16)

    def exchange(x):
        return lax.all_to_all(x, "dp", split_axis=0, concat_axis=0, tiled=True)

    got_tok = exchange(jnp.concatenate([send_tok, send_row], axis=1))
    got_cot = exchange(send_cot)
    got_row = got_tok[:, width].astype(jnp.int32)
    place = (got_row[None, :] == jnp.arange(rows)[:, None]).astype(BF16)
    x_mine = dot(place, got_tok[:, :width], 1, 0).astype(BF16)
    cot_mine = dot(place, got_cot, 1, 0).astype(BF16)
    x_all = f(both(x_mine))
    cot_all = both(cot_mine)
    cot_four = share(cot_all)

    pos_half = jnp.arange(rows, dtype=jnp.int32)
    pos = jnp.concatenate([pos_half + core * rows, pos_half + (1 - core) * rows])
    len_rows = [lengths[0]] + [hop(lengths, m)[0] for m in masks]
    allowed, live = allowed_pairs(len_rows[0], pos)

    xhat, inv = norm_stats(x_all)
    normed = (xhat * f(attn_norm_gain) + f(attn_norm_bias)).astype(BF16)
    normed_four = share(normed)
    q_bias, v_bias = f(qv_bias[0]), f(qv_bias[1])
    q = (dot(normed, w_qkv[0], 1, 0) + q_bias).astype(BF16)
    k = dot(normed, w_qkv[1], 1, 0).astype(BF16)
    v = (dot(normed, w_qkv[2], 1, 0) + v_bias).astype(BF16)
    qh, kh, vh = heads_of(q), heads_of(k), heads_of(v)
    probs, context, head_top = attention(qh, kh, vh, allowed, live)
    part = dot(context, out_weight, 1, 0).astype(BF16)
    part_other = flip(swap(part))
    middle = x_all + (f(part) + f(part_other)) + f(out_bias)
    mhat, minv = norm_stats(middle)
    normed_mid = (mhat * f(mlp_norm_gain) + f(mlp_norm_bias)).astype(BF16)
    mid_four = share(normed_mid)

    pre = dot(normed_mid, up_weight, 1, 0) + f(up_bias)
    act, slope = gelu_parts(pre)
    act = act.astype(BF16)
    grad_pre = (dot(cot_all, down_weight, 1, 1) * slope).astype(BF16)
    gmid_part = dot(grad_pre, up_weight, 1, 1).astype(BF16)
    gmid_norm = f(gmid_part) + f(flip(swap(gmid_part)))
    mlp_part = dot(act, down_weight, 1, 0).astype(BF16)
    mlp_mine = f(mlp_part[:rows]) + f(swap(mlp_part[rows:]))
    final_mine = middle[:rows] + mlp_mine + f(down_bias)
    grad_mid = f(cot_all) + norm_grad(mhat, minv, f(mlp_norm_gain), gmid_norm)
    grad_attn = grad_mid.astype(BF16)
    gattn_four = share(grad_attn)

    grad_context = dot(grad_attn, out_weight, 1, 1).astype(BF16)
    gq, gk, gv = attention_grad(qh, kh, vh, probs, heads_of(grad_context))
    gnorm_part = (
        dot(gq, w_qkv[0], 1, 1) + dot(gk, w_qkv[1], 1, 1) + dot(gv, w_qkv[2], 1, 1)
    ).astype(BF16)
    gnorm = f(gnorm_part[:rows]) + f(swap(gnorm_part[rows:]))
    grad_in = grad_mid[:rows] + norm_grad(xhat[:rows], inv[:rows], f(attn_norm_gain), gnorm)

    def quarter_of(x, axis, size):
        return lax.dynamic_slice_in_dim(x, quarter * size, size, axis)

    up_q = quarter_of(up_weight, 1, quarter_hidden)
    down_q = quarter_of(down_weight, 0, quarter_hidden)
    pre_q = dot(mid_four, up_q, 1, 0) + f(quarter_of(up_bias, 0, quarter_hidden))
    act_q, slope_q = gelu_parts(pre_q)
    act_q = act_q.astype(BF16)
    gpre_q = (dot(cot_four, down_q, 1, 1) * slope_q).astype(BF16)
    g_down = dot(cot_four, act_q, 0, 0)
    g_up = dot(mid_four, gpre_q, 0, 0)

    w_q = quarter_of(w_qkv, 2, quarter_cols)
    out_q = quarter_of(out_weight, 0, quarter_cols)
    bias_q = quarter_of(qv_bias, 1, quarter_cols)
    q4 = (dot(normed_four, w_q[0], 1, 0) + f(bias_q[0])).astype(BF16)
    k4 = dot(normed_four, w_q[1], 1, 0).astype(BF16)
    v4 = (dot(normed_four, w_q[2], 1, 0) + f(bias_q[1])).astype(BF16)
    gc4 = dot(gattn_four, out_q, 1, 1).astype(BF16)
    grads4, ctx4 = [], []
    for g in range(4):
        s = slice(g * 2 * rows, (g + 1) * 2 * rows)
        al, lv = allowed_pairs(len_rows[g], pos)
        hq, hk, hv = heads_of(q4[s]), heads_of(k4[s]), heads_of(v4[s])
        pr, cx, _ = attention(hq, hk, hv, al, lv)
        ctx4.append(cx)
        grads4.append(jnp.concatenate(attention_grad(hq, hk, hv, pr, heads_of(gc4[s])), axis=1))
    g_qkv = dot(normed_four, jnp.concatenate(grads4, axis=0), 0, 0)
    g_out = dot(gattn_four, jnp.concatenate(ctx4, axis=0), 0, 0)

    def reduce_rows(g):
        w = g.shape[1]
        cur = g.reshape((2,) * n_bits + (width // n_dp, w))
        for b in rs_bits:
            axis = n_bits - 1 - b
            mine = (me >> b) & 1
            keep = lax.dynamic_index_in_dim(cur, mine, axis, keepdims=True)
            send = lax.dynamic_index_in_dim(cur, 1 - mine, axis, keepdims=True)
            shape = send.shape
            send = send.astype(BF16).reshape(-1, w)
            cur = keep + f(hop(send, 1 << b)).reshape(shape)
        cur = cur.reshape(2, 2, width // n_dp, w).reshape(4, width // n_dp, w).astype(BF16)
        pieces = [lax.dynamic_index_in_dim(cur, quarter, 0, keepdims=False)]
        for j, m in enumerate(masks):
            pieces.append(hop(lax.dynamic_index_in_dim(cur, quarter ^ (j + 1), 0, keepdims=False), m))
        stacked = jnp.stack(pieces)
        return [
            f(lax.dynamic_index_in_dim(stacked, quarter ^ j, 0, keepdims=False)) for j in range(4)
        ]

    down_pieces = reduce_rows(g_down)
    up_pieces = reduce_rows(g_up)
    attn_pieces = reduce_rows(jnp.concatenate([g_qkv, g_out], axis=1))
    grad_down = jnp.concatenate(down_pieces, axis=1).T
    grad_up = jnp.concatenate(up_pieces, axis=1)
    grad_qkv = jnp.transpose(
        jnp.stack(
            [
                jnp.concatenate(
                    [p[:, c * quarter_cols : (c + 1) * quarter_cols] for p in attn_pieces], axis=1
                )
                for c in range(3)
            ]
        ),
        (1, 0, 2),
    )
    grad_out = jnp.concatenate([p[:, 3 * quarter_cols :] for p in attn_pieces], axis=1).T

    sum0 = lambda x: jnp.sum(f(x), axis=0)
    mid_grad_mine = gmid_norm[:rows]
    vectors = jnp.stack(
        [
            jnp.sum(gnorm * xhat[:rows], axis=0),
            jnp.sum(gnorm, axis=0),
            jnp.sum(grad_mid[:rows], axis=0),
            jnp.sum(mid_grad_mine * mhat[:rows], axis=0),
            jnp.sum(mid_grad_mine, axis=0),
            sum0(cot_mine),
        ]
    )
    own_sums = jnp.concatenate([sum0(gq), sum0(gv), sum0(grad_pre)])
    n_vec = vectors.size
    sums = jnp.concatenate([vectors.reshape(-1), own_sums])
    tops = jnp.pad(head_top, (0, 128 - head_top.shape[0]), constant_values=masked_value)
    n_sum = sums.size
    msg = jnp.concatenate([sums, tops])
    for b in range(n_bits):
        got = hop(msg, 1 << b)
        msg = jnp.concatenate([msg[:n_sum] + got[:n_sum], jnp.maximum(msg[n_sum:], got[n_sum:])])
    global_top = msg[n_sum : n_sum + head_top.shape[0]]
    other = swap(msg[:n_sum])
    vector_sum = (msg[:n_vec] + other[:n_vec]).reshape(6, width)
    own, oth = msg[n_vec:n_sum], other[n_vec:]
    first = jnp.where(core == 0, own, oth)
    second = jnp.where(core == 0, oth, own)
    qv_sum = jnp.stack(
        [
            jnp.concatenate([first[:cols], second[:cols]]),
            jnp.concatenate([first[cols : 2 * cols], second[cols : 2 * cols]]),
        ]
    )
    up_sum = jnp.concatenate([first[2 * cols :], second[2 * cols :]])

    def back(x):
        y = dot(place, x.astype(BF16), 0, 0).astype(BF16)
        return dot(pick, exchange(y), 0, 0).astype(BF16)

    out_tokens = back(final_mine)
    grad_tokens = back(grad_in)

    threshold = clip_tau[0].astype(F32)
    head_factor = jnp.sqrt(threshold / jnp.maximum(global_top, threshold))
    column_factor = jnp.repeat(head_factor, HD)
    clipped_qk = (f(qkv_weight[:, 0:2]) * column_factor).astype(BF16)
    clipped_q_bias = (f(qv_bias[0]) * column_factor).astype(BF16)
    return (
        out_tokens,
        grad_tokens,
        grad_qkv,
        grad_out,
        grad_up,
        grad_down,
        qv_sum,
        up_sum,
        vector_sum,
        head_factor,
        clipped_qk,
        clipped_q_bias,
    )

def solution(mesh):
    placed = (
        P(("dp", "tensor"), None),
        P(("dp", "tensor"), None),
        P(("dp", "tensor")),
        P("dp", None),
        P(),
        P(),
        P(),
        P(None, None, "tensor"),
        P(None, "tensor"),
        P("tensor", None),
        P(),
        P(),
        P(),
        P(None, "tensor"),
        P("tensor"),
        P("tensor", None),
        P(),
    )
    return jax.shard_map(
        local,
        mesh=mesh,
        in_specs=placed,
        out_specs=(
            P(("dp", "tensor"), None),
            P(("dp", "tensor"), None),
            P("dp", None, "tensor"),
            P("tensor", "dp"),
            P("dp", "tensor"),
            P("tensor", "dp"),
            P(),
            P(),
            P(),
            P("tensor"),
            P(None, None, "tensor"),
            P("tensor"),
        ),
        check_vma=False,
    )
```

```python
import functools
import jax
import jax.numpy as jnp
from jax import lax
from jax.experimental import pallas as pl
from jax.experimental.pallas import tpu as pltpu
from jax.sharding import PartitionSpec as P

HD = 64
AG_BITS = (0, 2)
PAD = 128

epsilon = 1e-05
masked_value = -1e30
gelu_coef = 0.7978845608028654
F32 = jnp.float32
BF16 = jnp.bfloat16
I32 = jnp.int32


def f(x):
    return x.astype(F32)


def dot(a, b, ca, cb):
    return lax.dot_general(a, b, (((ca,), (cb,)), ((), ())), preferred_element_type=F32)


def nn(a, b):
    return dot(a, b, 1, 0)


def nt(a, b):
    return dot(a, b, 1, 1)


def tn(a, b):
    return dot(a, b, 0, 0)


def norm_stats(values):
    row_mean = jnp.mean(values, axis=-1, keepdims=True)
    centered = values - row_mean
    variance = jnp.mean(centered * centered, axis=-1, keepdims=True)
    inv = lax.rsqrt(variance + epsilon)
    return centered * inv, inv


def norm_grad(xhat, inv, gain, grad):
    scaled = grad * gain
    a = jnp.mean(scaled, axis=-1, keepdims=True)
    b = jnp.mean(scaled * xhat, axis=-1, keepdims=True)
    return inv * (scaled - a - xhat * b)


def gelu_parts(p):
    p2 = p * p
    th = jnp.tanh(gelu_coef * (p + 0.044715 * p2 * p))
    half = 0.5 * (1.0 + th)
    slope = half + 0.5 * p * (1.0 - th * th) * (gelu_coef * (1.0 + 3.0 * 0.044715 * p2))
    return p * half, slope


def iota(shape, axis):
    return lax.broadcasted_iota(I32, shape, axis)


def place_matrix(ids):
    rows = ids.shape[0]
    return (ids == f(iota((rows, rows), 1))).astype(BF16)


def pair_mask(ends, core, rows):
    group = 2 * rows
    pos_r = (iota((group, 1), 0) + core * rows) & (group - 1)
    pos_c = (iota((1, group), 1) + core * rows) & (group - 1)
    sid_r = sum((pos_r >= e).astype(I32) for e in ends)
    sid_c = sum((pos_c >= e).astype(I32) for e in ends)
    sid_r = jnp.where(pos_r < ends[-1], sid_r, -1)
    same = (sid_r == sid_c).astype(I32) * (pos_c <= pos_r).astype(I32)
    diagonal = (pos_r == pos_c).astype(I32)
    return (same + diagonal) > 0, sid_r >= 0


def half_lanes():
    lane = iota((1, PAD), 1)
    low = (lane < HD).astype(F32)
    return (low.astype(BF16), (1.0 - low).astype(BF16)), (low, 1.0 - low)


def head_probs(q2, k2, lanes, mask):
    s = jnp.where(mask, nt(q2 * lanes, k2) * 0.125, masked_value)
    top = jnp.max(s, axis=-1, keepdims=True)
    e = jnp.exp(s - top)
    total = jnp.sum(e, axis=-1, keepdims=True)
    return e, top, total


def head_grad(q2, k2, v2, gc2, lanes, p):
    gp = nt(gc2 * lanes, v2)
    row_dot = jnp.sum(p * gp, axis=-1, keepdims=True)
    ds = (p * (gp - row_dot)).astype(BF16)
    return nn(ds, k2) * 0.125, tn(ds, q2) * 0.125, tn(p.astype(BF16), gc2)


def kernel_call(body, outs, args, smem=(), flops=0, scratch=(), blocks=None, grid=None):
    blocks = blocks or {}
    specs = []
    scalars = []
    n_bytes = 0
    for i, a in enumerate(args):
        n_bytes += a.size * a.dtype.itemsize
        if i in blocks:
            specs.append(blocks[i])
        elif i in smem:
            specs.append(pl.BlockSpec(memory_space=pltpu.SMEM))
        else:
            specs.append(pl.BlockSpec(memory_space=pltpu.VMEM))
    shapes = [jax.ShapeDtypeStruct(s, d) for s, d in outs]
    out_specs = [pl.BlockSpec(memory_space=pltpu.VMEM) for _ in outs]
    return pl.pallas_call(
        body,
        out_shape=shapes,
        in_specs=specs,
        out_specs=out_specs,
        scratch_shapes=list(scratch),
        compiler_params=pltpu.CompilerParams(vmem_limit_bytes=48 << 20),
        cost_estimate=pl.CostEstimate(
            flops=int(flops), transcendentals=0, bytes_accessed=int(n_bytes)
        ),
        name=body.func.__name__ if hasattr(body, "func") else body.__name__,
    )(*args)


def route_kernel(n_dp, lens, route, tokens, cotangent, msg, msg_cot, pick_out):
    rows, width = tokens.shape
    row = jnp.broadcast_to(f(route[...]), (rows, rows))
    col = row.T
    group = float(2 * rows)
    dest_r = jnp.floor(row / group)
    dest_c = jnp.floor(col / group)
    before = iota((rows, rows), 0) < iota((rows, rows), 1)
    same = jnp.where(before, (dest_r == dest_c).astype(F32), 0.0)
    rank = dest_r[0:1] * (rows // n_dp) + jnp.sum(same, axis=0, keepdims=True)
    pick = (jnp.broadcast_to(rank, (rows, rows)) == f(iota((rows, rows), 0))).astype(F32)
    place = row - jnp.floor(row / float(rows)) * float(rows)
    ids = jnp.sum(pick * place, axis=1, keepdims=True)
    lane = iota((rows, PAD), 1)
    extra = jnp.where(lane == 0, ids, 0.0)
    for i in range(4):
        extra = jnp.where(lane == i + 1, f(lens[0, i]), extra)
    pick_b = pick.astype(BF16)
    pick_out[...] = pick_b
    msg[:, :width] = nn(pick_b, tokens[...]).astype(BF16)
    msg[:, width:] = extra.astype(BF16)
    msg_cot[...] = nn(pick_b, cotangent[...]).astype(BF16)


def ends_of(lens):
    e = [lens[0, 0]]
    for i in range(1, 4):
        e.append(e[-1] + lens[0, i])
    return e


def attn_kernel(
    sc, lens, mine, other, vecs, w_qkv, qv_bias, w_out, x_out, normed_out, qkv_out, ctx_out, lse_out, top_out, part_out
):
    rows = mine.shape[0]
    width = w_out.shape[1]
    cols = w_out.shape[0]
    for i, half in enumerate((mine, other)):
        put = place_matrix(f(half[:, width : width + 1]))
        x = tn(put, half[:, :width])
        s = slice(i * rows, (i + 1) * rows)
        x_out[s, :] = x.astype(BF16)
        xhat, _ = norm_stats(x)
        normed_out[s, :] = (xhat * vecs[0:1, :] + vecs[1:2, :]).astype(BF16)
    normed = normed_out[...]
    for c in range(3):
        y = nn(normed, w_qkv[c])
        if c == 0:
            y = y + f(qv_bias[0:1, :])
        if c == 2:
            y = y + f(qv_bias[1:2, :])
        qkv_out[:, c * cols : (c + 1) * cols] = y.astype(BF16)
    mask, live = pair_mask(ends_of(lens), sc[0], rows)
    lanes_b, lanes_f = half_lanes()
    lane = iota((1, PAD), 1)
    lse = jnp.zeros((2 * rows, PAD), F32)
    for pair in range(cols // PAD):
        s = slice(pair * PAD, (pair + 1) * PAD)
        q2 = qkv_out[:, s]
        k2 = qkv_out[:, slice(cols + pair * PAD, cols + (pair + 1) * PAD)]
        v2 = qkv_out[:, slice(2 * cols + pair * PAD, 2 * cols + (pair + 1) * PAD)]
        out = jnp.zeros((2 * rows, PAD), F32)
        for i in range(2):
            e, top, total = head_probs(q2, k2, lanes_b[i], mask)
            probs = (e * (1.0 / total)).astype(BF16)
            out = out + nn(probs, v2) * lanes_f[i]
            h = 2 * pair + i
            lse = jnp.where(lane == h, top + jnp.log(total), lse)
            best = jnp.max(jnp.where(live, top, masked_value), axis=0, keepdims=True)
            top_out[h : h + 1, :] = jnp.broadcast_to(best, (1, PAD))
        ctx_out[:, s] = out.astype(BF16)
    lse_out[...] = lse
    part_out[...] = nn(ctx_out[...], w_out[...]).astype(BF16)


def cot_kernel(mine, other, cot_mine, cot_other, cot_out):
    rows = mine.shape[0]
    for i, (ids, c) in enumerate(((mine, cot_mine), (other, cot_other))):
        put = place_matrix(f(ids[:, 0:1]))
        cot_out[i * rows : (i + 1) * rows, :] = tn(put, c[...]).astype(BF16)


def middle_kernel(x, part, recv, vecs, middle_out, mid_out):
    rows = x.shape[0] // 2
    for i in range(2):
        s = slice(i * rows, (i + 1) * rows)
        o = slice((1 - i) * rows, (2 - i) * rows)
        middle = f(x[s, :]) + (f(part[s, :]) + f(recv[o, :])) + vecs[2:3, :]
        middle_out[s, :] = middle
        mhat, _ = norm_stats(middle)
        mid_out[s, :] = (mhat * vecs[3:4, :] + vecs[4:5, :]).astype(BF16)


TILE = 512


def mlp_kernel(mid, cot, vecs, up, down, gmid_out, act_out, sums_out, acc):
    width, hidden = up.shape
    per_row = width // TILE
    for t in range(hidden // TILE):
        s = slice(t * TILE, (t + 1) * TILE)
        bias = vecs[6 + t // per_row : 7 + t // per_row, (t % per_row) * TILE : (t % per_row + 1) * TILE]
        act, slope = gelu_parts(nn(mid[...], up[:, s]) + bias)
        act_out[:, s] = act.astype(BF16)
        gpre = (nt(cot[...], down[s, :]) * slope).astype(BF16)
        sums_out[:, s] = jnp.sum(f(gpre), axis=0, keepdims=True)
        g = nt(gpre, up[:, s])
        if t == 0:
            acc[...] = g
        else:
            acc[...] += g
    gmid_out[...] = acc[...].astype(BF16)


def mlp_out_kernel(act, down, mine_out, other_out):
    rows = mine_out.shape[0]
    y = nn(act[...], down[...])
    mine_out[...] = y[:rows]
    other_out[...] = y[rows:].astype(BF16)


def gmid_kernel(part, recv, middle, cot, vecs, gmid_out, gattn_out, sums_out):
    rows = part.shape[0] // 2
    for i in range(2):
        s = slice(i * rows, (i + 1) * rows)
        o = slice((1 - i) * rows, (2 - i) * rows)
        g = f(part[s, :]) + f(recv[o, :])
        mhat, inv = norm_stats(middle[s, :])
        c = f(cot[s, :])
        gm = c + norm_grad(mhat, inv, vecs[3:4, :], g)
        gattn_out[s, :] = gm.astype(BF16)
        if i == 0:
            gmid_out[...] = gm
            sums_out[0:1, :] = jnp.sum(gm, axis=0, keepdims=True)
            sums_out[1:2, :] = jnp.sum(g * mhat, axis=0, keepdims=True)
            sums_out[2:3, :] = jnp.sum(g, axis=0, keepdims=True)
            sums_out[3:4, :] = jnp.sum(c, axis=0, keepdims=True)
            sums_out[4:8, :] = jnp.zeros((4, sums_out.shape[1]), F32)


def attn_grad_kernel(sc, lens, gattn, w_out, qkv, lse, w_qkv, mine_out, other_out, sums_out, gqkv):
    rows = gattn.shape[0] // 2
    cols = w_out.shape[0]
    gctx = nt(gattn[...], w_out[...]).astype(BF16)
    mask, _ = pair_mask(ends_of(lens), sc[0], rows)
    lanes_b, lanes_f = half_lanes()
    for pair in range(cols // PAD):
        cut = [slice(c * cols + pair * PAD, c * cols + (pair + 1) * PAD) for c in range(3)]
        q2, k2, v2 = (qkv[:, c] for c in cut)
        gc2 = gctx[:, pair * PAD : (pair + 1) * PAD]
        total = None
        for i in range(2):
            h = 2 * pair + i
            s = jnp.where(mask, nt(q2 * lanes_b[i], k2) * 0.125, masked_value)
            p = jnp.exp(s - lse[:, h : h + 1])
            g3 = [g * lanes_f[i] for g in head_grad(q2, k2, v2, gc2, lanes_b[i], p)]
            total = g3 if total is None else [a + b for a, b in zip(total, g3)]
        for c in range(3):
            g = total[c].astype(BF16)
            gqkv[:, cut[c]] = g
            sums_out[c : c + 1, pair * PAD : (pair + 1) * PAD] = jnp.sum(f(g), axis=0, keepdims=True)
    y = sum(nt(gqkv[:, c * cols : (c + 1) * cols], w_qkv[c]) for c in range(3))
    mine_out[...] = y[:rows]
    other_out[...] = y[rows:].astype(BF16)


def last_kernel(part, recv, x, gmid, vecs, ids, msg_out, sums_out):
    rows = part.shape[0]
    g = part[...] + f(recv[...])
    xhat, inv = norm_stats(f(x[:rows, :]))
    grad = (gmid[...] + norm_grad(xhat, inv, vecs[0:1, :], g)).astype(BF16)
    sums_out[0:1, :] = jnp.sum(g * xhat, axis=0, keepdims=True)
    sums_out[1:2, :] = jnp.sum(g, axis=0, keepdims=True)
    msg_out[...] = nn(place_matrix(f(ids[:, 0:1])), grad).astype(BF16)


def result_kernel(middle, part, recv, vecs, ids, msg_out):
    rows = part.shape[0]
    res = middle[:rows, :] + (part[...] + f(recv[...])) + vecs[5:6, :]
    msg_out[...] = nn(place_matrix(f(ids[:, 0:1])), res.astype(BF16)).astype(BF16)


def restore_kernel(pick, msg, out):
    out[...] = tn(pick[...], msg[...]).astype(BF16)


def run_lengths(bits, block):
    return {b: block << i for i, b in enumerate(sorted(bits))}


def split_rows(src, run, mine, send_out, keep_out, at):
    n = src.shape[0]
    for j in range(n // (2 * run)):
        k = pl.multiple_of(2 * run * j + mine * run, run)
        s = pl.multiple_of(2 * run * j + (1 - mine) * run, run)
        dst = slice(j * run, (j + 1) * run)
        keep_out[dst, at] = src[pl.ds(k, run), :]
        send_out[dst, at] = src[pl.ds(s, run), :].astype(BF16)


def gather_rows(own, halves, dst):
    n = own.shape[0]
    dst[:n, :] = own[...]
    for h in halves:
        r = h.shape[0]
        dst[n : n + r, :] = h[...]
        n += r


def mlp_weights_kernel(
    n_bits, bit, sc, mid, m1, m2, m3, o1, o2, o3, cot, c1, c2, c3, d1, d2, d3, bias, up, down,
    send_down, keep_down, send_up, keep_up, mids, cots, grad,
):
    gather_rows(mid, (m1, o1, m2, o2, m3, o3), mids)
    gather_rows(cot, (c1, d1, c2, d2, c3, d3), cots)
    mine = (sc[1] >> bit) & 1
    run = (mids.shape[1] >> n_bits) << bit
    act, slope = gelu_parts(nn(mids[...], up[...]) + bias[...])
    every = slice(None)
    grad[...] = tn(cots[...], act.astype(BF16))
    split_rows(grad, run, mine, send_down, keep_down, every)
    gpre = (nt(cots[...], down[...]) * slope).astype(BF16)
    grad[...] = tn(mids[...], gpre)
    split_rows(grad, run, mine, send_up, keep_up, every)


def attn_weights_kernel(
    n_bits, bit, n_dp, sc, ids, nrm, m1, m2, m3, o1, o2, o3, ga, c1, c2, c3, d1, d2, d3, qv_bias, w_qkv, w_out,
    send_out, keep_out, norms, gattns, ctx, gqkv, grad,
):
    gather_rows(nrm, (m1, o1, m2, o2, m3, o3), norms)
    gather_rows(ga, (c1, d1, c2, d2, c3, d3), gattns)
    rows = nrm.shape[0] // 2
    group = 2 * rows
    me = sc[1]
    mine = (me >> bit) & 1
    run = (norms.shape[1] >> n_bits) << bit
    masks = (0, 1 << AG_BITS[0], 1 << AG_BITS[1], (1 << AG_BITS[0]) | (1 << AG_BITS[1]))
    norm4 = norms[...]
    q4 = (nn(norm4, w_qkv[0]) + f(qv_bias[0:1, :])).astype(BF16)
    k4 = nn(norm4, w_qkv[1]).astype(BF16)
    v4 = (nn(norm4, w_qkv[2]) + f(qv_bias[1:2, :])).astype(BF16)
    gc4 = nt(gattns[...], w_out[...]).astype(BF16)
    lanes_b, lanes_f = half_lanes()
    table = f(ids[...])
    from_dp = iota((rows, 1), 0) // (rows // n_dp)
    first = iota((rows, 1), 0) == from_dp * (rows // n_dp)
    for g in range(4):
        chosen = jnp.where((from_dp == (me ^ masks[g])) & first, table, 0.0)
        lens = jnp.sum(chosen, axis=0, keepdims=True)
        ends = [lens[:, 1:2]]
        for i in range(2, 5):
            ends.append(ends[-1] + lens[:, i : i + 1])
        mask, _ = pair_mask([e.astype(I32) for e in ends], sc[0], rows)
        s = slice(g * group, (g + 1) * group)
        q2, k2, v2, gc2 = q4[s], k4[s], v4[s], gc4[s]
        out = jnp.zeros((group, PAD), F32)
        total = None
        for i in range(2):
            e, _, denom = head_probs(q2, k2, lanes_b[i], mask)
            p = e * (1.0 / denom)
            out = out + nn(p.astype(BF16), v2) * lanes_f[i]
            g3 = [x * lanes_f[i] for x in head_grad(q2, k2, v2, gc2, lanes_b[i], p)]
            total = g3 if total is None else [a + b for a, b in zip(total, g3)]
        ctx[s, :] = out.astype(BF16)
        for c in range(3):
            gqkv[s, c * PAD : (c + 1) * PAD] = total[c].astype(BF16)
    grad[:, : 3 * PAD] = tn(norm4, gqkv[...])
    grad[:, 3 * PAD :] = tn(gattns[...], ctx[...])
    split_rows(grad, run, mine, send_out, keep_out, slice(None))


def step_kernel(bit, run, sc, keep, recv, send_out, keep_out, cur):
    cur[...] = keep[...] + f(recv[...])
    split_rows(cur, run, (sc[1] >> bit) & 1, send_out, keep_out, slice(None))


def pieces_kernel(sc, keep, recv, own, p1, p2, p3, cur):
    cur[...] = keep[...] + f(recv[...])
    n = own.shape[0]
    q = sc[2]
    for j, out in enumerate((own, p1, p2, p3)):
        out[...] = cur[pl.ds(pl.multiple_of((q ^ j) * n, n), n), :].astype(out.dtype)


def join_mlp_kernel(sc, own, p1, p2, p3, out):
    w = own.shape[1]
    for j, p in enumerate((own, p1, p2, p3)):
        out[:, pl.ds(pl.multiple_of((sc[2] ^ j) * w, w), w)] = f(p[...])


def join_attn_kernel(sc, own, p1, p2, p3, qkv_out, out_out):
    w = own.shape[1] // 4
    for j, p in enumerate((own, p1, p2, p3)):
        at = pl.ds(pl.multiple_of((sc[2] ^ j) * w, w), w)
        for c in range(3):
            qkv_out[c, :, at] = f(p[:, c * w : (c + 1) * w])
        out_out[:, at] = f(p[:, 3 * w :])


def local(
    tokens,
    cotangent,
    route,
    lengths,
    clip_tau,
    attn_norm_gain,
    attn_norm_bias,
    qkv_weight,
    qv_bias,
    out_weight,
    out_bias,
    mlp_norm_gain,
    mlp_norm_bias,
    up_weight,
    up_bias,
    down_weight,
    down_bias,
):
    n_dp = lax.axis_size("dp")
    n_bits = n_dp.bit_length() - 1
    rs_bits = [b for b in range(n_bits) if b not in AG_BITS]
    masks = [1 << AG_BITS[0], 1 << AG_BITS[1], (1 << AG_BITS[0]) | (1 << AG_BITS[1])]
    me = lax.axis_index("dp")
    core = lax.axis_index("tensor")
    rows, width = tokens.shape
    group = 2 * rows
    cols = qkv_weight.shape[2]
    hidden = up_weight.shape[1]
    q_cols = cols // 4
    q_hidden = hidden // 4
    quarter = ((me >> AG_BITS[0]) & 1) + 2 * ((me >> AG_BITS[1]) & 1)
    sc = jnp.stack([core, me, quarter, core]).astype(I32)

    def swap(x):
        return lax.ppermute(x, "tensor", [(0, 1), (1, 0)])

    def hop(x, mask):
        return lax.ppermute(x, "dp", [(i, i ^ mask) for i in range(n_dp)])

    def exchange(x):
        return lax.all_to_all(x, "dp", split_axis=0, concat_axis=0, tiled=True)

    def share(own):
        got = [hop(own[:rows], m) for m in masks]
        return got + [swap(g) for g in got]

    w_qkv = jnp.transpose(qkv_weight, (1, 0, 2))
    vecs = jnp.concatenate(
        [attn_norm_gain, attn_norm_bias, out_bias, mlp_norm_gain, mlp_norm_bias, down_bias, up_bias]
    ).astype(F32).reshape(-1, width)

    msg, msg_cot, pick = kernel_call(
        functools.partial(route_kernel, n_dp),
        [((rows, width + PAD), BF16), ((rows, width), BF16), ((rows, rows), BF16)],
        [lengths, route.reshape(1, rows), tokens, cotangent],
        smem=(0,),
        flops=4 * rows * rows * width,
    )
    got = exchange(msg)
    got_cot = exchange(msg_cot)
    other = swap(got)
    x, normed, qkv, ctx, lse, tops, part = kernel_call(
        attn_kernel,
        [
            ((group, width), BF16),
            ((group, width), BF16),
            ((group, 3 * cols), BF16),
            ((group, cols), BF16),
            ((group, PAD), F32),
            ((cols // HD, PAD), F32),
            ((group, width), BF16),
        ],
        [sc, lengths, got, other, vecs, w_qkv, qv_bias, out_weight],
        smem=(0, 1),
        flops=2 * group * width * 4 * cols * 3,
    )
    ids = got[:, width:]
    ids_other = other[:, width:]
    (cot,) = kernel_call(
        cot_kernel, [((group, width), BF16)], [ids, ids_other, got_cot, swap(got_cot)], flops=1 << 27
    )
    middle, mid = kernel_call(
        middle_kernel, [((group, width), F32), ((group, width), BF16)], [x, part, swap(part), vecs], flops=1 << 28
    )
    gmid_part, act, up_sums = kernel_call(
        mlp_kernel,
        [((group, width), BF16), ((group, hidden), BF16), ((1, hidden), F32)],
        [mid, cot, vecs, up_weight, down_weight],
        flops=2 * group * width * hidden * 3,
        scratch=[pltpu.VMEM((group, width), F32)],
    )
    gmid, gattn, mid_sums = kernel_call(
        gmid_kernel,
        [((rows, width), F32), ((group, width), BF16), ((8, width), F32)],
        [gmid_part, swap(gmid_part), middle, cot, vecs],
        flops=1 << 28,
    )
    gn_mine, gn_other, qkv_sums = kernel_call(
        attn_grad_kernel,
        [((rows, width), F32), ((rows, width), BF16), ((3, cols), F32)],
        [sc, lengths, gattn, out_weight, qkv, lse, w_qkv],
        smem=(0, 1),
        flops=2 * group * width * 4 * cols * 3,
        scratch=[pltpu.VMEM((group, 3 * cols), BF16)],
    )
    back_grad, norm_sums = kernel_call(
        last_kernel,
        [((rows, width), BF16), ((2, width), F32)],
        [gn_mine, swap(gn_other), x, gmid, vecs, ids],
        flops=1 << 27,
    )
    mlp_mine, mlp_other = kernel_call(
        mlp_out_kernel,
        [((rows, width), F32), ((rows, width), BF16)],
        [act, down_weight],
        flops=2 * group * width * hidden,
    )
    (back_out,) = kernel_call(
        result_kernel, [((rows, width), BF16)], [middle, mlp_mine, swap(mlp_other), vecs, ids], flops=1 << 27
    )

    def restore(y):
        return kernel_call(restore_kernel, [((rows, width), BF16)], [pick, exchange(y)], flops=1 << 26)[0]

    block = width // n_dp
    first = rs_bits[0]
    up_q = lax.dynamic_slice_in_dim(up_weight, quarter * q_hidden, q_hidden, 1)
    down_q = lax.dynamic_slice_in_dim(down_weight, quarter * q_hidden, q_hidden, 0)
    bias_q = f(lax.dynamic_slice_in_dim(up_bias, quarter * q_hidden, q_hidden, 0)).reshape(1, -1)
    cots = share(cot)
    mids = share(mid)
    half = ((width // 2, q_hidden), BF16), ((width // 2, q_hidden), F32)
    send_down, keep_down, send_up, keep_up = kernel_call(
        functools.partial(mlp_weights_kernel, n_bits, first),
        [half[0], half[1], half[0], half[1]],
        [sc, mid] + mids + [cot] + cots + [bias_q, up_q, down_q],
        smem=(0,),
        flops=2 * 4 * group * width * q_hidden * 4,
        scratch=[
            pltpu.VMEM((4 * group, width), BF16),
            pltpu.VMEM((4 * group, width), BF16),
            pltpu.VMEM((width, q_hidden), F32),
        ],
    )
    w_q = lax.dynamic_slice_in_dim(w_qkv, quarter * q_cols, q_cols, 2)
    out_q = lax.dynamic_slice_in_dim(out_weight, quarter * q_cols, q_cols, 0)
    qv_q = lax.dynamic_slice_in_dim(qv_bias, quarter * q_cols, q_cols, 1)
    norms = share(normed)
    gattns = share(gattn)
    send_attn, keep_attn = kernel_call(
        functools.partial(attn_weights_kernel, n_bits, first, n_dp),
        [((width // 2, 4 * q_cols), BF16), ((width // 2, 4 * q_cols), F32)],
        [sc, ids, normed] + norms + [gattn] + gattns + [qv_q, w_q, out_q],
        smem=(0,),
        flops=2 * 4 * group * width * q_cols * 12,
        scratch=[
            pltpu.VMEM((4 * group, width), BF16),
            pltpu.VMEM((4 * group, width), BF16),
            pltpu.VMEM((4 * group, q_cols), BF16),
            pltpu.VMEM((4 * group, 3 * q_cols), BF16),
            pltpu.VMEM((width, 4 * q_cols), F32),
        ],
    )

    def reduce_rows(send, keep):
        w = send.shape[1]
        left = [b for b in range(n_bits) if b != first]
        for at, b in enumerate(rs_bits):
            recv = hop(send, 1 << b)
            n = keep.shape[0]
            if at + 1 == len(rs_bits):
                break
            nxt = rs_bits[at + 1]
            run = run_lengths(left, block)[nxt]
            left.remove(nxt)
            send, keep = kernel_call(
                functools.partial(step_kernel, nxt, run),
                [((n // 2, w), BF16), ((n // 2, w), F32)],
                [sc, keep, recv],
                smem=(0,),
                flops=1 << 26,
                scratch=[pltpu.VMEM((n, w), F32)],
            )
        pieces = kernel_call(
            pieces_kernel,
            [((block, w), F32)] + [((block, w), BF16)] * 3,
            [sc, keep, recv],
            smem=(0,),
            flops=1 << 26,
            scratch=[pltpu.VMEM((n, w), F32)],
        )
        return [pieces[0]] + [hop(p, m) for p, m in zip(pieces[1:], masks)]

    down_pieces = reduce_rows(send_down, keep_down)
    up_pieces = reduce_rows(send_up, keep_up)
    attn_pieces = reduce_rows(send_attn, keep_attn)
    grad_down = kernel_call(join_mlp_kernel, [((block, hidden), F32)], [sc] + down_pieces, smem=(0,))[0].T
    grad_up = kernel_call(join_mlp_kernel, [((block, hidden), F32)], [sc] + up_pieces, smem=(0,))[0]
    grad_qkv, grad_out = kernel_call(
        join_attn_kernel, [((3, block, cols), F32), ((block, cols), F32)], [sc] + attn_pieces, smem=(0,)
    )
    grad_qkv = jnp.transpose(grad_qkv, (1, 0, 2))
    grad_out = grad_out.T

    n_vec = 6 * width
    sums = jnp.concatenate(
        [
            norm_sums.reshape(-1),
            mid_sums[:4].reshape(-1),
            qkv_sums[0],
            qkv_sums[2],
            up_sums.reshape(-1),
        ]
    )
    n_sum = sums.size
    msg = jnp.concatenate([sums, jnp.pad(tops[:, 0], (0, PAD - tops.shape[0]))])
    for b in range(n_bits):
        came = hop(msg, 1 << b)
        msg = jnp.concatenate([msg[:n_sum] + came[:n_sum], jnp.maximum(msg[n_sum:], came[n_sum:])])
    global_top = msg[n_sum : n_sum + tops.shape[0]]
    theirs = swap(msg[:n_sum])
    vector_sum = (msg[:n_vec] + theirs[:n_vec]).reshape(6, width)
    own, oth = msg[n_vec:n_sum], theirs[n_vec:]
    one = jnp.where(core == 0, own, oth)
    two = jnp.where(core == 0, oth, own)
    qv_sum = jnp.stack(
        [
            jnp.concatenate([one[:cols], two[:cols]]),
            jnp.concatenate([one[cols : 2 * cols], two[cols : 2 * cols]]),
        ]
    )
    up_sum = jnp.concatenate([one[2 * cols :], two[2 * cols :]])

    out_tokens = restore(back_out)
    grad_tokens = restore(back_grad)

    threshold = clip_tau[0].astype(F32)
    head_factor = jnp.sqrt(threshold / jnp.maximum(global_top, threshold))
    column_factor = jnp.repeat(head_factor, HD)
    clipped_qk = (f(qkv_weight[:, 0:2]) * column_factor).astype(BF16)
    clipped_q_bias = (f(qv_bias[0]) * column_factor).astype(BF16)
    return (
        out_tokens,
        grad_tokens,
        grad_qkv,
        grad_out,
        grad_up,
        grad_down,
        qv_sum,
        up_sum,
        vector_sum,
        head_factor,
        clipped_qk,
        clipped_q_bias,
    )

def solution(mesh):
    placed = (
        P(("dp", "tensor"), None),
        P(("dp", "tensor"), None),
        P(("dp", "tensor")),
        P("dp", None),
        P(),
        P(),
        P(),
        P(None, None, "tensor"),
        P(None, "tensor"),
        P("tensor", None),
        P(),
        P(),
        P(),
        P(None, "tensor"),
        P("tensor"),
        P("tensor", None),
        P(),
    )
    return jax.shard_map(
        local,
        mesh=mesh,
        in_specs=placed,
        out_specs=(
            P(("dp", "tensor"), None),
            P(("dp", "tensor"), None),
            P("dp", None, "tensor"),
            P("tensor", "dp"),
            P("dp", "tensor"),
            P("tensor", "dp"),
            P(),
            P(),
            P(),
            P("tensor"),
            P(None, None, "tensor"),
            P("tensor"),
        ),
        check_vma=False,
    )
```

```python
import functools
import jax
import jax.numpy as jnp
from jax import lax
from jax.experimental import pallas as pl
from jax.experimental.pallas import tpu as pltpu
from jax.sharding import PartitionSpec as P

HD = 64
AG_BITS = (0, 1)
PAD = 128
COST = 1

epsilon = 1e-05
masked_value = -1e30
gelu_coef = 0.7978845608028654
F32 = jnp.float32
BF16 = jnp.bfloat16
I32 = jnp.int32


def f(x):
    return x.astype(F32)


def dot(a, b, ca, cb):
    return lax.dot_general(a, b, (((ca,), (cb,)), ((), ())), preferred_element_type=F32)


def nn(a, b):
    return dot(a, b, 1, 0)


def nt(a, b):
    return dot(a, b, 1, 1)


def tn(a, b):
    return dot(a, b, 0, 0)


def norm_stats(values):
    row_mean = jnp.mean(values, axis=-1, keepdims=True)
    centered = values - row_mean
    variance = jnp.mean(centered * centered, axis=-1, keepdims=True)
    inv = lax.rsqrt(variance + epsilon)
    return centered * inv, inv


def norm_grad(xhat, inv, gain, grad):
    scaled = grad * gain
    a = jnp.mean(scaled, axis=-1, keepdims=True)
    b = jnp.mean(scaled * xhat, axis=-1, keepdims=True)
    return inv * (scaled - a - xhat * b)


def gelu_parts(p):
    p2 = p * p
    th = jnp.tanh(gelu_coef * (p + 0.044715 * p2 * p))
    half = 0.5 * (1.0 + th)
    slope = half + 0.5 * p * (1.0 - th * th) * (gelu_coef * (1.0 + 3.0 * 0.044715 * p2))
    return p * half, slope


def iota(shape, axis):
    return lax.broadcasted_iota(I32, shape, axis)


def place_matrix(ids):
    rows = ids.shape[0]
    return (ids == f(iota((rows, rows), 1))).astype(BF16)


def pair_mask(ends, core, rows):
    group = 2 * rows
    pos_r = (iota((group, 1), 0) + core * rows) & (group - 1)
    pos_c = (iota((1, group), 1) + core * rows) & (group - 1)
    sid_r = sum((pos_r >= e).astype(I32) for e in ends)
    sid_c = sum((pos_c >= e).astype(I32) for e in ends)
    sid_r = jnp.where(pos_r < ends[-1], sid_r, -1)
    same = (sid_r == sid_c).astype(I32) * (pos_c <= pos_r).astype(I32)
    diagonal = (pos_r == pos_c).astype(I32)
    return (same + diagonal) > 0, sid_r >= 0


def half_lanes():
    lane = iota((1, PAD), 1)
    low = (lane < HD).astype(F32)
    return (low.astype(BF16), (1.0 - low).astype(BF16)), (low, 1.0 - low)


def head_probs(q2, k2, lanes, mask):
    s = jnp.where(mask, nt(q2 * lanes, k2) * 0.125, masked_value)
    top = jnp.max(s, axis=-1, keepdims=True)
    e = jnp.exp(s - top)
    total = jnp.sum(e, axis=-1, keepdims=True)
    return e, top, total


def head_grad(q2, k2, v2, gc2, lanes, p):
    gp = nt(gc2 * lanes, v2)
    row_dot = jnp.sum(p * gp, axis=-1, keepdims=True)
    ds = (p * (gp - row_dot)).astype(BF16)
    return nn(ds, k2) * 0.125, tn(ds, q2) * 0.125, tn(p.astype(BF16), gc2)


class Fetched:
    def __init__(self, ref, copies):
        self.ref, self.copies, self.shape = ref, copies, ref.shape

    def wait(self, k=None):
        for c in self.copies if k is None else [self.copies[k]]:
            c.wait()
        return self.ref


def whole(shape):
    return shape, lambda src, dst, sc: [(src, dst)]


def kernel_call(body, outs, args, smem=(), hbm=None, flops=0, scratch=(), limit=12):
    hbm = hbm or {}
    specs = []
    n_bytes = 0
    for i, a in enumerate(args):
        n_bytes += a.size * a.dtype.itemsize
        space = pltpu.HBM if i in hbm else pltpu.SMEM if i in smem else pltpu.VMEM
        specs.append(pl.BlockSpec(memory_space=space))
    shapes = [jax.ShapeDtypeStruct(s, d) for s, d in outs]
    out_specs = [pl.BlockSpec(memory_space=pltpu.VMEM) for _ in outs]
    args = [pltpu.with_memory_space_constraint(a, pltpu.HBM) if i in hbm else a for i, a in enumerate(args)]
    n_in, n_out, n_scratch = len(args), len(outs), len(scratch)
    extra = []
    for i, (shape, chunks) in hbm.items():
        extra.append(pltpu.VMEM(shape, args[i].dtype))
    n_chunks = {}
    for i, (shape, chunks) in hbm.items():
        n_chunks[i] = getattr(chunks, "count", 1)
        extra.append(pltpu.SemaphoreType.DMA((n_chunks[i],)))

    def run(*refs):
        ins = list(refs[:n_in])
        rest = refs[n_in + n_out + n_scratch :]
        sc = ins[0]
        for j, (i, (_, chunks)) in enumerate(hbm.items()):
            dst, sem = rest[j], rest[len(hbm) + j]
            copies = [
                pltpu.make_async_copy(a, b, sem.at[k]) for k, (a, b) in enumerate(chunks(ins[i], dst, sc))
            ]
            for c in copies:
                c.start()
            ins[i] = Fetched(dst, copies)
        body(*ins, *refs[n_in : n_in + n_out + n_scratch])

    return pl.pallas_call(
        run,
        out_shape=shapes,
        in_specs=specs,
        out_specs=out_specs,
        scratch_shapes=list(scratch) + extra,
        compiler_params=pltpu.CompilerParams(vmem_limit_bytes=limit << 20),
        cost_estimate=pl.CostEstimate(
            flops=int(flops * COST), transcendentals=0, bytes_accessed=int(n_bytes * COST)
        ),
        name=body.func.__name__ if hasattr(body, "func") else body.__name__,
    )(*args)


def chunked(count, make):
    def chunks(src, dst, sc):
        return [make(src, dst, sc, k) for k in range(count)]

    chunks.count = count
    return chunks


def by_row(count):
    return chunked(count, lambda src, dst, sc, k: (src.at[k], dst.at[k]))


def tiles(count, axis):
    def make(src, dst, sc, k):
        at = pl.ds(k * TILE, TILE)
        return (src.at[at, :], dst.at[at, :]) if axis == 0 else (src.at[:, at], dst.at[:, at])

    return chunked(count, make)


def columns(n, axis):
    def chunks(src, dst, sc):
        at = pl.ds(pl.multiple_of(sc[2] * n, n), n)
        if axis == 0:
            return [(src.at[at, :], dst)]
        return [(src.at[(slice(None),) * (len(src.shape) - 1) + (at,)], dst)]

    return chunks


def route_kernel(n_dp, route, lens, tokens, cotangent, msg, msg_cot, pick_out):
    rows, width = tokens.shape
    row = jnp.broadcast_to(f(route.wait()[...]), (rows, rows))
    col = row.T
    group = float(2 * rows)
    dest_r = jnp.floor(row / group)
    dest_c = jnp.floor(col / group)
    before = iota((rows, rows), 0) < iota((rows, rows), 1)
    same = jnp.where(before, (dest_r == dest_c).astype(F32), 0.0)
    rank = dest_r[0:1] * (rows // n_dp) + jnp.sum(same, axis=0, keepdims=True)
    pick = (jnp.broadcast_to(rank, (rows, rows)) == f(iota((rows, rows), 0))).astype(F32)
    place = row - jnp.floor(row / float(rows)) * float(rows)
    ids = jnp.sum(pick * place, axis=1, keepdims=True)
    lane = iota((rows, PAD), 1)
    extra = jnp.where(lane == 0, ids, 0.0)
    lens = f(lens.wait()[...])
    for i in range(4):
        extra = jnp.where(lane == i + 1, lens[:, i : i + 1], extra)
    pick_b = pick.astype(BF16)
    pick_out[...] = pick_b
    msg[:, :width] = nn(pick_b, tokens.wait()[...]).astype(BF16)
    msg[:, width:] = extra.astype(BF16)
    msg_cot[...] = nn(pick_b, cotangent.wait()[...]).astype(BF16)


def ends_of(sc):
    e = [sc[4]]
    for i in range(1, 4):
        e.append(e[-1] + sc[4 + i])
    return e


def attn_kernel(
    sc, mine, other, vecs, w_qkv, qv_bias, w_out, x_out, normed_out, qkv_out, lse_out, top_out, part_out, ctx_out
):
    rows = mine.shape[0]
    width = w_out.shape[1]
    cols = w_out.shape[0]
    for i, half in enumerate((mine, other)):
        put = place_matrix(f(half[:, width : width + 1]))
        x = tn(put, half[:, :width])
        s = slice(i * rows, (i + 1) * rows)
        x_out[s, :] = x.astype(BF16)
        xhat, _ = norm_stats(x)
        normed_out[s, :] = (xhat * vecs[0:1, :] + vecs[1:2, :]).astype(BF16)
    normed = normed_out[...]
    qv_bias = qv_bias.wait()
    for c in range(3):
        y = nn(normed, w_qkv.wait(c)[c])
        if c == 0:
            y = y + f(qv_bias[0:1, :])
        if c == 2:
            y = y + f(qv_bias[1:2, :])
        qkv_out[:, c * cols : (c + 1) * cols] = y.astype(BF16)
    mask, live = pair_mask(ends_of(sc), sc[0], rows)
    lanes_b, lanes_f = half_lanes()
    lane = iota((1, PAD), 1)
    lse = jnp.zeros((2 * rows, PAD), F32)
    for pair in range(cols // PAD):
        s = slice(pair * PAD, (pair + 1) * PAD)
        q2 = qkv_out[:, s]
        k2 = qkv_out[:, slice(cols + pair * PAD, cols + (pair + 1) * PAD)]
        v2 = qkv_out[:, slice(2 * cols + pair * PAD, 2 * cols + (pair + 1) * PAD)]
        out = jnp.zeros((2 * rows, PAD), F32)
        for i in range(2):
            e, top, total = head_probs(q2, k2, lanes_b[i], mask)
            probs = (e * (1.0 / total)).astype(BF16)
            out = out + nn(probs, v2) * lanes_f[i]
            h = 2 * pair + i
            lse = jnp.where(lane == h, top + jnp.log(total), lse)
            best = jnp.max(jnp.where(live, top, masked_value), axis=0, keepdims=True)
            top_out[h : h + 1, :] = jnp.broadcast_to(best, (1, PAD))
        ctx_out[:, s] = out.astype(BF16)
    lse_out[...] = lse
    part_out[...] = nn(ctx_out[...], w_out.wait()[...]).astype(BF16)


def middle_kernel(x, part, recv, vecs, mine, other, cot_mine, cot_other, middle_out, mid_out, cot_out, msg_out):
    rows, width = cot_mine.shape
    for i, (ids, c) in enumerate(((mine, cot_mine), (other, cot_other))):
        s = slice(i * rows, (i + 1) * rows)
        o = slice((1 - i) * rows, (2 - i) * rows)
        put = place_matrix(f(ids[:, width : width + 1]))
        cot = tn(put, c[...]).astype(BF16)
        cot_out[s, :] = cot
        middle = f(x[s, :]) + (f(part[s, :]) + f(recv[o, :])) + vecs[2:3, :]
        middle_out[s, :] = middle
        mhat, _ = norm_stats(middle)
        mid = (mhat * vecs[3:4, :] + vecs[4:5, :]).astype(BF16)
        mid_out[s, :] = mid
        if i == 0:
            msg_out[:, :width] = mid
            msg_out[:, width:] = cot


TILE = 512


def mlp_kernel(mid, cot, vecs, up, down, gmid_out, mine_out, other_out, sums_out, acc, acc_y):
    width, hidden = up.shape
    rows = mine_out.shape[0]
    per_row = width // TILE
    for t in range(hidden // TILE):
        s = slice(t * TILE, (t + 1) * TILE)
        bias = vecs[6 + t // per_row : 7 + t // per_row, (t % per_row) * TILE : (t % per_row + 1) * TILE]
        act, slope = gelu_parts(nn(mid[...], up.wait(t)[:, s]) + bias)
        gpre = (nt(cot[...], down.wait(t)[s, :]) * slope).astype(BF16)
        sums_out[:, s] = jnp.sum(f(gpre), axis=0, keepdims=True)
        g = nt(gpre, up.ref[:, s])
        y = nn(act.astype(BF16), down.ref[s, :])
        if t == 0:
            acc[...] = g
            acc_y[...] = y
        else:
            acc[...] += g
            acc_y[...] += y
    gmid_out[...] = acc[...].astype(BF16)
    mine_out[...] = acc_y[:rows, :]
    other_out[...] = acc_y[rows:, :].astype(BF16)


def gmid_kernel(part, recv, middle, cot, normed, vecs, gmid_out, gattn_out, sums_out, msg_out):
    rows, width = gmid_out.shape
    msg_out[:, width:] = normed[:rows, :]
    for i in range(2):
        s = slice(i * rows, (i + 1) * rows)
        o = slice((1 - i) * rows, (2 - i) * rows)
        g = f(part[s, :]) + f(recv[o, :])
        mhat, inv = norm_stats(middle[s, :])
        c = f(cot[s, :])
        gm = c + norm_grad(mhat, inv, vecs[3:4, :], g)
        gattn = gm.astype(BF16)
        gattn_out[s, :] = gattn
        if i == 0:
            gmid_out[...] = gm
            msg_out[:, :width] = gattn
            sums_out[0:1, :] = jnp.sum(gm, axis=0, keepdims=True)
            sums_out[1:2, :] = jnp.sum(g * mhat, axis=0, keepdims=True)
            sums_out[2:3, :] = jnp.sum(g, axis=0, keepdims=True)
            sums_out[3:4, :] = jnp.sum(c, axis=0, keepdims=True)
            sums_out[4:8, :] = jnp.zeros((4, sums_out.shape[1]), F32)


def attn_grad_kernel(sc, gattn, w_out, qkv, lse, w_qkv, mine_out, other_out, sums_out, gqkv):
    rows = gattn.shape[0] // 2
    cols = w_out.shape[0]
    mask, _ = pair_mask(ends_of(sc), sc[0], rows)
    gctx = nt(gattn[...], w_out.wait()[...]).astype(BF16)
    lanes_b, lanes_f = half_lanes()
    for pair in range(cols // PAD):
        cut = [slice(c * cols + pair * PAD, c * cols + (pair + 1) * PAD) for c in range(3)]
        q2, k2, v2 = (qkv[:, c] for c in cut)
        gc2 = gctx[:, pair * PAD : (pair + 1) * PAD]
        total = None
        for i in range(2):
            h = 2 * pair + i
            s = jnp.where(mask, nt(q2 * lanes_b[i], k2) * 0.125, masked_value)
            p = jnp.exp(s - lse[:, h : h + 1])
            g3 = [g * lanes_f[i] for g in head_grad(q2, k2, v2, gc2, lanes_b[i], p)]
            total = g3 if total is None else [a + b for a, b in zip(total, g3)]
        for c in range(3):
            g = total[c].astype(BF16)
            gqkv[:, cut[c]] = g
            sums_out[c : c + 1, pair * PAD : (pair + 1) * PAD] = jnp.sum(f(g), axis=0, keepdims=True)
    y = sum(nt(gqkv[:, c * cols : (c + 1) * cols], w_qkv.wait(c)[c]) for c in range(3))
    mine_out[...] = y[:rows]
    other_out[...] = y[rows:].astype(BF16)


def last_kernel(part, recv, x, gmid, middle, y_mine, y_other, vecs, ids, msg_out, sums_out):
    rows, width = part.shape
    put = place_matrix(f(ids[:, width : width + 1]))
    res = middle[:rows, :] + (y_mine[...] + f(y_other[...])) + vecs[5:6, :]
    msg_out[:, :width] = nn(put, res.astype(BF16)).astype(BF16)
    g = part[...] + f(recv[...])
    xhat, inv = norm_stats(f(x[:rows, :]))
    grad = (gmid[...] + norm_grad(xhat, inv, vecs[0:1, :], g)).astype(BF16)
    sums_out[0:1, :] = jnp.sum(g * xhat, axis=0, keepdims=True)
    sums_out[1:2, :] = jnp.sum(g, axis=0, keepdims=True)
    msg_out[:, width:] = nn(put, grad).astype(BF16)


def restore_kernel(pick, msg, out, grad):
    width = out.shape[1]
    y = tn(pick[...], msg[...]).astype(BF16)
    out[...] = y[:, :width]
    grad[...] = y[:, width:]


def clip_kernel(w, factor, out):
    for c in range(2):
        out[:, c, :] = (f(w[c]) * factor[...]).astype(BF16)


def run_lengths(bits, block):
    return {b: block << i for i, b in enumerate(sorted(bits))}


def split_rows(src, run, mine, send_out, keep_out, at):
    n = src.shape[0]
    for j in range(n // (2 * run)):
        k = pl.multiple_of(2 * run * j + mine * run, run)
        s = pl.multiple_of(2 * run * j + (1 - mine) * run, run)
        dst = slice(j * run, (j + 1) * run)
        keep_out[dst, at] = src[pl.ds(k, run), :]
        send_out[dst, at] = src[pl.ds(s, run), :].astype(BF16)


def gather_rows(own, halves, dst, at):
    n, width = own.shape
    dst[:n, :] = own[...]
    for h in halves:
        r = h.shape[0]
        dst[n : n + r, :] = h[:, at * width : (at + 1) * width]
        n += r


def mlp_weights_kernel(
    n_bits, bit, sc, mid, cot, m1, m2, m3, o1, o2, o3, bias, up, down,
    send_down, keep_down, send_up, keep_up, mids, cots, grad,
):
    gather_rows(mid, (m1, o1, m2, o2, m3, o3), mids, 0)
    gather_rows(cot, (m1, o1, m2, o2, m3, o3), cots, 1)
    mine = (sc[1] >> bit) & 1
    run = (mids.shape[1] >> n_bits) << bit
    act, slope = gelu_parts(nn(mids[...], up.wait()[...]) + f(bias.wait()[...]))
    every = slice(None)
    grad[...] = tn(cots[...], act.astype(BF16))
    split_rows(grad, run, mine, send_down, keep_down, every)
    gpre = (nt(cots[...], down.wait()[...]) * slope).astype(BF16)
    grad[...] = tn(mids[...], gpre)
    split_rows(grad, run, mine, send_up, keep_up, every)


def attn_weights_kernel(
    n_bits, bit, n_dp, sc, ids, nrm, ga, m1, m2, m3, o1, o2, o3, qv_bias, w_qkv, w_out,
    send_out, keep_out, norms, gattns, ctx, gqkv, grad,
):
    gather_rows(ga, (m1, o1, m2, o2, m3, o3), gattns, 0)
    gather_rows(nrm, (m1, o1, m2, o2, m3, o3), norms, 1)
    rows = nrm.shape[0] // 2
    group = 2 * rows
    me = sc[1]
    mine = (me >> bit) & 1
    run = (norms.shape[1] >> n_bits) << bit
    masks = (0, 1 << AG_BITS[0], 1 << AG_BITS[1], (1 << AG_BITS[0]) | (1 << AG_BITS[1]))
    norm4 = norms[...]
    w_qkv, qv_bias = w_qkv.wait(), qv_bias.wait()
    q4 = (nn(norm4, w_qkv[0]) + f(qv_bias[0:1, :])).astype(BF16)
    k4 = nn(norm4, w_qkv[1]).astype(BF16)
    v4 = (nn(norm4, w_qkv[2]) + f(qv_bias[1:2, :])).astype(BF16)
    gc4 = nt(gattns[...], w_out.wait()[...]).astype(BF16)
    lanes_b, lanes_f = half_lanes()
    table = f(ids[:, norms.shape[1] :])
    from_dp = iota((rows, 1), 0) // (rows // n_dp)
    first = iota((rows, 1), 0) == from_dp * (rows // n_dp)
    for g in range(4):
        chosen = jnp.where((from_dp == (me ^ masks[g])) & first, table, 0.0)
        lens = jnp.sum(chosen, axis=0, keepdims=True)
        ends = [lens[:, 1:2]]
        for i in range(2, 5):
            ends.append(ends[-1] + lens[:, i : i + 1])
        mask, _ = pair_mask([e.astype(I32) for e in ends], sc[0], rows)
        s = slice(g * group, (g + 1) * group)
        q2, k2, v2, gc2 = q4[s], k4[s], v4[s], gc4[s]
        out = jnp.zeros((group, PAD), F32)
        total = None
        for i in range(2):
            e, _, denom = head_probs(q2, k2, lanes_b[i], mask)
            p = e * (1.0 / denom)
            out = out + nn(p.astype(BF16), v2) * lanes_f[i]
            g3 = [x * lanes_f[i] for x in head_grad(q2, k2, v2, gc2, lanes_b[i], p)]
            total = g3 if total is None else [a + b for a, b in zip(total, g3)]
        ctx[s, :] = out.astype(BF16)
        for c in range(3):
            gqkv[s, c * PAD : (c + 1) * PAD] = total[c].astype(BF16)
    grad[:, : 3 * PAD] = tn(norm4, gqkv[...])
    grad[:, 3 * PAD :] = tn(gattns[...], ctx[...])
    split_rows(grad, run, mine, send_out, keep_out, slice(None))


def step_kernel(bit, run, sc, keep, recv, send_out, keep_out, cur):
    cur[...] = keep[...] + f(recv[...])
    split_rows(cur, run, (sc[1] >> bit) & 1, send_out, keep_out, slice(None))


def pieces_kernel(n_pairs, sc, *refs):
    pairs, (own, p1, p2, p3), cur = refs[: 2 * n_pairs], refs[2 * n_pairs : -1], refs[-1]
    n = own.shape[0]
    w = pairs[0].shape[1]
    for i in range(n_pairs):
        cur[:, i * w : (i + 1) * w] = pairs[2 * i][...] + f(pairs[2 * i + 1][...])
    q = sc[2]
    for j, out in enumerate((own, p1, p2, p3)):
        out[...] = cur[pl.ds(pl.multiple_of((q ^ j) * n, n), n), :].astype(out.dtype)


def join_mlp_kernel(sc, own, p1, p2, p3, down_out, up_out):
    w = own.shape[1] // 2
    for j, p in enumerate((own, p1, p2, p3)):
        at = pl.ds(pl.multiple_of((sc[2] ^ j) * w, w), w)
        down_out[:, at] = f(p[:, :w])
        up_out[:, at] = f(p[:, w:])


def join_attn_kernel(sc, own, p1, p2, p3, qkv_out, out_out):
    w = own.shape[1] // 4
    for j, p in enumerate((own, p1, p2, p3)):
        at = pl.ds(pl.multiple_of((sc[2] ^ j) * w, w), w)
        for c in range(3):
            qkv_out[c, :, at] = f(p[:, c * w : (c + 1) * w])
        out_out[:, at] = f(p[:, 3 * w :])


def after(x, *deps):
    return lax.optimization_barrier((x, *deps))[0]


def local(
    tokens,
    cotangent,
    route,
    lengths,
    clip_tau,
    attn_norm_gain,
    attn_norm_bias,
    qkv_weight,
    qv_bias,
    out_weight,
    out_bias,
    mlp_norm_gain,
    mlp_norm_bias,
    up_weight,
    up_bias,
    down_weight,
    down_bias,
):
    n_dp = lax.axis_size("dp")
    n_bits = n_dp.bit_length() - 1
    rs_bits = [b for b in range(n_bits) if b not in AG_BITS]
    masks = [1 << AG_BITS[0], 1 << AG_BITS[1], (1 << AG_BITS[0]) | (1 << AG_BITS[1])]
    me = lax.axis_index("dp")
    core = lax.axis_index("tensor")
    rows, width = tokens.shape
    group = 2 * rows
    cols = qkv_weight.shape[2]
    hidden = up_weight.shape[1]
    q_cols = cols // 4
    q_hidden = hidden // 4
    quarter = ((me >> AG_BITS[0]) & 1) + 2 * ((me >> AG_BITS[1]) & 1)
    sc = jnp.concatenate([jnp.stack([core, me, quarter, core]).astype(I32), lengths[0]])

    def swap(x):
        return lax.ppermute(x, "tensor", [(0, 1), (1, 0)])

    def hop(x, mask):
        return lax.ppermute(x, "dp", [(i, i ^ mask) for i in range(n_dp)])

    def exchange(x):
        return lax.all_to_all(x, "dp", split_axis=0, concat_axis=0, tiled=True)

    def share(own):
        got = [hop(own[:rows], m) for m in masks]
        return got + [swap(g) for g in got]

    w_qkv = jnp.transpose(qkv_weight, (1, 0, 2))
    vecs = jnp.concatenate(
        [attn_norm_gain, attn_norm_bias, out_bias, mlp_norm_gain, mlp_norm_bias, down_bias, up_bias]
    ).astype(F32).reshape(-1, width)

    msg, msg_cot, pick = kernel_call(
        functools.partial(route_kernel, n_dp),
        [((rows, width + PAD), BF16), ((rows, width), BF16), ((rows, rows), BF16)],
        [route.reshape(1, rows), lengths, tokens, cotangent],
        hbm={0: whole((1, rows)), 1: whole(lengths.shape), 2: whole(tokens.shape), 3: whole(tokens.shape)},
        flops=4 * rows * rows * width,
    )
    got = after(exchange(msg), vecs, sc)
    got_cot = exchange(msg_cot)
    other = swap(got)
    x, normed, qkv, lse, tops, part = kernel_call(
        attn_kernel,
        [
            ((group, width), BF16),
            ((group, width), BF16),
            ((group, 3 * cols), BF16),
            ((group, PAD), F32),
            ((cols // HD, PAD), F32),
            ((group, width), BF16),
        ],
        [sc, got, other, vecs, w_qkv, qv_bias, out_weight],
        smem=(0,),
        hbm={4: (w_qkv.shape, by_row(3)), 5: whole(qv_bias.shape), 6: whole(out_weight.shape)},
        flops=2 * group * width * 4 * cols * 3,
        scratch=[pltpu.VMEM((group, cols), BF16)],
        limit=20,
    )
    middle, mid, cot, msg_mlp = kernel_call(
        middle_kernel,
        [((group, width), F32), ((group, width), BF16), ((group, width), BF16), ((rows, 2 * width), BF16)],
        [x, part, swap(part), vecs, got, other, got_cot, swap(got_cot)],
        flops=1 << 28,
    )
    m1, m2 = (hop(msg_mlp, m) for m in masks[:2])
    gmid_part, mlp_mine, mlp_other, up_sums = kernel_call(
        mlp_kernel,
        [((group, width), BF16), ((rows, width), F32), ((rows, width), BF16), ((1, hidden), F32)],
        [mid, cot, vecs, up_weight, down_weight],
        hbm={3: (up_weight.shape, tiles(hidden // TILE, 1)), 4: (down_weight.shape, tiles(hidden // TILE, 0))},
        flops=2 * group * width * hidden * 4,
        scratch=[pltpu.VMEM((group, width), F32), pltpu.VMEM((group, width), F32)],
        limit=24,
    )
    gmid_part, m1, m2 = lax.optimization_barrier((gmid_part, m1, m2))
    m3 = hop(after(msg_mlp, gmid_part), masks[2])
    o1, o2 = swap(m1), swap(m2)
    gmid_recv = swap(gmid_part)
    gmid, gattn, mid_sums, msg_attn = kernel_call(
        gmid_kernel,
        [((rows, width), F32), ((group, width), BF16), ((8, width), F32), ((rows, 2 * width), BF16)],
        [gmid_part, gmid_recv, middle, cot, normed, vecs],
        flops=1 << 28,
    )
    gn_mine, gn_other, qkv_sums = kernel_call(
        attn_grad_kernel,
        [((rows, width), F32), ((rows, width), BF16), ((3, cols), F32)],
        [sc, gattn, out_weight, qkv, lse, w_qkv],
        smem=(0,),
        hbm={2: whole(out_weight.shape), 5: (w_qkv.shape, by_row(3))},
        flops=2 * group * width * 4 * cols * 3,
        scratch=[pltpu.VMEM((group, 3 * cols), BF16)],
        limit=20,
    )
    gn_other, m3, o1, o2 = lax.optimization_barrier((gn_other, m3, o1, o2))
    gn_recv = swap(gn_other)
    msg_attn = after(msg_attn, gn_other)
    a1, a2 = (hop(msg_attn, m) for m in masks[:2])
    mlp_shared = [m1, m2, m3, o1, o2, swap(m3)]
    back, norm_sums = kernel_call(
        last_kernel,
        [((rows, 2 * width), BF16), ((2, width), F32)],
        [gn_mine, gn_recv, x, gmid, middle, mlp_mine, swap(mlp_other), vecs, got],
        flops=1 << 28,
    )
    restored = exchange(back)

    block = width // n_dp
    first = rs_bits[0]
    def step(i, recv, keep):
        n, w = keep.shape
        left = [b for b in range(n_bits) if b not in rs_bits[:i]]
        run = run_lengths(left, block)[rs_bits[i]]
        return kernel_call(
            functools.partial(step_kernel, rs_bits[i], run),
            [((n // 2, w), BF16), ((n // 2, w), F32)],
            [sc, keep, recv],
            smem=(0,),
            flops=1 << 26,
            scratch=[pltpu.VMEM((n, w), F32)],
        )

    half = ((width // 2, q_hidden), BF16), ((width // 2, q_hidden), F32)
    send_down, keep_down, send_up, keep_up = kernel_call(
        functools.partial(mlp_weights_kernel, n_bits, first),
        [half[0], half[1], half[0], half[1]],
        [sc, after(mid, norm_sums), cot] + mlp_shared + [up_bias.reshape(1, hidden), up_weight, down_weight],
        smem=(0,),
        hbm={
            9: ((1, q_hidden), columns(q_hidden, 1)),
            10: ((width, q_hidden), columns(q_hidden, 1)),
            11: ((q_hidden, width), columns(q_hidden, 0)),
        },
        limit=28,
        flops=2 * 4 * group * width * q_hidden * 4,
        scratch=[
            pltpu.VMEM((4 * group, width), BF16),
            pltpu.VMEM((4 * group, width), BF16),
            pltpu.VMEM((width, q_hidden), F32),
        ],
    )
    send_down, send_up, a1, a2, restored = lax.optimization_barrier((send_down, send_up, a1, a2, restored))
    recv_down = hop(send_down, 1 << first)
    a3 = hop(after(msg_attn, send_up), masks[2])
    b1, b2 = swap(a1), swap(a2)
    a3, recv_down, b1, b2, send_up = lax.optimization_barrier((a3, recv_down, b1, b2, send_up))
    send_down, keep_down = step(1, recv_down, keep_down)
    recv_down, recv_up = hop(send_down, 1 << rs_bits[1]), hop(send_up, 1 << first)
    attn_shared = [a1, a2, a3, b1, b2, swap(a3)]
    out_tokens, grad_tokens = kernel_call(
        restore_kernel, [((rows, width), BF16)] * 2, [pick, restored], flops=1 << 27
    )

    send_attn, keep_attn = kernel_call(
        functools.partial(attn_weights_kernel, n_bits, first, n_dp),
        [((width // 2, 4 * q_cols), BF16), ((width // 2, 4 * q_cols), F32)],
        [sc, got, after(normed, send_up), gattn] + attn_shared + [qv_bias, w_qkv, out_weight],
        smem=(0,),
        hbm={
            10: ((2, q_cols), columns(q_cols, 1)),
            11: ((3, width, q_cols), columns(q_cols, 1)),
            12: ((q_cols, width), columns(q_cols, 0)),
        },
        limit=28,
        flops=2 * 4 * group * width * q_cols * 12,
        scratch=[
            pltpu.VMEM((4 * group, width), BF16),
            pltpu.VMEM((4 * group, width), BF16),
            pltpu.VMEM((4 * group, q_cols), BF16),
            pltpu.VMEM((4 * group, 3 * q_cols), BF16),
            pltpu.VMEM((width, 4 * q_cols), F32),
        ],
    )

    send_attn, recv_down, recv_up = lax.optimization_barrier((send_attn, recv_down, recv_up))
    attn_done = send_attn

    recv_attn = hop(send_attn, 1 << first)
    send_up, keep_up = step(1, recv_up, keep_up)
    recv_up = hop(send_up, 1 << rs_bits[1])
    send_attn, keep_attn = step(1, recv_attn, keep_attn)
    recv_attn = hop(send_attn, 1 << rs_bits[1])

    def rest(recv, keep):
        for i in range(2, len(rs_bits)):
            send, keep = step(i, recv, keep)
            recv = hop(send, 1 << rs_bits[i])
        return keep, recv

    def hand_out(*pairs):
        n, w = pairs[0][0].shape
        w *= len(pairs)
        pieces = kernel_call(
            functools.partial(pieces_kernel, len(pairs)),
            [((block, w), F32)] + [((block, w), BF16)] * 3,
            [sc] + [a for pair in pairs for a in pair],
            smem=(0,),
            flops=1 << 26,
            scratch=[pltpu.VMEM((n, w), F32)],
        )
        return [pieces[0]] + [hop(p, m) for p, m in zip(pieces[1:], masks)]

    mlp_pieces = hand_out(rest(recv_down, keep_down), rest(recv_up, keep_up))
    attn_pieces = hand_out(rest(recv_attn, keep_attn))
    grad_down, grad_up = kernel_call(
        join_mlp_kernel, [((block, hidden), F32), ((block, hidden), F32)], [sc] + mlp_pieces, smem=(0,)
    )
    grad_down = grad_down.T
    grad_qkv, grad_out = kernel_call(
        join_attn_kernel, [((3, block, cols), F32), ((block, cols), F32)], [sc] + attn_pieces, smem=(0,)
    )
    grad_qkv = jnp.transpose(grad_qkv, (1, 0, 2))
    grad_out = grad_out.T

    n_vec = 6 * width
    sums = jnp.concatenate(
        [
            norm_sums.reshape(-1),
            mid_sums[:4].reshape(-1),
            qkv_sums[0],
            qkv_sums[2],
            up_sums.reshape(-1),
        ]
    )
    n_sum = sums.size
    sums = after(sums, attn_done)
    msg = jnp.concatenate([sums, jnp.pad(tops[:, 0], (0, PAD - tops.shape[0]))]).reshape(-1, PAD)
    is_top = iota(msg.shape, 0) == n_sum // PAD
    for b in range(n_bits):
        came = hop(msg, 1 << b)
        msg = jnp.where(is_top, jnp.maximum(msg, came), msg + came)
    global_top = msg[-1, : tops.shape[0]]
    theirs = swap(msg).reshape(-1)
    msg = msg.reshape(-1)
    vector_sum = (msg[:n_vec] + theirs[:n_vec]).reshape(6, width)
    own, oth = msg[n_vec:n_sum], theirs[n_vec:n_sum]
    one = jnp.where(core == 0, own, oth)
    two = jnp.where(core == 0, oth, own)
    qv_sum = jnp.stack(
        [
            jnp.concatenate([one[:cols], two[:cols]]),
            jnp.concatenate([one[cols : 2 * cols], two[cols : 2 * cols]]),
        ]
    )
    up_sum = jnp.concatenate([one[2 * cols :], two[2 * cols :]])

    threshold = clip_tau[0].astype(F32)
    head_factor = jnp.sqrt(threshold / jnp.maximum(global_top, threshold))
    column_factor = jnp.repeat(head_factor, HD)
    clipped_qk = pl.pallas_call(
        clip_kernel,
        grid=(4,),
        out_shape=jax.ShapeDtypeStruct((width, 2, cols), BF16),
        in_specs=[
            pl.BlockSpec((2, width // 4, cols), lambda i: (0, i, 0)),
            pl.BlockSpec((1, cols), lambda i: (0, 0)),
        ],
        out_specs=pl.BlockSpec((width // 4, 2, cols), lambda i: (i, 0, 0)),
        name="clip_kernel",
    )(w_qkv, column_factor.reshape(1, cols))
    clipped_q_bias = (f(qv_bias[0]) * column_factor).astype(BF16)
    return (
        out_tokens,
        grad_tokens,
        grad_qkv,
        grad_out,
        grad_up,
        grad_down,
        qv_sum,
        up_sum,
        vector_sum,
        head_factor,
        clipped_qk,
        clipped_q_bias,
    )

def solution(mesh):
    placed = (
        P(("dp", "tensor"), None),
        P(("dp", "tensor"), None),
        P(("dp", "tensor")),
        P("dp", None),
        P(),
        P(),
        P(),
        P(None, None, "tensor"),
        P(None, "tensor"),
        P("tensor", None),
        P(),
        P(),
        P(),
        P(None, "tensor"),
        P("tensor"),
        P("tensor", None),
        P(),
    )
    return jax.shard_map(
        local,
        mesh=mesh,
        in_specs=placed,
        out_specs=(
            P(("dp", "tensor"), None),
            P(("dp", "tensor"), None),
            P("dp", None, "tensor"),
            P("tensor", "dp"),
            P("dp", "tensor"),
            P("tensor", "dp"),
            P(),
            P(),
            P(),
            P("tensor"),
            P(None, None, "tensor"),
            P("tensor"),
        ),
        check_vma=False,
    )
```

```python
import functools
import jax
import jax.numpy as jnp
from jax import lax
from jax.experimental import pallas as pl
from jax.experimental.pallas import tpu as pltpu
from jax.sharding import PartitionSpec as P

HD = 64
AG_BITS = (0, 2)
PAD = 128
COST = 1

epsilon = 1e-05
masked_value = -1e30
gelu_coef = 0.7978845608028654
F32 = jnp.float32
BF16 = jnp.bfloat16
I32 = jnp.int32


def f(x):
    return x.astype(F32)


def dot(a, b, ca, cb):
    return lax.dot_general(a, b, (((ca,), (cb,)), ((), ())), preferred_element_type=F32)


def nn(a, b):
    return dot(a, b, 1, 0)


def nt(a, b):
    return dot(a, b, 1, 1)


def tn(a, b):
    return dot(a, b, 0, 0)


def norm_stats(values):
    row_mean = jnp.mean(values, axis=-1, keepdims=True)
    centered = values - row_mean
    variance = jnp.mean(centered * centered, axis=-1, keepdims=True)
    inv = lax.rsqrt(variance + epsilon)
    return centered * inv, inv


def norm_grad(xhat, inv, gain, grad):
    scaled = grad * gain
    a = jnp.mean(scaled, axis=-1, keepdims=True)
    b = jnp.mean(scaled * xhat, axis=-1, keepdims=True)
    return inv * (scaled - a - xhat * b)


def gelu_parts(p):
    p2 = p * p
    th = jnp.tanh(gelu_coef * (p + 0.044715 * p2 * p))
    half = 0.5 * (1.0 + th)
    slope = half + 0.5 * p * (1.0 - th * th) * (gelu_coef * (1.0 + 3.0 * 0.044715 * p2))
    return p * half, slope


def iota(shape, axis):
    return lax.broadcasted_iota(I32, shape, axis)


def place_matrix(ids):
    rows = ids.shape[0]
    return (ids == f(iota((rows, rows), 1))).astype(BF16)


def pair_mask(ends, core, rows):
    group = 2 * rows
    pos_r = (iota((group, 1), 0) + core * rows) & (group - 1)
    pos_c = (iota((1, group), 1) + core * rows) & (group - 1)
    sid_r = sum((pos_r >= e).astype(I32) for e in ends)
    sid_c = sum((pos_c >= e).astype(I32) for e in ends)
    sid_r = jnp.where(pos_r < ends[-1], sid_r, -1)
    same = (sid_r == sid_c).astype(I32) * (pos_c <= pos_r).astype(I32)
    diagonal = (pos_r == pos_c).astype(I32)
    return (same + diagonal) > 0, sid_r >= 0


def half_lanes():
    lane = iota((1, PAD), 1)
    low = (lane < HD).astype(F32)
    return (low.astype(BF16), (1.0 - low).astype(BF16)), (low, 1.0 - low)


def head_probs(q2, k2, lanes, mask):
    s = jnp.where(mask, nt(q2 * lanes, k2) * 0.125, masked_value)
    top = jnp.max(s, axis=-1, keepdims=True)
    e = jnp.exp(s - top)
    total = jnp.sum(e, axis=-1, keepdims=True)
    return e, top, total


def head_grad(q2, k2, v2, gc2, lanes, p):
    gp = nt(gc2 * lanes, v2)
    row_dot = jnp.sum(p * gp, axis=-1, keepdims=True)
    ds = (p * (gp - row_dot)).astype(BF16)
    return nn(ds, k2) * 0.125, tn(ds, q2) * 0.125, tn(p.astype(BF16), gc2)


class Fetched:
    def __init__(self, ref, copies):
        self.ref, self.copies, self.shape = ref, copies, getattr(ref, "shape", None)

    def wait(self, k=None):
        for c in self.copies if k is None else [self.copies[k]]:
            c.wait()
        return self.ref


def whole(shape):
    return shape, lambda src, dst, sc: [(src, dst)]


def kernel_call(body, outs, args, smem=(), hbm=None, flops=0, scratch=(), limit=12):
    hbm = hbm or {}
    specs = []
    n_bytes = 0
    for i, a in enumerate(args):
        n_bytes += a.size * a.dtype.itemsize
        space = pltpu.HBM if i in hbm else pltpu.SMEM if i in smem else pltpu.VMEM
        specs.append(pl.BlockSpec(memory_space=space))
    shapes = [jax.ShapeDtypeStruct(s, d) for s, d in outs]
    out_specs = [pl.BlockSpec(memory_space=pltpu.VMEM) for _ in outs]
    args = [pltpu.with_memory_space_constraint(a, pltpu.HBM) if i in hbm else a for i, a in enumerate(args)]
    n_in, n_out, n_scratch = len(args), len(outs), len(scratch)
    extra = []
    own = [i for i, (shape, _) in hbm.items() if shape is not None]
    for i in own:
        extra.append(pltpu.VMEM(hbm[i][0], args[i].dtype))
    n_chunks = {}
    for i, (shape, chunks) in hbm.items():
        n_chunks[i] = getattr(chunks, "count", 1)
        extra.append(pltpu.SemaphoreType.DMA((n_chunks[i],)))

    def run(*refs):
        ins = list(refs[:n_in])
        rest = refs[n_in + n_out + n_scratch :]
        sc = ins[0]
        for j, (i, (_, chunks)) in enumerate(hbm.items()):
            dst = rest[own.index(i)] if i in own else refs[n_in + n_out :]
            sem = rest[len(own) + j]
            copies = [
                pltpu.make_async_copy(a, b, sem.at[k]) for k, (a, b) in enumerate(chunks(ins[i], dst, sc))
            ]
            for c in copies:
                c.start()
            ins[i] = Fetched(dst, copies)
        body(*ins, *refs[n_in : n_in + n_out + n_scratch])

    return pl.pallas_call(
        run,
        out_shape=shapes,
        in_specs=specs,
        out_specs=out_specs,
        scratch_shapes=list(scratch) + extra,
        compiler_params=pltpu.CompilerParams(vmem_limit_bytes=limit << 20),
        cost_estimate=pl.CostEstimate(
            flops=int(flops * COST), transcendentals=0, bytes_accessed=int(n_bytes * COST)
        ),
        name=body.func.__name__ if hasattr(body, "func") else body.__name__,
    )(*args)


def chunked(count, make):
    def chunks(src, dst, sc):
        return [make(src, dst, sc, k) for k in range(count)]

    chunks.count = count
    return chunks


def gathered(own_args, shared_args, rows):
    spec = {}
    for i, at in own_args:
        spec[i] = (None, chunked(1, lambda src, dst, sc, k, at=at: (src, dst[at].at[pl.ds(0, 2 * rows), :])))
    for j, i in enumerate(shared_args):

        def make(src, dst, sc, k, j=j):
            width = dst[0].shape[1]
            return src.at[:, pl.ds(k * width, width)], dst[k].at[pl.ds((2 + j) * rows, rows), :]

        spec[i] = (None, chunked(2, make))
    return spec


def by_row(count):
    return chunked(count, lambda src, dst, sc, k: (src.at[k], dst.at[k]))


def tiles(count, axis):
    def make(src, dst, sc, k):
        at = pl.ds(k * TILE, TILE)
        return (src.at[at, :], dst.at[at, :]) if axis == 0 else (src.at[:, at], dst.at[:, at])

    return chunked(count, make)


def columns(n, axis):
    def chunks(src, dst, sc):
        at = pl.ds(pl.multiple_of(sc[2] * n, n), n)
        if axis == 0:
            return [(src.at[at, :], dst)]
        return [(src.at[(slice(None),) * (len(src.shape) - 1) + (at,)], dst)]

    return chunks


def route_kernel(n_dp, route, lens, tokens, cotangent, msg, pick_out):
    rows, width = tokens.shape
    row = jnp.broadcast_to(f(route.wait()[...]), (rows, rows))
    col = row.T
    group = float(2 * rows)
    dest_r = jnp.floor(row / group)
    dest_c = jnp.floor(col / group)
    before = iota((rows, rows), 0) < iota((rows, rows), 1)
    same = jnp.where(before, (dest_r == dest_c).astype(F32), 0.0)
    rank = dest_r[0:1] * (rows // n_dp) + jnp.sum(same, axis=0, keepdims=True)
    pick = (jnp.broadcast_to(rank, (rows, rows)) == f(iota((rows, rows), 0))).astype(F32)
    place = row - jnp.floor(row / float(rows)) * float(rows)
    ids = jnp.sum(pick * place, axis=1, keepdims=True)
    lane = iota((rows, PAD), 1)
    extra = jnp.where(lane == 0, ids, 0.0)
    lens = f(lens.wait()[...])
    for i in range(4):
        extra = jnp.where(lane == i + 1, lens[:, i : i + 1], extra)
    pick_b = pick.astype(BF16)
    pick_out[...] = pick_b
    msg[:, :width] = nn(pick_b, tokens.wait()[...]).astype(BF16)
    msg[:, 2 * width :] = extra.astype(BF16)
    msg[:, width : 2 * width] = nn(pick_b, cotangent.wait()[...]).astype(BF16)


def ends_of(sc):
    e = [sc[4]]
    for i in range(1, 4):
        e.append(e[-1] + sc[4 + i])
    return e


def attn_kernel(
    sc, mine, other, vecs, w_qkv, qv_bias, w_out, x_out, normed_out, qkv_out, lse_out, top_out, part_out, ctx_out
):
    rows = mine.shape[0]
    width = w_out.shape[1]
    cols = w_out.shape[0]
    for i, half in enumerate((mine, other)):
        put = place_matrix(f(half[:, 2 * width : 2 * width + 1]))
        x = tn(put, half[:, :width])
        s = slice(i * rows, (i + 1) * rows)
        x_out[s, :] = x.astype(BF16)
        xhat, _ = norm_stats(x)
        normed_out[s, :] = (xhat * vecs[0:1, :] + vecs[1:2, :]).astype(BF16)
    normed = normed_out[...]
    qv_bias = qv_bias.wait()
    for c in range(3):
        y = nn(normed, w_qkv.wait(c)[c])
        if c == 0:
            y = y + f(qv_bias[0:1, :])
        if c == 2:
            y = y + f(qv_bias[1:2, :])
        qkv_out[:, c * cols : (c + 1) * cols] = y.astype(BF16)
    mask, live = pair_mask(ends_of(sc), sc[0], rows)
    lanes_b, lanes_f = half_lanes()
    lane = iota((1, PAD), 1)
    lse = jnp.zeros((2 * rows, PAD), F32)
    for pair in range(cols // PAD):
        s = slice(pair * PAD, (pair + 1) * PAD)
        q2 = qkv_out[:, s]
        k2 = qkv_out[:, slice(cols + pair * PAD, cols + (pair + 1) * PAD)]
        v2 = qkv_out[:, slice(2 * cols + pair * PAD, 2 * cols + (pair + 1) * PAD)]
        out = jnp.zeros((2 * rows, PAD), F32)
        for i in range(2):
            e, top, total = head_probs(q2, k2, lanes_b[i], mask)
            probs = (e * (1.0 / total)).astype(BF16)
            out = out + nn(probs, v2) * lanes_f[i]
            h = 2 * pair + i
            lse = jnp.where(lane == h, top + jnp.log(total), lse)
            best = jnp.max(jnp.where(live, top, masked_value), axis=0, keepdims=True)
            top_out[h : h + 1, :] = jnp.broadcast_to(best, (1, PAD))
        ctx_out[:, s] = out.astype(BF16)
    lse_out[...] = lse
    part_out[...] = nn(ctx_out[...], w_out.wait()[...]).astype(BF16)


def middle_kernel(x, part, recv, vecs, mine, other, middle_out, mid_out, cot_out, msg_out):
    rows, width = msg_out.shape[0], x.shape[1]
    for i, half in enumerate((mine, other)):
        s = slice(i * rows, (i + 1) * rows)
        o = slice((1 - i) * rows, (2 - i) * rows)
        put = place_matrix(f(half[:, 2 * width : 2 * width + 1]))
        cot = tn(put, half[:, width : 2 * width]).astype(BF16)
        cot_out[s, :] = cot
        middle = f(x[s, :]) + (f(part[s, :]) + f(recv[o, :])) + vecs[2:3, :]
        middle_out[s, :] = middle
        mhat, _ = norm_stats(middle)
        mid = (mhat * vecs[3:4, :] + vecs[4:5, :]).astype(BF16)
        mid_out[s, :] = mid
        if i == 0:
            msg_out[:, :width] = mid
            msg_out[:, width:] = cot


TILE = 512


def mlp_kernel(mid, cot, vecs, up, down, gmid_out, mine_out, other_out, sums_out, acc, acc_y):
    width, hidden = up.shape
    rows = mine_out.shape[0]
    per_row = width // TILE
    for t in range(hidden // TILE):
        s = slice(t * TILE, (t + 1) * TILE)
        bias = vecs[6 + t // per_row : 7 + t // per_row, (t % per_row) * TILE : (t % per_row + 1) * TILE]
        act, slope = gelu_parts(nn(mid[...], up.wait(t)[:, s]) + bias)
        gpre = (nt(cot[...], down.wait(t)[s, :]) * slope).astype(BF16)
        sums_out[:, s] = jnp.sum(f(gpre), axis=0, keepdims=True)
        g = nt(gpre, up.ref[:, s])
        y = nn(act.astype(BF16), down.ref[s, :])
        if t == 0:
            acc[...] = g
            acc_y[...] = y
        else:
            acc[...] += g
            acc_y[...] += y
    gmid_out[...] = acc[...].astype(BF16)
    mine_out[...] = acc_y[:rows, :]
    other_out[...] = acc_y[rows:, :].astype(BF16)


def gmid_kernel(part, recv, middle, cot, normed, vecs, gmid_out, gattn_out, sums_out, msg_out):
    rows, width = gmid_out.shape
    msg_out[:, width:] = normed[:rows, :]
    for i in range(2):
        s = slice(i * rows, (i + 1) * rows)
        o = slice((1 - i) * rows, (2 - i) * rows)
        g = f(part[s, :]) + f(recv[o, :])
        mhat, inv = norm_stats(middle[s, :])
        c = f(cot[s, :])
        gm = c + norm_grad(mhat, inv, vecs[3:4, :], g)
        gattn = gm.astype(BF16)
        gattn_out[s, :] = gattn
        if i == 0:
            gmid_out[...] = gm
            msg_out[:, :width] = gattn
            sums_out[0:1, :] = jnp.sum(gm, axis=0, keepdims=True)
            sums_out[1:2, :] = jnp.sum(g * mhat, axis=0, keepdims=True)
            sums_out[2:3, :] = jnp.sum(g, axis=0, keepdims=True)
            sums_out[3:4, :] = jnp.sum(c, axis=0, keepdims=True)
            sums_out[4:8, :] = jnp.zeros((4, sums_out.shape[1]), F32)


def attn_grad_kernel(sc, gattn, w_out, qkv, lse, w_qkv, mine_out, other_out, sums_out, gqkv):
    rows = gattn.shape[0] // 2
    cols = w_out.shape[0]
    mask, _ = pair_mask(ends_of(sc), sc[0], rows)
    gctx = nt(gattn[...], w_out.wait()[...]).astype(BF16)
    lanes_b, lanes_f = half_lanes()
    for pair in range(cols // PAD):
        cut = [slice(c * cols + pair * PAD, c * cols + (pair + 1) * PAD) for c in range(3)]
        q2, k2, v2 = (qkv[:, c] for c in cut)
        gc2 = gctx[:, pair * PAD : (pair + 1) * PAD]
        total = None
        for i in range(2):
            h = 2 * pair + i
            s = jnp.where(mask, nt(q2 * lanes_b[i], k2) * 0.125, masked_value)
            p = jnp.exp(s - lse[:, h : h + 1])
            g3 = [g * lanes_f[i] for g in head_grad(q2, k2, v2, gc2, lanes_b[i], p)]
            total = g3 if total is None else [a + b for a, b in zip(total, g3)]
        for c in range(3):
            g = total[c].astype(BF16)
            gqkv[:, cut[c]] = g
            sums_out[c : c + 1, pair * PAD : (pair + 1) * PAD] = jnp.sum(f(g), axis=0, keepdims=True)
    y = sum(nt(gqkv[:, c * cols : (c + 1) * cols], w_qkv.wait(c)[c]) for c in range(3))
    mine_out[...] = y[:rows]
    other_out[...] = y[rows:].astype(BF16)


def last_kernel(part, recv, x, gmid, middle, y_mine, y_other, vecs, ids, msg_out, sums_out):
    rows, width = part.shape
    put = place_matrix(f(ids[:, 2 * width : 2 * width + 1]))
    res = middle[:rows, :] + (y_mine[...] + f(y_other[...])) + vecs[5:6, :]
    msg_out[:, :width] = nn(put, res.astype(BF16)).astype(BF16)
    g = part[...] + f(recv[...])
    xhat, inv = norm_stats(f(x[:rows, :]))
    grad = (gmid[...] + norm_grad(xhat, inv, vecs[0:1, :], g)).astype(BF16)
    sums_out[0:1, :] = jnp.sum(g * xhat, axis=0, keepdims=True)
    sums_out[1:2, :] = jnp.sum(g, axis=0, keepdims=True)
    msg_out[:, width:] = nn(put, grad).astype(BF16)


def restore_kernel(pick, msg, out, grad):
    width = out.shape[1]
    y = tn(pick[...], msg[...]).astype(BF16)
    out[...] = y[:, :width]
    grad[...] = y[:, width:]


def clip_kernel(w, factor, out):
    for c in range(2):
        out[:, c, :] = (f(w[c]) * factor[...]).astype(BF16)


def run_lengths(bits, block):
    return {b: block << i for i, b in enumerate(sorted(bits))}


def split_rows(src, run, mine, send_out, keep_out, at):
    n = src.shape[0]
    for j in range(n // (2 * run)):
        k = pl.multiple_of(2 * run * j + mine * run, run)
        s = pl.multiple_of(2 * run * j + (1 - mine) * run, run)
        dst = slice(j * run, (j + 1) * run)
        keep_out[dst, at] = src[pl.ds(k, run), :]
        send_out[dst, at] = src[pl.ds(s, run), :].astype(BF16)


def mlp_weights_kernel(
    n_bits, bit, sc, mid, cot, m1, m2, m3, o1, o2, o3, vecs, up, down,
    send_down, keep_down, send_up, keep_up, mids, cots, grad,
):
    for x in (mid, cot, m1, m2, m3, o1, o2, o3):
        x.wait()
    q_hidden = down.shape[0]
    per_row = mids.shape[1] // q_hidden
    bias = jnp.zeros((1, q_hidden), F32)
    for k in range(4):
        part = vecs[6 + k // per_row : 7 + k // per_row, (k % per_row) * q_hidden : (k % per_row + 1) * q_hidden]
        bias = jnp.where(sc[2] == k, part, bias)
    mine = (sc[1] >> bit) & 1
    run = (mids.shape[1] >> n_bits) << bit
    act, slope = gelu_parts(nn(mids[...], up.wait()[...]) + bias)
    every = slice(None)
    grad[...] = tn(cots[...], act.astype(BF16))
    split_rows(grad, run, mine, send_down, keep_down, every)
    gpre = (nt(cots[...], down.wait()[...]) * slope).astype(BF16)
    grad[...] = tn(mids[...], gpre)
    split_rows(grad, run, mine, send_up, keep_up, every)


def attn_weights_kernel(
    n_bits, bit, n_dp, sc, ids, nrm, ga, m1, m2, m3, o1, o2, o3, qv_bias, w_qkv, w_out,
    send_out, keep_out, gattns, norms, ctx, gqkv, grad,
):
    for x in (ga, nrm, m1, m2, m3, o1, o2, o3):
        x.wait()
    rows = gattns.shape[0] // 8
    group = 2 * rows
    me = sc[1]
    mine = (me >> bit) & 1
    run = (norms.shape[1] >> n_bits) << bit
    masks = (0, 1 << AG_BITS[0], 1 << AG_BITS[1], (1 << AG_BITS[0]) | (1 << AG_BITS[1]))
    norm4 = norms[...]
    w_qkv, qv_bias = w_qkv.wait(), qv_bias.wait()
    q4 = (nn(norm4, w_qkv[0]) + f(qv_bias[0:1, :])).astype(BF16)
    k4 = nn(norm4, w_qkv[1]).astype(BF16)
    v4 = (nn(norm4, w_qkv[2]) + f(qv_bias[1:2, :])).astype(BF16)
    gc4 = nt(gattns[...], w_out.wait()[...]).astype(BF16)
    lanes_b, lanes_f = half_lanes()
    table = f(ids[:, 2 * norms.shape[1] :])
    from_dp = iota((rows, 1), 0) // (rows // n_dp)
    first = iota((rows, 1), 0) == from_dp * (rows // n_dp)
    for g in range(4):
        chosen = jnp.where((from_dp == (me ^ masks[g])) & first, table, 0.0)
        lens = jnp.sum(chosen, axis=0, keepdims=True)
        ends = [lens[:, 1:2]]
        for i in range(2, 5):
            ends.append(ends[-1] + lens[:, i : i + 1])
        mask, _ = pair_mask([e.astype(I32) for e in ends], sc[0], rows)
        s = slice(g * group, (g + 1) * group)
        q2, k2, v2, gc2 = q4[s], k4[s], v4[s], gc4[s]
        out = jnp.zeros((group, PAD), F32)
        total = None
        for i in range(2):
            e, _, denom = head_probs(q2, k2, lanes_b[i], mask)
            p = e * (1.0 / denom)
            out = out + nn(p.astype(BF16), v2) * lanes_f[i]
            g3 = [x * lanes_f[i] for x in head_grad(q2, k2, v2, gc2, lanes_b[i], p)]
            total = g3 if total is None else [a + b for a, b in zip(total, g3)]
        ctx[s, :] = out.astype(BF16)
        for c in range(3):
            gqkv[s, c * PAD : (c + 1) * PAD] = total[c].astype(BF16)
    grad[:, : 3 * PAD] = tn(norm4, gqkv[...])
    grad[:, 3 * PAD :] = tn(gattns[...], ctx[...])
    split_rows(grad, run, mine, send_out, keep_out, slice(None))


def step_kernel(bit, run, sc, keep, recv, send_out, keep_out, cur):
    cur[...] = keep[...] + f(recv[...])
    split_rows(cur, run, (sc[1] >> bit) & 1, send_out, keep_out, slice(None))


def pieces_kernel(n_pairs, sc, *refs):
    pairs, (own, p1, p2, p3), cur = refs[: 2 * n_pairs], refs[2 * n_pairs : -1], refs[-1]
    n = own.shape[0]
    w = pairs[0].shape[1]
    for i in range(n_pairs):
        cur[:, i * w : (i + 1) * w] = pairs[2 * i][...] + f(pairs[2 * i + 1][...])
    q = sc[2]
    for j, out in enumerate((own, p1, p2, p3)):
        out[...] = cur[pl.ds(pl.multiple_of((q ^ j) * n, n), n), :].astype(out.dtype)


def join_mlp_kernel(sc, own, p1, p2, p3, down_out, up_out):
    w = own.shape[1] // 2
    for j, p in enumerate((own, p1, p2, p3)):
        at = pl.ds(pl.multiple_of((sc[2] ^ j) * w, w), w)
        down_out[:, at] = f(p[:, :w])
        up_out[:, at] = f(p[:, w:])


def join_attn_kernel(sc, own, p1, p2, p3, qkv_out, out_out):
    w = own.shape[1] // 4
    for j, p in enumerate((own, p1, p2, p3)):
        at = pl.ds(pl.multiple_of((sc[2] ^ j) * w, w), w)
        for c in range(3):
            qkv_out[c, :, at] = f(p[:, c * w : (c + 1) * w])
        out_out[:, at] = f(p[:, 3 * w :])


def after(x, *deps):
    return lax.optimization_barrier((x, *deps))[0]


def local(
    tokens,
    cotangent,
    route,
    lengths,
    clip_tau,
    attn_norm_gain,
    attn_norm_bias,
    qkv_weight,
    qv_bias,
    out_weight,
    out_bias,
    mlp_norm_gain,
    mlp_norm_bias,
    up_weight,
    up_bias,
    down_weight,
    down_bias,
):
    n_dp = lax.axis_size("dp")
    n_bits = n_dp.bit_length() - 1
    rs_bits = [b for b in range(n_bits) if b not in AG_BITS]
    masks = [1 << AG_BITS[0], 1 << AG_BITS[1], (1 << AG_BITS[0]) | (1 << AG_BITS[1])]
    me = lax.axis_index("dp")
    core = lax.axis_index("tensor")
    rows, width = tokens.shape
    group = 2 * rows
    cols = qkv_weight.shape[2]
    hidden = up_weight.shape[1]
    q_cols = cols // 4
    q_hidden = hidden // 4
    quarter = ((me >> AG_BITS[0]) & 1) + 2 * ((me >> AG_BITS[1]) & 1)
    sc = jnp.concatenate([jnp.stack([core, me, quarter, core]).astype(I32), lengths[0]])

    def swap(x):
        return lax.ppermute(x, "tensor", [(0, 1), (1, 0)])

    def hop(x, mask):
        return lax.ppermute(x, "dp", [(i, i ^ mask) for i in range(n_dp)])

    def exchange(x):
        return lax.all_to_all(x, "dp", split_axis=0, concat_axis=0, tiled=True)

    def share(own):
        got = [hop(own[:rows], m) for m in masks]
        return got + [swap(g) for g in got]

    w_qkv = jnp.transpose(qkv_weight, (1, 0, 2))
    vecs = jnp.concatenate(
        [attn_norm_gain, attn_norm_bias, out_bias, mlp_norm_gain, mlp_norm_bias, down_bias, up_bias]
    ).astype(F32).reshape(-1, width)

    msg, pick = kernel_call(
        functools.partial(route_kernel, n_dp),
        [((rows, 2 * width + PAD), BF16), ((rows, rows), BF16)],
        [route.reshape(1, rows), lengths, tokens, cotangent],
        hbm={0: whole((1, rows)), 1: whole(lengths.shape), 2: whole(tokens.shape), 3: whole(tokens.shape)},
        flops=4 * rows * rows * width,
    )
    got = after(exchange(msg), vecs, sc)
    other = swap(got)
    x, normed, qkv, lse, tops, part = kernel_call(
        attn_kernel,
        [
            ((group, width), BF16),
            ((group, width), BF16),
            ((group, 3 * cols), BF16),
            ((group, PAD), F32),
            ((cols // HD, PAD), F32),
            ((group, width), BF16),
        ],
        [sc, got, other, vecs, w_qkv, qv_bias, out_weight],
        smem=(0,),
        hbm={4: (w_qkv.shape, by_row(3)), 5: whole(qv_bias.shape), 6: whole(out_weight.shape)},
        flops=2 * group * width * 4 * cols * 3,
        scratch=[pltpu.VMEM((group, cols), BF16)],
        limit=20,
    )
    middle, mid, cot, msg_mlp = kernel_call(
        middle_kernel,
        [((group, width), F32), ((group, width), BF16), ((group, width), BF16), ((rows, 2 * width), BF16)],
        [x, part, swap(part), vecs, got, other],
        flops=1 << 28,
    )
    m1, m2 = (hop(msg_mlp, m) for m in masks[:2])
    gmid_part, mlp_mine, mlp_other, up_sums = kernel_call(
        mlp_kernel,
        [((group, width), BF16), ((rows, width), F32), ((rows, width), BF16), ((1, hidden), F32)],
        [mid, cot, vecs, up_weight, down_weight],
        hbm={3: (up_weight.shape, tiles(hidden // TILE, 1)), 4: (down_weight.shape, tiles(hidden // TILE, 0))},
        flops=2 * group * width * hidden * 4,
        scratch=[pltpu.VMEM((group, width), F32), pltpu.VMEM((group, width), F32)],
        limit=24,
    )
    gmid_part, m1, m2 = lax.optimization_barrier((gmid_part, m1, m2))
    m3 = hop(after(msg_mlp, gmid_part), masks[2])
    o1, o2 = swap(m1), swap(m2)
    gmid_recv = swap(gmid_part)
    gmid, gattn, mid_sums, msg_attn = kernel_call(
        gmid_kernel,
        [((rows, width), F32), ((group, width), BF16), ((8, width), F32), ((rows, 2 * width), BF16)],
        [gmid_part, gmid_recv, middle, cot, normed, vecs],
        flops=1 << 28,
    )
    gn_mine, gn_other, qkv_sums = kernel_call(
        attn_grad_kernel,
        [((rows, width), F32), ((rows, width), BF16), ((3, cols), F32)],
        [sc, gattn, out_weight, qkv, lse, w_qkv],
        smem=(0,),
        hbm={2: whole(out_weight.shape), 5: (w_qkv.shape, by_row(3))},
        flops=2 * group * width * 4 * cols * 3,
        scratch=[pltpu.VMEM((group, 3 * cols), BF16)],
        limit=20,
    )
    gn_other, m3, o1, o2 = lax.optimization_barrier((gn_other, m3, o1, o2))
    gn_recv = swap(gn_other)
    msg_attn = after(msg_attn, gn_other)
    a1, a2 = (hop(msg_attn, m) for m in masks[:2])
    mlp_shared = [m1, m2, m3, o1, o2, swap(m3)]
    back, norm_sums = kernel_call(
        last_kernel,
        [((rows, 2 * width), BF16), ((2, width), F32)],
        [gn_mine, gn_recv, x, gmid, middle, mlp_mine, swap(mlp_other), vecs, got],
        flops=1 << 28,
    )

    n_vec = 6 * width
    sums = jnp.concatenate(
        [
            norm_sums.reshape(-1),
            mid_sums[:4].reshape(-1),
            qkv_sums[0],
            qkv_sums[2],
            up_sums.reshape(-1),
        ]
    )
    n_sum = sums.size
    msg = jnp.concatenate([sums, jnp.pad(tops[:, 0], (0, PAD - tops.shape[0]))]).reshape(-1, PAD)
    is_top = iota(msg.shape, 0) == n_sum // PAD

    def combine(msg, *came):
        return functools.reduce(lambda a, b: jnp.where(is_top, jnp.maximum(a, b), a + b), (msg, *came))

    came = [hop(msg, m) for m in masks]
    restored = exchange(back)

    block = width // n_dp
    first = rs_bits[0]
    def step(i, recv, keep):
        n, w = keep.shape
        left = [b for b in range(n_bits) if b not in rs_bits[:i]]
        run = run_lengths(left, block)[rs_bits[i]]
        return kernel_call(
            functools.partial(step_kernel, rs_bits[i], run),
            [((n // 2, w), BF16), ((n // 2, w), F32)],
            [sc, keep, recv],
            smem=(0,),
            flops=1 << 26,
            scratch=[pltpu.VMEM((n, w), F32)],
        )

    half = ((width // 2, q_hidden), BF16), ((width // 2, q_hidden), F32)
    send_down, keep_down, send_up, keep_up = kernel_call(
        functools.partial(mlp_weights_kernel, n_bits, first),
        [half[0], half[1], half[0], half[1]],
        [sc, after(mid, norm_sums), cot] + mlp_shared + [vecs, up_weight, down_weight],
        smem=(0,),
        hbm={
            **gathered([(1, 0), (2, 1)], [3, 6, 4, 7, 5, 8], rows),
            10: ((width, q_hidden), columns(q_hidden, 1)),
            11: ((q_hidden, width), columns(q_hidden, 0)),
        },
        limit=28,
        flops=2 * 4 * group * width * q_hidden * 4,
        scratch=[
            pltpu.VMEM((4 * group, width), BF16),
            pltpu.VMEM((4 * group, width), BF16),
            pltpu.VMEM((width, q_hidden), F32),
        ],
    )
    send_down, send_up, a1, a2, restored, *came = lax.optimization_barrier(
        (send_down, send_up, a1, a2, restored, *came)
    )
    msg = combine(msg, *came)
    a3 = hop(after(msg_attn, send_up), masks[2])
    b1, b2 = swap(a1), swap(a2)
    recv_down = hop(send_down, 1 << first)

    out_tokens, grad_tokens = kernel_call(
        restore_kernel, [((rows, width), BF16)] * 2, [pick, restored], flops=1 << 27
    )
    a3, b1, b2, recv_down, out_tokens, grad_tokens = lax.optimization_barrier(
        (a3, b1, b2, recv_down, out_tokens, grad_tokens)
    )
    attn_shared = [a1, a2, a3, b1, b2, swap(a3)]

    def hand_out(*pairs):
        n, w = pairs[0][0].shape
        w *= len(pairs)
        pieces = kernel_call(
            functools.partial(pieces_kernel, len(pairs)),
            [((block, w), F32)] + [((block, w), BF16)] * 3,
            [sc] + [a for pair in pairs for a in pair],
            smem=(0,),
            flops=1 << 26,
            scratch=[pltpu.VMEM((n, w), F32)],
        )
        return [pieces[0]] + [hop(p, m) for p, m in zip(pieces[1:], masks)]

    def clip(msg):
        threshold = clip_tau[0].astype(F32)
        head_factor = jnp.sqrt(threshold / jnp.maximum(msg[-1, : tops.shape[0]], threshold))
        column_factor = jnp.repeat(head_factor, HD)
        clipped_qk = pl.pallas_call(
            clip_kernel,
            grid=(4,),
            out_shape=jax.ShapeDtypeStruct((width, 2, cols), BF16),
            in_specs=[
                pl.BlockSpec((2, width // 4, cols), lambda i: (0, i, 0)),
                pl.BlockSpec((1, cols), lambda i: (0, 0)),
            ],
            out_specs=pl.BlockSpec((width // 4, 2, cols), lambda i: (i, 0, 0)),
            name="clip_kernel",
        )(w_qkv, column_factor.reshape(1, cols))
        return clipped_qk, head_factor, column_factor

    n_steps = len(rs_bits)
    recvs = {0: recv_down}
    sends = {1: send_up}
    keeps = {0: keep_down, 1: keep_up}
    for t in range(1, n_steps + 2):
        active = [i for i in range(3) if 0 <= t - i < n_steps]
        gate = ()
        for i in active:
            if t > i:
                sends[i], keeps[i] = step(t - i, recvs[i], keeps[i])
                gate = (sends[i],)
        for i in active:
            recvs[i] = hop(after(sends[i], *gate), 1 << rs_bits[t - i])
        extra = []
        if t <= n_steps:
            msg = after(msg, *gate)
            came = hop(msg, 1 << rs_bits[t - 1])
        if t == 1:
            send_attn, keep_attn = kernel_call(
                functools.partial(attn_weights_kernel, n_bits, first, n_dp),
                [((width // 2, 4 * q_cols), BF16), ((width // 2, 4 * q_cols), F32)],
                [sc, got, normed, gattn] + attn_shared + [qv_bias, w_qkv, out_weight],
                smem=(0,),
                hbm={
                    **gathered([(2, 1), (3, 0)], [4, 7, 5, 8, 6, 9], rows),
                    10: ((2, q_cols), columns(q_cols, 1)),
                    11: ((3, width, q_cols), columns(q_cols, 1)),
                    12: ((q_cols, width), columns(q_cols, 0)),
                },
                limit=28,
                flops=2 * 4 * group * width * q_cols * 12,
                scratch=[
                    pltpu.VMEM((4 * group, width), BF16),
                    pltpu.VMEM((4 * group, width), BF16),
                    pltpu.VMEM((4 * group, q_cols), BF16),
                    pltpu.VMEM((4 * group, 3 * q_cols), BF16),
                    pltpu.VMEM((width, 4 * q_cols), F32),
                ],
            )
            sends[2], keeps[2] = send_attn, keep_attn
            extra = [sends[2]]
        if t == n_steps + 1:
            mlp_pieces = hand_out((after(keeps[0], *gate), recvs[0]), (keeps[1], recvs[1]))
            clipped_qk, head_factor, column_factor = clip(msg)
            extra = mlp_pieces[1:] + [clipped_qk]
        done = lax.optimization_barrier([recvs[i] for i in active] + [came] + extra)
        recvs.update(zip(active, done))
        if t <= n_steps:
            msg = combine(msg, done[len(active)])
        if t == 1:
            sends[2] = done[-1]
        if t == n_steps + 1:
            mlp_pieces[1:], clipped_qk = done[-4:-1], done[-1]
    attn_pieces = hand_out((keeps[2], recvs[2]))
    grad_down, grad_up = kernel_call(
        join_mlp_kernel, [((block, hidden), F32), ((block, hidden), F32)], [sc] + mlp_pieces, smem=(0,)
    )
    grad_down, grad_up, *attn_pieces[1:] = lax.optimization_barrier((grad_down, grad_up, *attn_pieces[1:]))
    grad_down = grad_down.T
    grad_qkv, grad_out = kernel_call(
        join_attn_kernel, [((3, block, cols), F32), ((block, cols), F32)], [sc] + attn_pieces, smem=(0,)
    )
    grad_qkv = jnp.transpose(grad_qkv, (1, 0, 2))
    grad_out = grad_out.T

    theirs = swap(msg).reshape(-1)
    msg = msg.reshape(-1)
    vector_sum = (msg[:n_vec] + theirs[:n_vec]).reshape(6, width)
    own, oth = msg[n_vec:n_sum], theirs[n_vec:n_sum]
    one = jnp.where(core == 0, own, oth)
    two = jnp.where(core == 0, oth, own)
    qv_sum = jnp.stack(
        [
            jnp.concatenate([one[:cols], two[:cols]]),
            jnp.concatenate([one[cols : 2 * cols], two[cols : 2 * cols]]),
        ]
    )
    up_sum = jnp.concatenate([one[2 * cols :], two[2 * cols :]])

    clipped_q_bias = (f(qv_bias[0]) * column_factor).astype(BF16)
    return (
        out_tokens,
        grad_tokens,
        grad_qkv,
        grad_out,
        grad_up,
        grad_down,
        qv_sum,
        up_sum,
        vector_sum,
        head_factor,
        clipped_qk,
        clipped_q_bias,
    )

def solution(mesh):
    placed = (
        P(("dp", "tensor"), None),
        P(("dp", "tensor"), None),
        P(("dp", "tensor")),
        P("dp", None),
        P(),
        P(),
        P(),
        P(None, None, "tensor"),
        P(None, "tensor"),
        P("tensor", None),
        P(),
        P(),
        P(),
        P(None, "tensor"),
        P("tensor"),
        P("tensor", None),
        P(),
    )
    return jax.shard_map(
        local,
        mesh=mesh,
        in_specs=placed,
        out_specs=(
            P(("dp", "tensor"), None),
            P(("dp", "tensor"), None),
            P("dp", None, "tensor"),
            P("tensor", "dp"),
            P("dp", "tensor"),
            P("tensor", "dp"),
            P(),
            P(),
            P(),
            P("tensor"),
            P(None, None, "tensor"),
            P("tensor"),
        ),
        check_vma=False,
    )
```

```python
import functools
import jax
import jax.numpy as jnp
from jax import lax
from jax.experimental import pallas as pl
from jax.experimental.pallas import tpu as pltpu
from jax.sharding import PartitionSpec as P

HD = 64
AG_BITS = (0, 2)
PAD = 128
COST = 1

epsilon = 1e-05
masked_value = -1e30
gelu_coef = 0.7978845608028654
F32 = jnp.float32
BF16 = jnp.bfloat16
I32 = jnp.int32


def f(x):
    return x.astype(F32)


def dot(a, b, ca, cb):
    return lax.dot_general(a, b, (((ca,), (cb,)), ((), ())), preferred_element_type=F32)


def nn(a, b):
    return dot(a, b, 1, 0)


def nt(a, b):
    return dot(a, b, 1, 1)


def tn(a, b):
    return dot(a, b, 0, 0)


def norm_stats(values):
    row_mean = jnp.mean(values, axis=-1, keepdims=True)
    centered = values - row_mean
    variance = jnp.mean(centered * centered, axis=-1, keepdims=True)
    inv = lax.rsqrt(variance + epsilon)
    return centered * inv, inv


def norm_grad(xhat, inv, gain, grad):
    scaled = grad * gain
    a = jnp.mean(scaled, axis=-1, keepdims=True)
    b = jnp.mean(scaled * xhat, axis=-1, keepdims=True)
    return inv * (scaled - a - xhat * b)


def gelu_parts(p):
    p2 = p * p
    th = jnp.tanh(gelu_coef * (p + 0.044715 * p2 * p))
    half = 0.5 * (1.0 + th)
    slope = half + 0.5 * p * (1.0 - th * th) * (gelu_coef * (1.0 + 3.0 * 0.044715 * p2))
    return p * half, slope


def iota(shape, axis):
    return lax.broadcasted_iota(I32, shape, axis)


def place_matrix(ids):
    rows = ids.shape[0]
    return (ids == f(iota((rows, rows), 1))).astype(BF16)


def pair_mask(ends, core, rows):
    group = 2 * rows
    pos_r = (iota((group, 1), 0) + core * rows) & (group - 1)
    pos_c = (iota((1, group), 1) + core * rows) & (group - 1)
    sid_r = sum((pos_r >= e).astype(I32) for e in ends)
    sid_c = sum((pos_c >= e).astype(I32) for e in ends)
    sid_r = jnp.where(pos_r < ends[-1], sid_r, -1)
    same = (sid_r == sid_c).astype(I32) * (pos_c <= pos_r).astype(I32)
    diagonal = (pos_r == pos_c).astype(I32)
    return (same + diagonal) > 0, sid_r >= 0


def half_lanes():
    lane = iota((1, PAD), 1)
    low = (lane < HD).astype(F32)
    return (low.astype(BF16), (1.0 - low).astype(BF16)), (low, 1.0 - low)


def head_probs(q2, k2, lanes, mask):
    s = jnp.where(mask, nt(q2 * lanes, k2) * 0.125, masked_value)
    top = jnp.max(s, axis=-1, keepdims=True)
    e = jnp.exp(s - top)
    total = jnp.sum(e, axis=-1, keepdims=True)
    return e, top, total


def head_grad(q2, k2, v2, gc2, lanes, p):
    gp = nt(gc2 * lanes, v2)
    row_dot = jnp.sum(p * gp, axis=-1, keepdims=True)
    ds = (p * (gp - row_dot)).astype(BF16)
    return nn(ds, k2) * 0.125, tn(ds, q2) * 0.125, tn(p.astype(BF16), gc2)


class Fetched:
    def __init__(self, ref, copies):
        self.ref, self.copies, self.shape = ref, copies, getattr(ref, "shape", None)

    def wait(self, k=None):
        for c in self.copies if k is None else [self.copies[k]]:
            c.wait()
        return self.ref


def whole(shape):
    return shape, lambda src, dst, sc: [(src, dst)]


def kernel_call(body, outs, args, smem=(), hbm=None, flops=0, scratch=(), limit=12, loose=()):
    hbm = hbm or {}
    specs = []
    n_bytes = 0
    for i, a in enumerate(args):
        n_bytes += a.size * a.dtype.itemsize
        space = pl.ANY if i in loose else pltpu.HBM if i in hbm else pltpu.SMEM if i in smem else pltpu.VMEM
        specs.append(pl.BlockSpec(memory_space=space))
    shapes = [jax.ShapeDtypeStruct(s, d) for s, d in outs]
    out_specs = [pl.BlockSpec(memory_space=pltpu.VMEM) for _ in outs]
    args = [pltpu.with_memory_space_constraint(a, pltpu.HBM) if i in hbm and i not in loose else a for i, a in enumerate(args)]
    n_in, n_out, n_scratch = len(args), len(outs), len(scratch)
    extra = []
    own = [i for i, (shape, _) in hbm.items() if shape is not None]
    for i in own:
        extra.append(pltpu.VMEM(hbm[i][0], args[i].dtype))
    n_chunks = {}
    for i, (shape, chunks) in hbm.items():
        n_chunks[i] = getattr(chunks, "count", 1)
        extra.append(pltpu.SemaphoreType.DMA((n_chunks[i],)))

    def run(*refs):
        ins = list(refs[:n_in])
        rest = refs[n_in + n_out + n_scratch :]
        sc = ins[0]
        for j, (i, (_, chunks)) in enumerate(hbm.items()):
            dst = rest[own.index(i)] if i in own else refs[n_in + n_out :]
            sem = rest[len(own) + j]
            copies = [
                pltpu.make_async_copy(a, b, sem.at[k]) for k, (a, b) in enumerate(chunks(ins[i], dst, sc))
            ]
            for c in copies:
                c.start()
            ins[i] = Fetched(dst, copies)
        body(*ins, *refs[n_in : n_in + n_out + n_scratch])

    return pl.pallas_call(
        run,
        out_shape=shapes,
        in_specs=specs,
        out_specs=out_specs,
        scratch_shapes=list(scratch) + extra,
        compiler_params=pltpu.CompilerParams(vmem_limit_bytes=limit << 20),
        cost_estimate=pl.CostEstimate(
            flops=int(flops * COST), transcendentals=0, bytes_accessed=int(n_bytes * COST)
        ),
        name=body.func.__name__ if hasattr(body, "func") else body.__name__,
    )(*args)


def chunked(count, make):
    def chunks(src, dst, sc):
        return [make(src, dst, sc, k) for k in range(count)]

    chunks.count = count
    return chunks


def gathered(own_args, shared_args, rows, start=2):
    spec = {}
    for i, at in own_args:
        spec[i] = (None, chunked(1, lambda src, dst, sc, k, at=at: (src, dst[at].at[pl.ds(0, 2 * rows), :])))
    for j, i in enumerate(shared_args):

        def make(src, dst, sc, k, j=j):
            width = dst[0].shape[1]
            return src.at[:, pl.ds(k * width, width)], dst[k].at[pl.ds((start + j) * rows, rows), :]

        spec[i] = (None, chunked(2, make))
    return spec


def by_row(count):
    return chunked(count, lambda src, dst, sc, k: (src.at[k], dst.at[k]))


def tiles(count, axis):
    def make(src, dst, sc, k):
        at = pl.ds(k * TILE, TILE)
        return (src.at[at, :], dst.at[at, :]) if axis == 0 else (src.at[:, at], dst.at[:, at])

    return chunked(count, make)


def columns(n, axis):
    def chunks(src, dst, sc):
        at = pl.ds(pl.multiple_of(sc[2] * n, n), n)
        if axis == 0:
            return [(src.at[at, :], dst)]
        return [(src.at[(slice(None),) * (len(src.shape) - 1) + (at,)], dst)]

    return chunks


def route_kernel(n_dp, route, lens, tokens, cotangent, msg, pick_out):
    rows, width = tokens.shape
    row = jnp.broadcast_to(f(route.wait()[...]), (rows, rows))
    col = row.T
    group = float(2 * rows)
    dest_r = jnp.floor(row / group)
    dest_c = jnp.floor(col / group)
    before = iota((rows, rows), 0) < iota((rows, rows), 1)
    same = jnp.where(before, (dest_r == dest_c).astype(F32), 0.0)
    rank = dest_r[0:1] * (rows // n_dp) + jnp.sum(same, axis=0, keepdims=True)
    pick = (jnp.broadcast_to(rank, (rows, rows)) == f(iota((rows, rows), 0))).astype(F32)
    place = row - jnp.floor(row / float(rows)) * float(rows)
    ids = jnp.sum(pick * place, axis=1, keepdims=True)
    lane = iota((rows, PAD), 1)
    extra = jnp.where(lane == 0, ids, 0.0)
    lens = f(lens.wait()[...])
    for i in range(4):
        extra = jnp.where(lane == i + 1, lens[:, i : i + 1], extra)
    pick_b = pick.astype(BF16)
    pick_out[...] = pick_b
    msg[:, :width] = nn(pick_b, tokens.wait()[...]).astype(BF16)
    msg[:, 2 * width :] = extra.astype(BF16)
    msg[:, width : 2 * width] = nn(pick_b, cotangent.wait()[...]).astype(BF16)


def ends_of(sc):
    e = [sc[4]]
    for i in range(1, 4):
        e.append(e[-1] + sc[4 + i])
    return e


def attn_kernel(
    sc, mine, other, vecs, w_qkv, qv_bias, w_out, x_out, normed_out, qkv_out, lse_out, top_out, part_out, ctx_out
):
    rows = mine.shape[0]
    width = w_out.shape[1]
    cols = w_out.shape[0]
    for i, half in enumerate((mine, other)):
        put = place_matrix(f(half[:, 2 * width : 2 * width + 1]))
        x = tn(put, half[:, :width])
        s = slice(i * rows, (i + 1) * rows)
        x_out[s, :] = x.astype(BF16)
        xhat, _ = norm_stats(x)
        normed_out[s, :] = (xhat * vecs[0:1, :] + vecs[1:2, :]).astype(BF16)
    normed = normed_out[...]
    qv_bias = qv_bias.wait()
    for c in range(3):
        y = nn(normed, w_qkv.wait(c)[c])
        if c == 0:
            y = y + f(qv_bias[0:1, :])
        if c == 2:
            y = y + f(qv_bias[1:2, :])
        qkv_out[:, c * cols : (c + 1) * cols] = y.astype(BF16)
    mask, live = pair_mask(ends_of(sc), sc[0], rows)
    lanes_b, lanes_f = half_lanes()
    lane = iota((1, PAD), 1)
    lse = jnp.zeros((2 * rows, PAD), F32)
    for pair in range(cols // PAD):
        s = slice(pair * PAD, (pair + 1) * PAD)
        q2 = qkv_out[:, s]
        k2 = qkv_out[:, slice(cols + pair * PAD, cols + (pair + 1) * PAD)]
        v2 = qkv_out[:, slice(2 * cols + pair * PAD, 2 * cols + (pair + 1) * PAD)]
        out = jnp.zeros((2 * rows, PAD), F32)
        for i in range(2):
            e, top, total = head_probs(q2, k2, lanes_b[i], mask)
            probs = (e * (1.0 / total)).astype(BF16)
            out = out + nn(probs, v2) * lanes_f[i]
            h = 2 * pair + i
            lse = jnp.where(lane == h, top + jnp.log(total), lse)
            best = jnp.max(jnp.where(live, top, masked_value), axis=0, keepdims=True)
            top_out[h : h + 1, :] = jnp.broadcast_to(best, (1, PAD))
        ctx_out[:, s] = out.astype(BF16)
    lse_out[...] = lse
    part_out[...] = nn(ctx_out[...], w_out.wait()[...]).astype(BF16)


def middle_kernel(x, part, recv, vecs, mine, other, middle_out, mid_out, cot_out, msg_out):
    rows, width = msg_out.shape[0], x.shape[1]
    for i, half in enumerate((mine, other)):
        s = slice(i * rows, (i + 1) * rows)
        o = slice((1 - i) * rows, (2 - i) * rows)
        put = place_matrix(f(half[:, 2 * width : 2 * width + 1]))
        cot = tn(put, half[:, width : 2 * width]).astype(BF16)
        cot_out[s, :] = cot
        middle = f(x[s, :]) + (f(part[s, :]) + f(recv[o, :])) + vecs[2:3, :]
        middle_out[s, :] = middle
        mhat, _ = norm_stats(middle)
        mid = (mhat * vecs[3:4, :] + vecs[4:5, :]).astype(BF16)
        mid_out[s, :] = mid
        if i == 0:
            msg_out[:, :width] = mid
            msg_out[:, width:] = cot


TILE = 1024


def mlp_kernel(mid, cot, vecs, up, down, gmid_out, mine_out, other_out, sums_out, acc, acc_y):
    width, hidden = up.shape
    rows = mine_out.shape[0]
    per_row = width // TILE
    for t in range(hidden // TILE):
        s = slice(t * TILE, (t + 1) * TILE)
        bias = vecs[6 + t // per_row : 7 + t // per_row, (t % per_row) * TILE : (t % per_row + 1) * TILE]
        act, slope = gelu_parts(nn(mid[...], up.wait(t)[:, s]) + bias)
        gpre = (nt(cot[...], down.wait(t)[s, :]) * slope).astype(BF16)
        sums_out[:, s] = jnp.sum(f(gpre), axis=0, keepdims=True)
        g = nt(gpre, up.ref[:, s])
        y = nn(act.astype(BF16), down.ref[s, :])
        if t == 0:
            acc[...] = g
            acc_y[...] = y
        else:
            acc[...] += g
            acc_y[...] += y
    gmid_out[...] = acc[...].astype(BF16)
    mine_out[...] = acc_y[:rows, :]
    other_out[...] = acc_y[rows:, :].astype(BF16)


def gmid_kernel(part, recv, middle, cot, normed, vecs, gmid_out, gattn_out, sums_out, msg_out):
    rows, width = gmid_out.shape
    msg_out[:, width:] = normed[:rows, :]
    for i in range(2):
        s = slice(i * rows, (i + 1) * rows)
        o = slice((1 - i) * rows, (2 - i) * rows)
        g = f(part[s, :]) + f(recv[o, :])
        mhat, inv = norm_stats(middle[s, :])
        c = f(cot[s, :])
        gm = c + norm_grad(mhat, inv, vecs[3:4, :], g)
        gattn = gm.astype(BF16)
        gattn_out[s, :] = gattn
        if i == 0:
            gmid_out[...] = gm
            msg_out[:, :width] = gattn
            sums_out[0:1, :] = jnp.sum(gm, axis=0, keepdims=True)
            sums_out[1:2, :] = jnp.sum(g * mhat, axis=0, keepdims=True)
            sums_out[2:3, :] = jnp.sum(g, axis=0, keepdims=True)
            sums_out[3:4, :] = jnp.sum(c, axis=0, keepdims=True)
            sums_out[4:8, :] = jnp.zeros((4, sums_out.shape[1]), F32)


def attn_grad_kernel(sc, gattn, w_out, qkv, lse, w_qkv, mine_out, other_out, sums_out, gqkv):
    rows = gattn.shape[0] // 2
    cols = w_out.shape[0]
    mask, _ = pair_mask(ends_of(sc), sc[0], rows)
    gctx = nt(gattn[...], w_out.wait()[...]).astype(BF16)
    lanes_b, lanes_f = half_lanes()
    for pair in range(cols // PAD):
        cut = [slice(c * cols + pair * PAD, c * cols + (pair + 1) * PAD) for c in range(3)]
        q2, k2, v2 = (qkv[:, c] for c in cut)
        gc2 = gctx[:, pair * PAD : (pair + 1) * PAD]
        total = None
        for i in range(2):
            h = 2 * pair + i
            s = jnp.where(mask, nt(q2 * lanes_b[i], k2) * 0.125, masked_value)
            p = jnp.exp(s - lse[:, h : h + 1])
            g3 = [g * lanes_f[i] for g in head_grad(q2, k2, v2, gc2, lanes_b[i], p)]
            total = g3 if total is None else [a + b for a, b in zip(total, g3)]
        for c in range(3):
            g = total[c].astype(BF16)
            gqkv[:, cut[c]] = g
            sums_out[c : c + 1, pair * PAD : (pair + 1) * PAD] = jnp.sum(f(g), axis=0, keepdims=True)
    y = sum(nt(gqkv[:, c * cols : (c + 1) * cols], w_qkv.wait(c)[c]) for c in range(3))
    mine_out[...] = y[:rows]
    other_out[...] = y[rows:].astype(BF16)


def last_kernel(part, recv, x, gmid, middle, y_mine, y_other, vecs, ids, msg_out, sums_out):
    rows, width = part.shape
    put = place_matrix(f(ids[:, 2 * width : 2 * width + 1]))
    res = middle[:rows, :] + (y_mine[...] + f(y_other[...])) + vecs[5:6, :]
    msg_out[:, :width] = nn(put, res.astype(BF16)).astype(BF16)
    g = part[...] + f(recv[...])
    xhat, inv = norm_stats(f(x[:rows, :]))
    grad = (gmid[...] + norm_grad(xhat, inv, vecs[0:1, :], g)).astype(BF16)
    sums_out[0:1, :] = jnp.sum(g * xhat, axis=0, keepdims=True)
    sums_out[1:2, :] = jnp.sum(g, axis=0, keepdims=True)
    msg_out[:, width:] = nn(put, grad).astype(BF16)


def restore_kernel(pick, msg, out, grad):
    width = out.shape[1]
    y = tn(pick[...], msg[...]).astype(BF16)
    out[...] = y[:, :width]
    grad[...] = y[:, width:]


def clip_kernel(w, factor, out):
    for c in range(2):
        out[:, c, :] = (f(w[c]) * factor[...]).astype(BF16)


def run_lengths(bits, block):
    return {b: block << i for i, b in enumerate(sorted(bits))}


def split_rows(src, run, mine, send_out, keep_out, at):
    n = src.shape[0]
    for j in range(n // (2 * run)):
        k = pl.multiple_of(2 * run * j + mine * run, run)
        s = pl.multiple_of(2 * run * j + (1 - mine) * run, run)
        dst = slice(j * run, (j + 1) * run)
        keep_out[dst, at] = src[pl.ds(k, run), :]
        send_out[dst, at] = src[pl.ds(s, run), :].astype(BF16)


def mlp_weights_kernel(
    n_bits, bit, sc, mid, cot, m1, m2, m3, o1, o2, o3, vecs, up, down,
    send_down, keep_down, send_up, keep_up, mids, cots, grad,
):
    for x in (mid, cot, m1, m2, m3, o1, o2, o3):
        x.wait()
    q_hidden = down.shape[0]
    per_row = mids.shape[1] // q_hidden
    bias = jnp.zeros((1, q_hidden), F32)
    for k in range(4):
        part = vecs[6 + k // per_row : 7 + k // per_row, (k % per_row) * q_hidden : (k % per_row + 1) * q_hidden]
        bias = jnp.where(sc[2] == k, part, bias)
    mine = (sc[1] >> bit) & 1
    run = (mids.shape[1] >> n_bits) << bit
    act, slope = gelu_parts(nn(mids[...], up.wait()[...]) + bias)
    every = slice(None)
    grad[...] = tn(cots[...], act.astype(BF16))
    split_rows(grad, run, mine, send_down, keep_down, every)
    gpre = (nt(cots[...], down.wait()[...]) * slope).astype(BF16)
    grad[...] = tn(mids[...], gpre)
    split_rows(grad, run, mine, send_up, keep_up, every)


def attn_quarter(n_dp, masks, sc, ids, qv_bias, w_qkv, w_out, gattns, norms, ctx, gqkv):
    group = norms.shape[0] // len(masks)
    rows = group // 2
    me = sc[1]
    norm4 = norms[...]
    w_qkv, qv_bias = w_qkv.wait(), qv_bias.wait()
    q4 = (nn(norm4, w_qkv[0]) + f(qv_bias[0:1, :])).astype(BF16)
    k4 = nn(norm4, w_qkv[1]).astype(BF16)
    v4 = (nn(norm4, w_qkv[2]) + f(qv_bias[1:2, :])).astype(BF16)
    gc4 = nt(gattns[...], w_out.wait()[...]).astype(BF16)
    lanes_b, lanes_f = half_lanes()
    table = f(ids[:, 2 * norms.shape[1] :])
    from_dp = iota((rows, 1), 0) // (rows // n_dp)
    first = iota((rows, 1), 0) == from_dp * (rows // n_dp)
    for g, bits in enumerate(masks):
        chosen = jnp.where((from_dp == (me ^ bits)) & first, table, 0.0)
        lens = jnp.sum(chosen, axis=0, keepdims=True)
        ends = [lens[:, 1:2]]
        for i in range(2, 5):
            ends.append(ends[-1] + lens[:, i : i + 1])
        mask, _ = pair_mask([e.astype(I32) for e in ends], sc[0], rows)
        s = slice(g * group, (g + 1) * group)
        q2, k2, v2, gc2 = q4[s], k4[s], v4[s], gc4[s]
        out = jnp.zeros((group, PAD), F32)
        total = None
        for i in range(2):
            e, _, denom = head_probs(q2, k2, lanes_b[i], mask)
            p = e * (1.0 / denom)
            out = out + nn(p.astype(BF16), v2) * lanes_f[i]
            g3 = [x * lanes_f[i] for x in head_grad(q2, k2, v2, gc2, lanes_b[i], p)]
            total = g3 if total is None else [a + b for a, b in zip(total, g3)]
        ctx[s, :] = out.astype(BF16)
        for c in range(3):
            gqkv[s, c * PAD : (c + 1) * PAD] = total[c].astype(BF16)


def attn_first_kernel(
    n_dp, masks, sc, ids, nrm, ga, m1, m2, o1, o2, qv_bias, w_qkv, w_out, grad, gattns, norms, ctx, gqkv
):
    for x in (ga, nrm, m1, m2, o1, o2):
        x.wait()
    attn_quarter(n_dp, masks, sc, ids, qv_bias, w_qkv, w_out, gattns, norms, ctx, gqkv)
    grad[:, : 3 * PAD] = tn(norms[...], gqkv[...])
    grad[:, 3 * PAD :] = tn(gattns[...], ctx[...])


def attn_weights_kernel(
    n_bits, bit, n_dp, masks, sc, ids, base, m3, o3, qv_bias, w_qkv, w_out,
    send_out, keep_out, gattns, norms, ctx, gqkv, grad,
):
    m3.wait()
    o3.wait()
    run = (norms.shape[1] >> n_bits) << bit
    attn_quarter(n_dp, masks, sc, ids, qv_bias, w_qkv, w_out, gattns, norms, ctx, gqkv)
    grad[:, : 3 * PAD] = base[:, : 3 * PAD] + tn(norms[...], gqkv[...])
    grad[:, 3 * PAD :] = base[:, 3 * PAD :] + tn(gattns[...], ctx[...])
    split_rows(grad, run, (sc[1] >> bit) & 1, send_out, keep_out, slice(None))


def step_kernel(bit, run, sc, keep, recv, send_out, keep_out, cur):
    cur[...] = keep[...] + f(recv[...])
    split_rows(cur, run, (sc[1] >> bit) & 1, send_out, keep_out, slice(None))


def pieces_kernel(n_pairs, sc, *refs):
    pairs, (own, p1, p2, p3), cur = refs[: 2 * n_pairs], refs[2 * n_pairs : -1], refs[-1]
    n = own.shape[0]
    w = pairs[0].shape[1]
    for i in range(n_pairs):
        cur[:, i * w : (i + 1) * w] = pairs[2 * i][...] + f(pairs[2 * i + 1][...])
    q = sc[2]
    for j, out in enumerate((own, p1, p2, p3)):
        out[...] = cur[pl.ds(pl.multiple_of((q ^ j) * n, n), n), :].astype(out.dtype)


def join_mlp_kernel(sc, own, p1, p2, p3, down_out, up_out):
    w = own.shape[1] // 2
    for j, p in enumerate((own, p1, p2, p3)):
        at = pl.ds(pl.multiple_of((sc[2] ^ j) * w, w), w)
        down_out[:, at] = f(p[:, :w])
        up_out[:, at] = f(p[:, w:])


def join_attn_kernel(sc, own, p1, p2, p3, qkv_out, out_out):
    w = own.shape[1] // 4
    for j, p in enumerate((own, p1, p2, p3)):
        at = pl.ds(pl.multiple_of((sc[2] ^ j) * w, w), w)
        for c in range(3):
            qkv_out[c, :, at] = f(p[:, c * w : (c + 1) * w])
        out_out[:, at] = f(p[:, 3 * w :])


def after(x, *deps):
    return lax.optimization_barrier((x, *deps))[0]


def local(
    tokens,
    cotangent,
    route,
    lengths,
    clip_tau,
    attn_norm_gain,
    attn_norm_bias,
    qkv_weight,
    qv_bias,
    out_weight,
    out_bias,
    mlp_norm_gain,
    mlp_norm_bias,
    up_weight,
    up_bias,
    down_weight,
    down_bias,
):
    n_dp = lax.axis_size("dp")
    n_bits = n_dp.bit_length() - 1
    rs_bits = [b for b in range(n_bits) if b not in AG_BITS]
    masks = [1 << AG_BITS[0], 1 << AG_BITS[1], (1 << AG_BITS[0]) | (1 << AG_BITS[1])]
    me = lax.axis_index("dp")
    core = lax.axis_index("tensor")
    rows, width = tokens.shape
    group = 2 * rows
    cols = qkv_weight.shape[2]
    hidden = up_weight.shape[1]
    q_cols = cols // 4
    q_hidden = hidden // 4
    quarter = ((me >> AG_BITS[0]) & 1) + 2 * ((me >> AG_BITS[1]) & 1)
    sc = jnp.concatenate([jnp.stack([core, me, quarter, core]).astype(I32), lengths[0]])

    def swap(x):
        return lax.ppermute(x, "tensor", [(0, 1), (1, 0)])

    def hop(x, mask):
        return lax.ppermute(x, "dp", [(i, i ^ mask) for i in range(n_dp)])

    def exchange(x):
        return lax.all_to_all(x, "dp", split_axis=0, concat_axis=0, tiled=True)

    def share(own):
        got = [hop(own[:rows], m) for m in masks]
        return got + [swap(g) for g in got]

    w_qkv = jnp.transpose(qkv_weight, (1, 0, 2))
    vecs = jnp.concatenate(
        [attn_norm_gain, attn_norm_bias, out_bias, mlp_norm_gain, mlp_norm_bias, down_bias, up_bias]
    ).astype(F32).reshape(-1, width)

    msg, pick = kernel_call(
        functools.partial(route_kernel, n_dp),
        [((rows, 2 * width + PAD), BF16), ((rows, rows), BF16)],
        [route.reshape(1, rows), lengths, tokens, cotangent],
        hbm={0: whole((1, rows)), 1: whole(lengths.shape), 2: whole(tokens.shape), 3: whole(tokens.shape)},
        flops=4 * rows * rows * width,
    )
    got = after(exchange(msg), vecs, sc)
    other = swap(got)
    x, normed, qkv, lse, tops, part = kernel_call(
        attn_kernel,
        [
            ((group, width), BF16),
            ((group, width), BF16),
            ((group, 3 * cols), BF16),
            ((group, PAD), F32),
            ((cols // HD, PAD), F32),
            ((group, width), BF16),
        ],
        [sc, got, other, vecs, w_qkv, qv_bias, out_weight],
        smem=(0,),
        hbm={4: (w_qkv.shape, by_row(3)), 5: whole(qv_bias.shape), 6: whole(out_weight.shape)},
        flops=2 * group * width * 4 * cols * 3,
        scratch=[pltpu.VMEM((group, cols), BF16)],
        limit=20,
    )
    middle, mid, cot, msg_mlp = kernel_call(
        middle_kernel,
        [((group, width), F32), ((group, width), BF16), ((group, width), BF16), ((rows, 2 * width), BF16)],
        [x, part, swap(part), vecs, got, other],
        flops=1 << 28,
    )
    m1, m2 = (hop(msg_mlp, m) for m in masks[:2])
    gmid_part, mlp_mine, mlp_other, up_sums = kernel_call(
        mlp_kernel,
        [((group, width), BF16), ((rows, width), F32), ((rows, width), BF16), ((1, hidden), F32)],
        [mid, cot, vecs, up_weight, down_weight],
        hbm={3: (up_weight.shape, tiles(hidden // TILE, 1)), 4: (down_weight.shape, tiles(hidden // TILE, 0))},
        flops=2 * group * width * hidden * 4,
        scratch=[pltpu.VMEM((group, width), F32), pltpu.VMEM((group, width), F32)],
        limit=24,
    )
    gmid_part, m1, m2 = lax.optimization_barrier((gmid_part, m1, m2))
    m3 = hop(m2, masks[0])
    o1, o2 = swap(m1), swap(m2)
    gmid_recv = swap(gmid_part)
    gmid, gattn, mid_sums, msg_attn = kernel_call(
        gmid_kernel,
        [((rows, width), F32), ((group, width), BF16), ((8, width), F32), ((rows, 2 * width), BF16)],
        [gmid_part, gmid_recv, middle, cot, normed, vecs],
        flops=1 << 28,
    )
    gn_mine, gn_other, qkv_sums = kernel_call(
        attn_grad_kernel,
        [((rows, width), F32), ((rows, width), BF16), ((3, cols), F32)],
        [sc, gattn, out_weight, qkv, lse, w_qkv],
        smem=(0,),
        hbm={2: whole(out_weight.shape), 5: (w_qkv.shape, by_row(3))},
        flops=2 * group * width * 4 * cols * 3,
        scratch=[pltpu.VMEM((group, 3 * cols), BF16)],
        limit=20,
    )
    gn_other, m3, o1, o2 = lax.optimization_barrier((gn_other, m3, o1, o2))
    gn_recv = swap(gn_other)
    msg_attn = after(msg_attn, gn_other)
    a1, a2 = (hop(msg_attn, m) for m in masks[:2])
    mlp_shared = [m1, m2, m3, o1, o2, swap(m3)]
    back, norm_sums = kernel_call(
        last_kernel,
        [((rows, 2 * width), BF16), ((2, width), F32)],
        [gn_mine, gn_recv, x, gmid, middle, mlp_mine, swap(mlp_other), vecs, got],
        flops=1 << 28,
    )

    n_vec = 6 * width
    sums = jnp.concatenate(
        [
            norm_sums.reshape(-1),
            mid_sums[:4].reshape(-1),
            qkv_sums[0],
            qkv_sums[2],
            up_sums.reshape(-1),
        ]
    )
    n_sum = sums.size
    msg = jnp.concatenate([sums, jnp.pad(tops[:, 0], (0, PAD - tops.shape[0]))]).reshape(-1, PAD)
    is_top = iota(msg.shape, 0) == n_sum // PAD

    def combine(msg, *came):
        return functools.reduce(lambda a, b: jnp.where(is_top, jnp.maximum(a, b), a + b), (msg, *came))

    near = [1 << b for b in rs_bits[:2]]
    came = [hop(msg, m) for m in near + [near[0] | near[1]]]
    later = [b for b in range(n_bits) if b not in rs_bits[:2]]
    restored = exchange(back)

    block = width // n_dp
    first = rs_bits[0]
    def step(i, recv, keep):
        n, w = keep.shape
        left = [b for b in range(n_bits) if b not in rs_bits[:i]]
        run = run_lengths(left, block)[rs_bits[i]]
        return kernel_call(
            functools.partial(step_kernel, rs_bits[i], run),
            [((n // 2, w), BF16), ((n // 2, w), F32)],
            [sc, keep, recv],
            smem=(0,),
            flops=1 << 26,
            scratch=[pltpu.VMEM((n, w), F32)],
        )

    half = ((width // 2, q_hidden), BF16), ((width // 2, q_hidden), F32)
    send_down, keep_down, send_up, keep_up = kernel_call(
        functools.partial(mlp_weights_kernel, n_bits, first),
        [half[0], half[1], half[0], half[1]],
        [sc, after(mid, norm_sums), cot] + mlp_shared + [vecs, up_weight, down_weight],
        smem=(0,),
        hbm={
            **gathered([(1, 0), (2, 1)], [3, 6, 4, 7, 5, 8], rows),
            10: ((width, q_hidden), columns(q_hidden, 1)),
            11: ((q_hidden, width), columns(q_hidden, 0)),
        },
        limit=28,
        flops=2 * 4 * group * width * q_hidden * 4,
        scratch=[
            pltpu.VMEM((4 * group, width), BF16),
            pltpu.VMEM((4 * group, width), BF16),
            pltpu.VMEM((width, q_hidden), F32),
        ],
    )
    send_down, send_up, a1, a2, restored, *came = lax.optimization_barrier(
        (send_down, send_up, a1, a2, restored, *came)
    )
    msg = combine(msg, *came)
    a3 = hop(a1, masks[1])
    b1, b2 = swap(a1), swap(a2)
    recv_down = hop(send_down, 1 << first)

    def attn_scratch(n):
        return [
            pltpu.VMEM((n * group, width), BF16),
            pltpu.VMEM((n * group, width), BF16),
            pltpu.VMEM((n * group, q_cols), BF16),
            pltpu.VMEM((n * group, 3 * q_cols), BF16),
        ]

    def quarter_weights(i):
        return {
            i: ((2, q_cols), columns(q_cols, 1)),
            i + 1: ((3, width, q_cols), columns(q_cols, 1)),
            i + 2: ((q_cols, width), columns(q_cols, 0)),
        }

    (part_attn,) = kernel_call(
        functools.partial(attn_first_kernel, n_dp, [0] + masks[:2]),
        [((width, 4 * q_cols), F32)],
        [sc, got, normed, gattn, a1, a2, b1, b2, qv_bias, w_qkv, out_weight],
        smem=(0,),
        hbm={**gathered([(2, 1), (3, 0)], [4, 6, 5, 7], rows), **quarter_weights(8)},
        limit=24,
        loose=(6, 7),
        flops=2 * 3 * group * width * q_cols * 12,
        scratch=attn_scratch(3),
    )
    a3, recv_down, part_attn = lax.optimization_barrier((a3, recv_down, part_attn))

    def hand_out(*pairs):
        n, w = pairs[0][0].shape
        w *= len(pairs)
        pieces = kernel_call(
            functools.partial(pieces_kernel, len(pairs)),
            [((block, w), F32)] + [((block, w), BF16)] * 3,
            [sc] + [a for pair in pairs for a in pair],
            smem=(0,),
            flops=1 << 26,
            scratch=[pltpu.VMEM((n, w), F32)],
        )
        return [pieces[0]] + [hop(p, m) for p, m in zip(pieces[1:], masks)]

    def clip(msg):
        threshold = clip_tau[0].astype(F32)
        head_factor = jnp.sqrt(threshold / jnp.maximum(msg[-1, : tops.shape[0]], threshold))
        column_factor = jnp.repeat(head_factor, HD)
        clipped_qk = pl.pallas_call(
            clip_kernel,
            grid=(4,),
            out_shape=jax.ShapeDtypeStruct((width, 2, cols), BF16),
            in_specs=[
                pl.BlockSpec((2, width // 4, cols), lambda i: (0, i, 0)),
                pl.BlockSpec((1, cols), lambda i: (0, 0)),
            ],
            out_specs=pl.BlockSpec((width // 4, 2, cols), lambda i: (i, 0, 0)),
            name="clip_kernel",
        )(w_qkv, column_factor.reshape(1, cols))
        return clipped_qk, head_factor, column_factor

    n_steps = len(rs_bits)
    recvs = {0: recv_down}
    sends = {1: send_up}
    keeps = {0: keep_down, 1: keep_up}
    for t in range(1, n_steps + 2):
        active = [i for i in range(3) if 0 <= t - i < n_steps]
        gate = ()
        for i in active:
            if t > i:
                sends[i], keeps[i] = step(t - i, recvs[i], keeps[i])
                gate = (sends[i],)
        for i in active:
            recvs[i] = hop(after(sends[i], *gate), 1 << rs_bits[t - i])
        extra = []
        if t <= n_steps:
            msg = after(msg, *gate)
            came = hop(msg, 1 << later[t - 1])
        if t == 1:
            send_attn, keep_attn = kernel_call(
                functools.partial(attn_weights_kernel, n_bits, first, n_dp, masks[2:]),
                [((width // 2, 4 * q_cols), BF16), ((width // 2, 4 * q_cols), F32)],
                [sc, got, part_attn, a3, swap(a3), qv_bias, w_qkv, out_weight],
                smem=(0,),
                hbm={**gathered([], [3, 4], rows, 0), **quarter_weights(5)},
                limit=20,
                loose=(4,),
                flops=2 * group * width * q_cols * 12,
                scratch=attn_scratch(1) + [pltpu.VMEM((width, 4 * q_cols), F32)],
            )
            sends[2], keeps[2] = send_attn, keep_attn
            out_tokens, grad_tokens = kernel_call(
                restore_kernel,
                [((rows, width), BF16)] * 2,
                [pick, after(restored, *gate)],
                flops=1 << 27,
            )
            extra = [out_tokens, grad_tokens, sends[2]]
        if t == n_steps + 1:
            mlp_pieces = hand_out((after(keeps[0], *gate), recvs[0]), (keeps[1], recvs[1]))
            clipped_qk, head_factor, column_factor = clip(msg)
            extra = mlp_pieces[1:] + [clipped_qk]
        done = lax.optimization_barrier([recvs[i] for i in active] + [came] + extra)
        recvs.update(zip(active, done))
        if t <= n_steps:
            msg = combine(msg, done[len(active)])
        if t == 1:
            out_tokens, grad_tokens, sends[2] = done[-3:]
        if t == n_steps + 1:
            mlp_pieces[1:], clipped_qk = done[-4:-1], done[-1]
    attn_pieces = hand_out((keeps[2], recvs[2]))
    grad_down, grad_up = kernel_call(
        join_mlp_kernel, [((block, hidden), F32), ((block, hidden), F32)], [sc] + mlp_pieces, smem=(0,)
    )
    grad_down, grad_up, *attn_pieces[1:] = lax.optimization_barrier((grad_down, grad_up, *attn_pieces[1:]))
    grad_down = grad_down.T
    grad_qkv, grad_out = kernel_call(
        join_attn_kernel, [((3, block, cols), F32), ((block, cols), F32)], [sc] + attn_pieces, smem=(0,)
    )
    grad_qkv = jnp.transpose(grad_qkv, (1, 0, 2))
    grad_out = grad_out.T

    theirs = swap(msg).reshape(-1)
    msg = msg.reshape(-1)
    vector_sum = (msg[:n_vec] + theirs[:n_vec]).reshape(6, width)
    own, oth = msg[n_vec:n_sum], theirs[n_vec:n_sum]
    one = jnp.where(core == 0, own, oth)
    two = jnp.where(core == 0, oth, own)
    qv_sum = jnp.stack(
        [
            jnp.concatenate([one[:cols], two[:cols]]),
            jnp.concatenate([one[cols : 2 * cols], two[cols : 2 * cols]]),
        ]
    )
    up_sum = jnp.concatenate([one[2 * cols :], two[2 * cols :]])

    clipped_q_bias = (f(qv_bias[0]) * column_factor).astype(BF16)
    return (
        out_tokens,
        grad_tokens,
        grad_qkv,
        grad_out,
        grad_up,
        grad_down,
        qv_sum,
        up_sum,
        vector_sum,
        head_factor,
        clipped_qk,
        clipped_q_bias,
    )

def solution(mesh):
    placed = (
        P(("dp", "tensor"), None),
        P(("dp", "tensor"), None),
        P(("dp", "tensor")),
        P("dp", None),
        P(),
        P(),
        P(),
        P(None, None, "tensor"),
        P(None, "tensor"),
        P("tensor", None),
        P(),
        P(),
        P(),
        P(None, "tensor"),
        P("tensor"),
        P("tensor", None),
        P(),
    )
    return jax.shard_map(
        local,
        mesh=mesh,
        in_specs=placed,
        out_specs=(
            P(("dp", "tensor"), None),
            P(("dp", "tensor"), None),
            P("dp", None, "tensor"),
            P("tensor", "dp"),
            P("dp", "tensor"),
            P("tensor", "dp"),
            P(),
            P(),
            P(),
            P("tensor"),
            P(None, None, "tensor"),
            P("tensor"),
        ),
        check_vma=False,
    )
```

```python
import functools
import jax
import jax.numpy as jnp
from jax import lax
from jax.experimental import pallas as pl
from jax.experimental.pallas import tpu as pltpu
from jax.sharding import PartitionSpec as P

HD = 64
AG_BITS = (0, 2)
PAD = 128
COST = 1

epsilon = 1e-05
masked_value = -1e30
gelu_coef = 0.7978845608028654
F32 = jnp.float32
BF16 = jnp.bfloat16
I32 = jnp.int32


def f(x):
    return x.astype(F32)


def dot(a, b, ca, cb):
    return lax.dot_general(a, b, (((ca,), (cb,)), ((), ())), preferred_element_type=F32)


def nn(a, b):
    return dot(a, b, 1, 0)


def nt(a, b):
    return dot(a, b, 1, 1)


def tn(a, b):
    return dot(a, b, 0, 0)


def norm_stats(values):
    row_mean = jnp.mean(values, axis=-1, keepdims=True)
    centered = values - row_mean
    variance = jnp.mean(centered * centered, axis=-1, keepdims=True)
    inv = lax.rsqrt(variance + epsilon)
    return centered * inv, inv


def norm_grad(xhat, inv, gain, grad):
    scaled = grad * gain
    a = jnp.mean(scaled, axis=-1, keepdims=True)
    b = jnp.mean(scaled * xhat, axis=-1, keepdims=True)
    return inv * (scaled - a - xhat * b)


def gelu_parts(p):
    p2 = p * p
    th = jnp.tanh(gelu_coef * (p + 0.044715 * p2 * p))
    half = 0.5 * (1.0 + th)
    slope = half + 0.5 * p * (1.0 - th * th) * (gelu_coef * (1.0 + 3.0 * 0.044715 * p2))
    return p * half, slope


def iota(shape, axis):
    return lax.broadcasted_iota(I32, shape, axis)


def place_matrix(ids):
    rows = ids.shape[0]
    return (ids == f(iota((rows, rows), 1))).astype(BF16)


def pair_mask(ends, core, rows):
    group = 2 * rows
    pos_r = (iota((group, 1), 0) + core * rows) & (group - 1)
    pos_c = (iota((1, group), 1) + core * rows) & (group - 1)
    sid_r = sum((pos_r >= e).astype(I32) for e in ends)
    sid_c = sum((pos_c >= e).astype(I32) for e in ends)
    sid_r = jnp.where(pos_r < ends[-1], sid_r, -1)
    same = (sid_r == sid_c).astype(I32) * (pos_c <= pos_r).astype(I32)
    diagonal = (pos_r == pos_c).astype(I32)
    return (same + diagonal) > 0, sid_r >= 0


def half_lanes():
    lane = iota((1, PAD), 1)
    low = (lane < HD).astype(F32)
    return (low.astype(BF16), (1.0 - low).astype(BF16)), (low, 1.0 - low)


def head_probs(q2, k2, lanes, mask):
    s = jnp.where(mask, nt(q2 * lanes, k2) * 0.125, masked_value)
    top = jnp.max(s, axis=-1, keepdims=True)
    e = jnp.exp(s - top)
    total = jnp.sum(e, axis=-1, keepdims=True)
    return e, top, total


def head_grad(q2, k2, v2, gc2, lanes, p):
    gp = nt(gc2 * lanes, v2)
    row_dot = jnp.sum(p * gp, axis=-1, keepdims=True)
    ds = (p * (gp - row_dot)).astype(BF16)
    return nn(ds, k2) * 0.125, tn(ds, q2) * 0.125, tn(p.astype(BF16), gc2)


class Fetched:
    def __init__(self, ref, copies):
        self.ref, self.copies, self.shape = ref, copies, getattr(ref, "shape", None)

    def wait(self, k=None):
        for c in self.copies if k is None else [self.copies[k]]:
            c.wait()
        return self.ref


def whole(shape):
    return shape, lambda src, dst, sc: [(src, dst)]


def kernel_call(body, outs, args, smem=(), hbm=None, flops=0, scratch=(), limit=12, loose=()):
    hbm = hbm or {}
    specs = []
    n_bytes = 0
    for i, a in enumerate(args):
        n_bytes += a.size * a.dtype.itemsize
        space = pl.ANY if i in loose else pltpu.HBM if i in hbm else pltpu.SMEM if i in smem else pltpu.VMEM
        specs.append(pl.BlockSpec(memory_space=space))
    shapes = [jax.ShapeDtypeStruct(s, d) for s, d in outs]
    out_specs = [pl.BlockSpec(memory_space=pltpu.VMEM) for _ in outs]
    args = [pltpu.with_memory_space_constraint(a, pltpu.HBM) if i in hbm and i not in loose else a for i, a in enumerate(args)]
    n_in, n_out, n_scratch = len(args), len(outs), len(scratch)
    extra = []
    own = [i for i, (shape, _) in hbm.items() if shape is not None]
    for i in own:
        extra.append(pltpu.VMEM(hbm[i][0], args[i].dtype))
    n_chunks = {}
    for i, (shape, chunks) in hbm.items():
        n_chunks[i] = getattr(chunks, "count", 1)
        extra.append(pltpu.SemaphoreType.DMA((n_chunks[i],)))

    def run(*refs):
        ins = list(refs[:n_in])
        rest = refs[n_in + n_out + n_scratch :]
        sc = ins[0]
        for j, (i, (_, chunks)) in enumerate(hbm.items()):
            dst = rest[own.index(i)] if i in own else refs[n_in + n_out :]
            sem = rest[len(own) + j]
            copies = [
                pltpu.make_async_copy(a, b, sem.at[k]) for k, (a, b) in enumerate(chunks(ins[i], dst, sc))
            ]
            for c in copies:
                c.start()
            ins[i] = Fetched(dst, copies)
        body(*ins, *refs[n_in : n_in + n_out + n_scratch])

    return pl.pallas_call(
        run,
        out_shape=shapes,
        in_specs=specs,
        out_specs=out_specs,
        scratch_shapes=list(scratch) + extra,
        compiler_params=pltpu.CompilerParams(vmem_limit_bytes=limit << 20),
        cost_estimate=pl.CostEstimate(
            flops=int(flops * COST), transcendentals=0, bytes_accessed=int(n_bytes * COST)
        ),
        name=body.func.__name__ if hasattr(body, "func") else body.__name__,
    )(*args)


def chunked(count, make):
    def chunks(src, dst, sc):
        return [make(src, dst, sc, k) for k in range(count)]

    chunks.count = count
    return chunks


def gathered(own_args, shared_args, rows, start=2):
    spec = {}
    for i, at in own_args:
        spec[i] = (None, chunked(1, lambda src, dst, sc, k, at=at: (src, dst[at].at[pl.ds(0, 2 * rows), :])))
    for j, i in enumerate(shared_args):

        def make(src, dst, sc, k, j=j):
            width = dst[0].shape[1]
            return src.at[:, pl.ds(k * width, width)], dst[k].at[pl.ds((start + j) * rows, rows), :]

        spec[i] = (None, chunked(2, make))
    return spec


def by_row(count):
    return chunked(count, lambda src, dst, sc, k: (src.at[k], dst.at[k]))


def tiles(count, axis):
    def make(src, dst, sc, k):
        at = pl.ds(k * TILE, TILE)
        return (src.at[at, :], dst.at[at, :]) if axis == 0 else (src.at[:, at], dst.at[:, at])

    return chunked(count, make)


def columns(n, axis):
    def chunks(src, dst, sc):
        at = pl.ds(pl.multiple_of(sc[2] * n, n), n)
        if axis == 0:
            return [(src.at[at, :], dst)]
        return [(src.at[(slice(None),) * (len(src.shape) - 1) + (at,)], dst)]

    return chunks


def route_kernel(n_dp, route, lens, tokens, cotangent, msg, pick_out):
    rows, width = tokens.shape
    row = jnp.broadcast_to(f(route.wait()[...]), (rows, rows))
    col = row.T
    group = float(2 * rows)
    dest_r = jnp.floor(row / group)
    dest_c = jnp.floor(col / group)
    before = iota((rows, rows), 0) < iota((rows, rows), 1)
    same = jnp.where(before, (dest_r == dest_c).astype(F32), 0.0)
    rank = dest_r[0:1] * (rows // n_dp) + jnp.sum(same, axis=0, keepdims=True)
    pick = (jnp.broadcast_to(rank, (rows, rows)) == f(iota((rows, rows), 0))).astype(F32)
    place = row - jnp.floor(row / float(rows)) * float(rows)
    ids = jnp.sum(pick * place, axis=1, keepdims=True)
    lane = iota((rows, PAD), 1)
    extra = jnp.where(lane == 0, ids, 0.0)
    lens = f(lens.wait()[...])
    for i in range(4):
        extra = jnp.where(lane == i + 1, lens[:, i : i + 1], extra)
    pick_b = pick.astype(BF16)
    pick_out[...] = pick_b
    msg[:, :width] = nn(pick_b, tokens.wait()[...]).astype(BF16)
    msg[:, 2 * width :] = extra.astype(BF16)
    msg[:, width : 2 * width] = nn(pick_b, cotangent.wait()[...]).astype(BF16)


def ends_of(sc):
    e = [sc[4]]
    for i in range(1, 4):
        e.append(e[-1] + sc[4 + i])
    return e


def attn_kernel(
    sc, mine, other, vecs, w_qkv, qv_bias, w_out, x_out, normed_out, qkv_out, lse_out, top_out, part_out, ctx_out
):
    rows = mine.shape[0]
    width = w_out.shape[1]
    cols = w_out.shape[0]
    for i, half in enumerate((mine, other)):
        put = place_matrix(f(half[:, 2 * width : 2 * width + 1]))
        x = tn(put, half[:, :width])
        s = slice(i * rows, (i + 1) * rows)
        x_out[s, :] = x.astype(BF16)
        xhat, _ = norm_stats(x)
        normed_out[s, :] = (xhat * vecs[0:1, :] + vecs[1:2, :]).astype(BF16)
    normed = normed_out[...]
    qv_bias = qv_bias.wait()
    for c in range(3):
        y = nn(normed, w_qkv.wait(c)[c])
        if c == 0:
            y = y + f(qv_bias[0:1, :])
        if c == 2:
            y = y + f(qv_bias[1:2, :])
        qkv_out[:, c * cols : (c + 1) * cols] = y.astype(BF16)
    mask, live = pair_mask(ends_of(sc), sc[0], rows)
    lanes_b, lanes_f = half_lanes()
    lane = iota((1, PAD), 1)
    lse = jnp.zeros((2 * rows, PAD), F32)
    for pair in range(cols // PAD):
        s = slice(pair * PAD, (pair + 1) * PAD)
        q2 = qkv_out[:, s]
        k2 = qkv_out[:, slice(cols + pair * PAD, cols + (pair + 1) * PAD)]
        v2 = qkv_out[:, slice(2 * cols + pair * PAD, 2 * cols + (pair + 1) * PAD)]
        out = jnp.zeros((2 * rows, PAD), F32)
        for i in range(2):
            e, top, total = head_probs(q2, k2, lanes_b[i], mask)
            probs = (e * (1.0 / total)).astype(BF16)
            out = out + nn(probs, v2) * lanes_f[i]
            h = 2 * pair + i
            lse = jnp.where(lane == h, top + jnp.log(total), lse)
            best = jnp.max(jnp.where(live, top, masked_value), axis=0, keepdims=True)
            top_out[h : h + 1, :] = jnp.broadcast_to(best, (1, PAD))
        ctx_out[:, s] = out.astype(BF16)
    lse_out[...] = lse
    part_out[...] = nn(ctx_out[...], w_out.wait()[...]).astype(BF16)


def middle_kernel(x, part, recv, vecs, mine, other, middle_out, mid_out, cot_out, msg_out):
    rows, width = msg_out.shape[0], x.shape[1]
    for i, half in enumerate((mine, other)):
        s = slice(i * rows, (i + 1) * rows)
        o = slice((1 - i) * rows, (2 - i) * rows)
        put = place_matrix(f(half[:, 2 * width : 2 * width + 1]))
        cot = tn(put, half[:, width : 2 * width]).astype(BF16)
        cot_out[s, :] = cot
        middle = f(x[s, :]) + (f(part[s, :]) + f(recv[o, :])) + vecs[2:3, :]
        middle_out[s, :] = middle
        mhat, _ = norm_stats(middle)
        mid = (mhat * vecs[3:4, :] + vecs[4:5, :]).astype(BF16)
        mid_out[s, :] = mid
        if i == 0:
            msg_out[:, :width] = mid
            msg_out[:, width:] = cot


TILE = 1024


def mlp_kernel(mid, cot, vecs, up, down, gmid_out, mine_out, other_out, sums_out, acc, acc_y):
    width, hidden = up.shape
    rows = mine_out.shape[0]
    per_row = width // TILE
    for t in range(hidden // TILE):
        s = slice(t * TILE, (t + 1) * TILE)
        bias = vecs[6 + t // per_row : 7 + t // per_row, (t % per_row) * TILE : (t % per_row + 1) * TILE]
        act, slope = gelu_parts(nn(mid[...], up.wait(t)[:, s]) + bias)
        gpre = (nt(cot[...], down.wait(t)[s, :]) * slope).astype(BF16)
        sums_out[:, s] = jnp.sum(f(gpre), axis=0, keepdims=True)
        g = nt(gpre, up.ref[:, s])
        y = nn(act.astype(BF16), down.ref[s, :])
        if t == 0:
            acc[...] = g
            acc_y[...] = y
        else:
            acc[...] += g
            acc_y[...] += y
    gmid_out[...] = acc[...].astype(BF16)
    mine_out[...] = acc_y[:rows, :]
    other_out[...] = acc_y[rows:, :].astype(BF16)


def gmid_kernel(part, recv, middle, cot, normed, vecs, gmid_out, gattn_out, sums_out, msg_out):
    rows, width = gmid_out.shape
    msg_out[:, width:] = normed[:rows, :]
    for i in range(2):
        s = slice(i * rows, (i + 1) * rows)
        o = slice((1 - i) * rows, (2 - i) * rows)
        g = f(part[s, :]) + f(recv[o, :])
        mhat, inv = norm_stats(middle[s, :])
        c = f(cot[s, :])
        gm = c + norm_grad(mhat, inv, vecs[3:4, :], g)
        gattn = gm.astype(BF16)
        gattn_out[s, :] = gattn
        if i == 0:
            gmid_out[...] = gm
            msg_out[:, :width] = gattn
            sums_out[0:1, :] = jnp.sum(gm, axis=0, keepdims=True)
            sums_out[1:2, :] = jnp.sum(g * mhat, axis=0, keepdims=True)
            sums_out[2:3, :] = jnp.sum(g, axis=0, keepdims=True)
            sums_out[3:4, :] = jnp.sum(c, axis=0, keepdims=True)
            sums_out[4:8, :] = jnp.zeros((4, sums_out.shape[1]), F32)


def attn_grad_kernel(sc, gattn, w_out, qkv, lse, w_qkv, mine_out, other_out, sums_out, gqkv):
    rows = gattn.shape[0] // 2
    cols = w_out.shape[0]
    mask, _ = pair_mask(ends_of(sc), sc[0], rows)
    gctx = nt(gattn[...], w_out.wait()[...]).astype(BF16)
    lanes_b, lanes_f = half_lanes()
    for pair in range(cols // PAD):
        cut = [slice(c * cols + pair * PAD, c * cols + (pair + 1) * PAD) for c in range(3)]
        q2, k2, v2 = (qkv[:, c] for c in cut)
        gc2 = gctx[:, pair * PAD : (pair + 1) * PAD]
        total = None
        for i in range(2):
            h = 2 * pair + i
            s = jnp.where(mask, nt(q2 * lanes_b[i], k2) * 0.125, masked_value)
            p = jnp.exp(s - lse[:, h : h + 1])
            g3 = [g * lanes_f[i] for g in head_grad(q2, k2, v2, gc2, lanes_b[i], p)]
            total = g3 if total is None else [a + b for a, b in zip(total, g3)]
        for c in range(3):
            g = total[c].astype(BF16)
            gqkv[:, cut[c]] = g
            sums_out[c : c + 1, pair * PAD : (pair + 1) * PAD] = jnp.sum(f(g), axis=0, keepdims=True)
    y = sum(nt(gqkv[:, c * cols : (c + 1) * cols], w_qkv.wait(c)[c]) for c in range(3))
    mine_out[...] = y[:rows]
    other_out[...] = y[rows:].astype(BF16)


def last_kernel(part, recv, x, gmid, middle, y_mine, y_other, vecs, ids, msg_out, sums_out):
    rows, width = part.shape
    put = place_matrix(f(ids[:, 2 * width : 2 * width + 1]))
    res = middle[:rows, :] + (y_mine[...] + f(y_other[...])) + vecs[5:6, :]
    msg_out[:, :width] = nn(put, res.astype(BF16)).astype(BF16)
    g = part[...] + f(recv[...])
    xhat, inv = norm_stats(f(x[:rows, :]))
    grad = (gmid[...] + norm_grad(xhat, inv, vecs[0:1, :], g)).astype(BF16)
    sums_out[0:1, :] = jnp.sum(g * xhat, axis=0, keepdims=True)
    sums_out[1:2, :] = jnp.sum(g, axis=0, keepdims=True)
    msg_out[:, width:] = nn(put, grad).astype(BF16)


def restore_kernel(pick, msg, out, grad):
    width = out.shape[1]
    y = tn(pick[...], msg[...]).astype(BF16)
    out[...] = y[:, :width]
    grad[...] = y[:, width:]


def clip_kernel(w, factor, out):
    for c in range(2):
        out[:, c, :] = (f(w[c]) * factor[...]).astype(BF16)


def run_lengths(bits, block):
    return {b: block << i for i, b in enumerate(sorted(bits))}


def split_rows(src, run, mine, send_out, keep_out, at):
    n = src.shape[0]
    for j in range(n // (2 * run)):
        k = pl.multiple_of(2 * run * j + mine * run, run)
        s = pl.multiple_of(2 * run * j + (1 - mine) * run, run)
        dst = slice(j * run, (j + 1) * run)
        keep_out[dst, at] = src[pl.ds(k, run), :]
        send_out[dst, at] = src[pl.ds(s, run), :].astype(BF16)


def mlp_weights_kernel(
    n_bits, bit, sc, mid, cot, m1, m2, m3, o1, o2, o3, vecs, up, down,
    send_down, keep_down, send_up, keep_up, mids, cots, grad,
):
    for x in (mid, cot, m1, m2, m3, o1, o2, o3):
        x.wait()
    q_hidden = down.shape[0]
    per_row = mids.shape[1] // q_hidden
    bias = jnp.zeros((1, q_hidden), F32)
    for k in range(4):
        part = vecs[6 + k // per_row : 7 + k // per_row, (k % per_row) * q_hidden : (k % per_row + 1) * q_hidden]
        bias = jnp.where(sc[2] == k, part, bias)
    mine = (sc[1] >> bit) & 1
    run = (mids.shape[1] >> n_bits) << bit
    act, slope = gelu_parts(nn(mids[...], up.wait()[...]) + bias)
    every = slice(None)
    grad[...] = tn(cots[...], act.astype(BF16))
    split_rows(grad, run, mine, send_down, keep_down, every)
    gpre = (nt(cots[...], down.wait()[...]) * slope).astype(BF16)
    grad[...] = tn(mids[...], gpre)
    split_rows(grad, run, mine, send_up, keep_up, every)


def attn_quarter(n_dp, masks, sc, ids, qv_bias, w_qkv, w_out, gattns, norms, ctx, gqkv):
    group = norms.shape[0] // len(masks)
    rows = group // 2
    me = sc[1]
    norm4 = norms[...]
    w_qkv, qv_bias = w_qkv.wait(), qv_bias.wait()
    q4 = (nn(norm4, w_qkv[0]) + f(qv_bias[0:1, :])).astype(BF16)
    k4 = nn(norm4, w_qkv[1]).astype(BF16)
    v4 = (nn(norm4, w_qkv[2]) + f(qv_bias[1:2, :])).astype(BF16)
    gc4 = nt(gattns[...], w_out.wait()[...]).astype(BF16)
    lanes_b, lanes_f = half_lanes()
    table = f(ids[:, 2 * norms.shape[1] :])
    from_dp = iota((rows, 1), 0) // (rows // n_dp)
    first = iota((rows, 1), 0) == from_dp * (rows // n_dp)
    for g, bits in enumerate(masks):
        chosen = jnp.where((from_dp == (me ^ bits)) & first, table, 0.0)
        lens = jnp.sum(chosen, axis=0, keepdims=True)
        ends = [lens[:, 1:2]]
        for i in range(2, 5):
            ends.append(ends[-1] + lens[:, i : i + 1])
        mask, _ = pair_mask([e.astype(I32) for e in ends], sc[0], rows)
        s = slice(g * group, (g + 1) * group)
        q2, k2, v2, gc2 = q4[s], k4[s], v4[s], gc4[s]
        out = jnp.zeros((group, PAD), F32)
        total = None
        for i in range(2):
            e, _, denom = head_probs(q2, k2, lanes_b[i], mask)
            p = e * (1.0 / denom)
            out = out + nn(p.astype(BF16), v2) * lanes_f[i]
            g3 = [x * lanes_f[i] for x in head_grad(q2, k2, v2, gc2, lanes_b[i], p)]
            total = g3 if total is None else [a + b for a, b in zip(total, g3)]
        ctx[s, :] = out.astype(BF16)
        for c in range(3):
            gqkv[s, c * PAD : (c + 1) * PAD] = total[c].astype(BF16)


def attn_first_kernel(
    n_dp, masks, sc, ids, nrm, ga, m1, m2, o1, o2, qv_bias, w_qkv, w_out, grad, gattns, norms, ctx, gqkv
):
    for x in (ga, nrm, m1, m2, o1, o2):
        x.wait()
    attn_quarter(n_dp, masks, sc, ids, qv_bias, w_qkv, w_out, gattns, norms, ctx, gqkv)
    grad[:, : 3 * PAD] = tn(norms[...], gqkv[...])
    grad[:, 3 * PAD :] = tn(gattns[...], ctx[...])


def attn_weights_kernel(
    n_bits, bit, n_dp, masks, sc, ids, base, m3, o3, qv_bias, w_qkv, w_out,
    send_out, keep_out, gattns, norms, ctx, gqkv, grad,
):
    m3.wait()
    o3.wait()
    run = (norms.shape[1] >> n_bits) << bit
    attn_quarter(n_dp, masks, sc, ids, qv_bias, w_qkv, w_out, gattns, norms, ctx, gqkv)
    grad[:, : 3 * PAD] = base[:, : 3 * PAD] + tn(norms[...], gqkv[...])
    grad[:, 3 * PAD :] = base[:, 3 * PAD :] + tn(gattns[...], ctx[...])
    split_rows(grad, run, (sc[1] >> bit) & 1, send_out, keep_out, slice(None))


def step_kernel(bit, run, sc, keep, recv, send_out, keep_out, cur):
    cur[...] = keep[...] + f(recv[...])
    split_rows(cur, run, (sc[1] >> bit) & 1, send_out, keep_out, slice(None))


def pieces_kernel(n_pairs, sc, *refs):
    pairs, (own, p1, p2, p3), cur = refs[: 2 * n_pairs], refs[2 * n_pairs : -1], refs[-1]
    n = own.shape[0]
    w = pairs[0].shape[1]
    for i in range(n_pairs):
        cur[:, i * w : (i + 1) * w] = pairs[2 * i][...] + f(pairs[2 * i + 1][...])
    q = sc[2]
    for j, out in enumerate((own, p1, p2, p3)):
        out[...] = cur[pl.ds(pl.multiple_of((q ^ j) * n, n), n), :].astype(out.dtype)


def join_mlp_kernel(sc, own, p1, p2, p3, out):
    w = own.shape[1]
    for j, p in enumerate((own, p1, p2, p3)):
        out[:, pl.ds(pl.multiple_of((sc[2] ^ j) * w, w), w)] = f(p[...])


def join_attn_kernel(sc, own, p1, p2, p3, qkv_out, out_out):
    w = own.shape[1] // 4
    for j, p in enumerate((own, p1, p2, p3)):
        at = pl.ds(pl.multiple_of((sc[2] ^ j) * w, w), w)
        for c in range(3):
            qkv_out[c, :, at] = f(p[:, c * w : (c + 1) * w])
        out_out[:, at] = f(p[:, 3 * w :])


def after(x, *deps):
    return lax.optimization_barrier((x, *deps))[0]


def local(
    tokens,
    cotangent,
    route,
    lengths,
    clip_tau,
    attn_norm_gain,
    attn_norm_bias,
    qkv_weight,
    qv_bias,
    out_weight,
    out_bias,
    mlp_norm_gain,
    mlp_norm_bias,
    up_weight,
    up_bias,
    down_weight,
    down_bias,
):
    n_dp = lax.axis_size("dp")
    n_bits = n_dp.bit_length() - 1
    rs_bits = [b for b in range(n_bits) if b not in AG_BITS]
    masks = [1 << AG_BITS[0], 1 << AG_BITS[1], (1 << AG_BITS[0]) | (1 << AG_BITS[1])]
    me = lax.axis_index("dp")
    core = lax.axis_index("tensor")
    rows, width = tokens.shape
    group = 2 * rows
    cols = qkv_weight.shape[2]
    hidden = up_weight.shape[1]
    q_cols = cols // 4
    q_hidden = hidden // 4
    quarter = ((me >> AG_BITS[0]) & 1) + 2 * ((me >> AG_BITS[1]) & 1)
    sc = jnp.concatenate([jnp.stack([core, me, quarter, core]).astype(I32), lengths[0]])

    def swap(x):
        return lax.ppermute(x, "tensor", [(0, 1), (1, 0)])

    def hop(x, mask):
        return lax.ppermute(x, "dp", [(i, i ^ mask) for i in range(n_dp)])

    def exchange(x):
        return lax.all_to_all(x, "dp", split_axis=0, concat_axis=0, tiled=True)

    def share(own):
        got = [hop(own[:rows], m) for m in masks]
        return got + [swap(g) for g in got]

    w_qkv = jnp.transpose(qkv_weight, (1, 0, 2))
    vecs = jnp.concatenate(
        [attn_norm_gain, attn_norm_bias, out_bias, mlp_norm_gain, mlp_norm_bias, down_bias, up_bias]
    ).astype(F32).reshape(-1, width)

    msg, pick = kernel_call(
        functools.partial(route_kernel, n_dp),
        [((rows, 2 * width + PAD), BF16), ((rows, rows), BF16)],
        [route.reshape(1, rows), lengths, tokens, cotangent],
        hbm={0: whole((1, rows)), 1: whole(lengths.shape), 2: whole(tokens.shape), 3: whole(tokens.shape)},
        flops=4 * rows * rows * width,
    )
    got = after(exchange(msg), vecs, sc)
    other = swap(got)
    x, normed, qkv, lse, tops, part = kernel_call(
        attn_kernel,
        [
            ((group, width), BF16),
            ((group, width), BF16),
            ((group, 3 * cols), BF16),
            ((group, PAD), F32),
            ((cols // HD, PAD), F32),
            ((group, width), BF16),
        ],
        [sc, got, other, vecs, w_qkv, qv_bias, out_weight],
        smem=(0,),
        hbm={4: (w_qkv.shape, by_row(3)), 5: whole(qv_bias.shape), 6: whole(out_weight.shape)},
        flops=2 * group * width * 4 * cols * 3,
        scratch=[pltpu.VMEM((group, cols), BF16)],
        limit=20,
    )
    middle, mid, cot, msg_mlp = kernel_call(
        middle_kernel,
        [((group, width), F32), ((group, width), BF16), ((group, width), BF16), ((rows, 2 * width), BF16)],
        [x, part, swap(part), vecs, got, other],
        flops=1 << 28,
    )
    m1, m2 = (hop(msg_mlp, m) for m in masks[:2])
    gmid_part, mlp_mine, mlp_other, up_sums = kernel_call(
        mlp_kernel,
        [((group, width), BF16), ((rows, width), F32), ((rows, width), BF16), ((1, hidden), F32)],
        [mid, cot, vecs, up_weight, down_weight],
        hbm={3: (up_weight.shape, tiles(hidden // TILE, 1)), 4: (down_weight.shape, tiles(hidden // TILE, 0))},
        flops=2 * group * width * hidden * 4,
        scratch=[pltpu.VMEM((group, width), F32), pltpu.VMEM((group, width), F32)],
        limit=24,
    )
    gmid_part, m1, m2 = lax.optimization_barrier((gmid_part, m1, m2))
    m3 = hop(m2, masks[0])
    o1, o2 = swap(m1), swap(m2)
    gmid_recv = swap(gmid_part)
    gmid, gattn, mid_sums, msg_attn = kernel_call(
        gmid_kernel,
        [((rows, width), F32), ((group, width), BF16), ((8, width), F32), ((rows, 2 * width), BF16)],
        [gmid_part, gmid_recv, middle, cot, normed, vecs],
        flops=1 << 28,
    )
    gn_mine, gn_other, qkv_sums = kernel_call(
        attn_grad_kernel,
        [((rows, width), F32), ((rows, width), BF16), ((3, cols), F32)],
        [sc, gattn, out_weight, qkv, lse, w_qkv],
        smem=(0,),
        hbm={2: whole(out_weight.shape), 5: (w_qkv.shape, by_row(3))},
        flops=2 * group * width * 4 * cols * 3,
        scratch=[pltpu.VMEM((group, 3 * cols), BF16)],
        limit=20,
    )
    gn_other, m3, o1, o2 = lax.optimization_barrier((gn_other, m3, o1, o2))
    gn_recv = swap(gn_other)
    msg_attn = after(msg_attn, gn_other)
    a1, a2 = (hop(msg_attn, m) for m in masks[:2])
    mlp_shared = [m1, m2, m3, o1, o2, swap(m3)]
    back, norm_sums = kernel_call(
        last_kernel,
        [((rows, 2 * width), BF16), ((2, width), F32)],
        [gn_mine, gn_recv, x, gmid, middle, mlp_mine, swap(mlp_other), vecs, got],
        flops=1 << 28,
    )

    n_vec = 6 * width
    sums = jnp.concatenate(
        [
            norm_sums.reshape(-1),
            mid_sums[:4].reshape(-1),
            qkv_sums[0],
            qkv_sums[2],
            up_sums.reshape(-1),
        ]
    )
    n_sum = sums.size
    msg = jnp.concatenate([sums, jnp.pad(tops[:, 0], (0, PAD - tops.shape[0]))]).reshape(-1, PAD)
    is_top = iota(msg.shape, 0) == n_sum // PAD

    def combine(msg, *came):
        return functools.reduce(lambda a, b: jnp.where(is_top, jnp.maximum(a, b), a + b), (msg, *came))

    near = [1 << b for b in rs_bits[:2]]
    came = [hop(msg, m) for m in near + [near[0] | near[1]]]
    later = [b for b in range(n_bits) if b not in rs_bits[:2]]
    restored = exchange(back)

    block = width // n_dp
    first = rs_bits[0]
    def step(i, recv, keep):
        n, w = keep.shape
        left = [b for b in range(n_bits) if b not in rs_bits[:i]]
        run = run_lengths(left, block)[rs_bits[i]]
        return kernel_call(
            functools.partial(step_kernel, rs_bits[i], run),
            [((n // 2, w), BF16), ((n // 2, w), F32)],
            [sc, keep, recv],
            smem=(0,),
            flops=1 << 26,
            scratch=[pltpu.VMEM((n, w), F32)],
        )

    half = ((width // 2, q_hidden), BF16), ((width // 2, q_hidden), F32)
    send_down, keep_down, send_up, keep_up = kernel_call(
        functools.partial(mlp_weights_kernel, n_bits, first),
        [half[0], half[1], half[0], half[1]],
        [sc, after(mid, norm_sums), cot] + mlp_shared + [vecs, up_weight, down_weight],
        smem=(0,),
        hbm={
            **gathered([(1, 0), (2, 1)], [3, 6, 4, 7, 5, 8], rows),
            10: ((width, q_hidden), columns(q_hidden, 1)),
            11: ((q_hidden, width), columns(q_hidden, 0)),
        },
        limit=28,
        flops=2 * 4 * group * width * q_hidden * 4,
        scratch=[
            pltpu.VMEM((4 * group, width), BF16),
            pltpu.VMEM((4 * group, width), BF16),
            pltpu.VMEM((width, q_hidden), F32),
        ],
    )
    send_down, send_up, a1, a2, restored, *came = lax.optimization_barrier(
        (send_down, send_up, a1, a2, restored, *came)
    )
    msg = combine(msg, *came)
    a3 = hop(a1, masks[1])
    b1, b2 = swap(a1), swap(a2)
    recv_down = hop(send_down, 1 << first)

    def attn_scratch(n):
        return [
            pltpu.VMEM((n * group, width), BF16),
            pltpu.VMEM((n * group, width), BF16),
            pltpu.VMEM((n * group, q_cols), BF16),
            pltpu.VMEM((n * group, 3 * q_cols), BF16),
        ]

    def quarter_weights(i):
        return {
            i: ((2, q_cols), columns(q_cols, 1)),
            i + 1: ((3, width, q_cols), columns(q_cols, 1)),
            i + 2: ((q_cols, width), columns(q_cols, 0)),
        }

    (part_attn,) = kernel_call(
        functools.partial(attn_first_kernel, n_dp, [0] + masks[:2]),
        [((width, 4 * q_cols), F32)],
        [sc, got, normed, gattn, a1, a2, b1, b2, qv_bias, w_qkv, out_weight],
        smem=(0,),
        hbm={**gathered([(2, 1), (3, 0)], [4, 6, 5, 7], rows), **quarter_weights(8)},
        limit=24,
        loose=(6, 7),
        flops=2 * 3 * group * width * q_cols * 12,
        scratch=attn_scratch(3),
    )
    a3, recv_down, part_attn = lax.optimization_barrier((a3, recv_down, part_attn))

    def hand_out(*pairs):
        n, w = pairs[0][0].shape
        w *= len(pairs)
        pieces = kernel_call(
            functools.partial(pieces_kernel, len(pairs)),
            [((block, w), F32)] + [((block, w), BF16)] * 3,
            [sc] + [a for pair in pairs for a in pair],
            smem=(0,),
            flops=1 << 26,
            scratch=[pltpu.VMEM((n, w), F32)],
        )
        return [pieces[0]] + [hop(p, m) for p, m in zip(pieces[1:], masks)]

    def clip(msg):
        threshold = clip_tau[0].astype(F32)
        head_factor = jnp.sqrt(threshold / jnp.maximum(msg[-1, : tops.shape[0]], threshold))
        column_factor = jnp.repeat(head_factor, HD)
        clipped_qk = pl.pallas_call(
            clip_kernel,
            grid=(4,),
            out_shape=jax.ShapeDtypeStruct((width, 2, cols), BF16),
            in_specs=[
                pl.BlockSpec((2, width // 4, cols), lambda i: (0, i, 0)),
                pl.BlockSpec((1, cols), lambda i: (0, 0)),
            ],
            out_specs=pl.BlockSpec((width // 4, 2, cols), lambda i: (i, 0, 0)),
            name="clip_kernel",
        )(w_qkv, column_factor.reshape(1, cols))
        return clipped_qk, head_factor, column_factor

    def join_mlp(pieces):
        return kernel_call(join_mlp_kernel, [((block, hidden), F32)], [sc] + pieces, smem=(0,))[0]

    n_steps = len(rs_bits)
    recvs = {0: recv_down}
    sends = {1: send_up}
    keeps = {0: keep_down, 1: keep_up}
    for t in range(1, n_steps + 2):
        active = [i for i in range(3) if 0 <= t - i < n_steps]
        gate = ()
        for i in active:
            if t > i:
                sends[i], keeps[i] = step(t - i, recvs[i], keeps[i])
                gate = (sends[i],)
        for i in active:
            recvs[i] = hop(after(sends[i], *gate), 1 << rs_bits[t - i])
        extra = []
        if t <= n_steps:
            msg = after(msg, *gate)
            came = hop(msg, 1 << later[t - 1])
        if t == 1:
            send_attn, keep_attn = kernel_call(
                functools.partial(attn_weights_kernel, n_bits, first, n_dp, masks[2:]),
                [((width // 2, 4 * q_cols), BF16), ((width // 2, 4 * q_cols), F32)],
                [sc, got, part_attn, a3, swap(a3), qv_bias, w_qkv, out_weight],
                smem=(0,),
                hbm={**gathered([], [3, 4], rows, 0), **quarter_weights(5)},
                limit=20,
                loose=(4,),
                flops=2 * group * width * q_cols * 12,
                scratch=attn_scratch(1) + [pltpu.VMEM((width, 4 * q_cols), F32)],
            )
            sends[2], keeps[2] = send_attn, keep_attn
            out_tokens, grad_tokens = kernel_call(
                restore_kernel,
                [((rows, width), BF16)] * 2,
                [pick, after(restored, *gate)],
                flops=1 << 27,
            )
            extra = [out_tokens, grad_tokens, sends[2]]
        if t >= n_steps:
            mlp_pieces = hand_out((after(keeps[t - n_steps], *gate), recvs[t - n_steps]))
            extra = mlp_pieces[1:]
        if t == n_steps + 1:
            clipped_qk, head_factor, column_factor = clip(msg)
            extra = extra + [clipped_qk, grad_down]
        done = lax.optimization_barrier([recvs[i] for i in active] + [came] + extra)
        recvs.update(zip(active, done))
        if t <= n_steps:
            msg = combine(msg, done[len(active)])
        if t == 1:
            out_tokens, grad_tokens, sends[2] = done[-3:]
        if t == n_steps + 1:
            mlp_pieces[1:], clipped_qk, grad_down = done[-5:-2], done[-2], done[-1]
            grad_up = join_mlp(mlp_pieces)
        if t == n_steps:
            mlp_pieces[1:] = done[-3:]
            grad_down = join_mlp(mlp_pieces)
    attn_pieces = hand_out((keeps[2], recvs[2]))
    grad_up, *attn_pieces[1:] = lax.optimization_barrier((grad_up, *attn_pieces[1:]))
    grad_down = grad_down.T
    grad_qkv, grad_out = kernel_call(
        join_attn_kernel, [((3, block, cols), F32), ((block, cols), F32)], [sc] + attn_pieces, smem=(0,)
    )
    grad_qkv = jnp.transpose(grad_qkv, (1, 0, 2))
    grad_out = grad_out.T

    theirs = swap(msg).reshape(-1)
    msg = msg.reshape(-1)
    vector_sum = (msg[:n_vec] + theirs[:n_vec]).reshape(6, width)
    own, oth = msg[n_vec:n_sum], theirs[n_vec:n_sum]
    one = jnp.where(core == 0, own, oth)
    two = jnp.where(core == 0, oth, own)
    qv_sum = jnp.stack(
        [
            jnp.concatenate([one[:cols], two[:cols]]),
            jnp.concatenate([one[cols : 2 * cols], two[cols : 2 * cols]]),
        ]
    )
    up_sum = jnp.concatenate([one[2 * cols :], two[2 * cols :]])

    clipped_q_bias = (f(qv_bias[0]) * column_factor).astype(BF16)
    return (
        out_tokens,
        grad_tokens,
        grad_qkv,
        grad_out,
        grad_up,
        grad_down,
        qv_sum,
        up_sum,
        vector_sum,
        head_factor,
        clipped_qk,
        clipped_q_bias,
    )

def solution(mesh):
    placed = (
        P(("dp", "tensor"), None),
        P(("dp", "tensor"), None),
        P(("dp", "tensor")),
        P("dp", None),
        P(),
        P(),
        P(),
        P(None, None, "tensor"),
        P(None, "tensor"),
        P("tensor", None),
        P(),
        P(),
        P(),
        P(None, "tensor"),
        P("tensor"),
        P("tensor", None),
        P(),
    )
    return jax.shard_map(
        local,
        mesh=mesh,
        in_specs=placed,
        out_specs=(
            P(("dp", "tensor"), None),
            P(("dp", "tensor"), None),
            P("dp", None, "tensor"),
            P("tensor", "dp"),
            P("dp", "tensor"),
            P("tensor", "dp"),
            P(),
            P(),
            P(),
            P("tensor"),
            P(None, None, "tensor"),
            P("tensor"),
        ),
        check_vma=False,
    )
```

```python
import functools
import jax
import jax.numpy as jnp
from jax import lax
from jax.experimental import pallas as pl
from jax.experimental.pallas import tpu as pltpu
from jax.sharding import PartitionSpec as P

HD = 64
AG_BITS = (0, 2)
PAD = 128
COST = 1

epsilon = 1e-05
masked_value = -1e30
gelu_coef = 0.7978845608028654
F32 = jnp.float32
BF16 = jnp.bfloat16
I32 = jnp.int32


def f(x):
    return x.astype(F32)


def dot(a, b, ca, cb):
    return lax.dot_general(a, b, (((ca,), (cb,)), ((), ())), preferred_element_type=F32)


def nn(a, b):
    return dot(a, b, 1, 0)


def nt(a, b):
    return dot(a, b, 1, 1)


def tn(a, b):
    return dot(a, b, 0, 0)


def norm_stats(values):
    row_mean = jnp.mean(values, axis=-1, keepdims=True)
    centered = values - row_mean
    variance = jnp.mean(centered * centered, axis=-1, keepdims=True)
    inv = lax.rsqrt(variance + epsilon)
    return centered * inv, inv


def norm_grad(xhat, inv, gain, grad):
    scaled = grad * gain
    a = jnp.mean(scaled, axis=-1, keepdims=True)
    b = jnp.mean(scaled * xhat, axis=-1, keepdims=True)
    return inv * (scaled - a - xhat * b)


def gelu_parts(p):
    p2 = p * p
    th = jnp.tanh(gelu_coef * (p + 0.044715 * p2 * p))
    half = 0.5 * (1.0 + th)
    slope = half + 0.5 * p * (1.0 - th * th) * (gelu_coef * (1.0 + 3.0 * 0.044715 * p2))
    return p * half, slope


def iota(shape, axis):
    return lax.broadcasted_iota(I32, shape, axis)


def place_matrix(ids):
    rows = ids.shape[0]
    return (ids == f(iota((rows, rows), 1))).astype(BF16)


def pair_mask(ends, core, rows):
    group = 2 * rows
    pos_r = (iota((group, 1), 0) + core * rows) & (group - 1)
    pos_c = (iota((1, group), 1) + core * rows) & (group - 1)
    sid_r = sum((pos_r >= e).astype(I32) for e in ends)
    sid_c = sum((pos_c >= e).astype(I32) for e in ends)
    sid_r = jnp.where(pos_r < ends[-1], sid_r, -1)
    same = (sid_r == sid_c).astype(I32) * (pos_c <= pos_r).astype(I32)
    diagonal = (pos_r == pos_c).astype(I32)
    return (same + diagonal) > 0, sid_r >= 0


def half_lanes():
    lane = iota((1, PAD), 1)
    low = (lane < HD).astype(F32)
    return (low.astype(BF16), (1.0 - low).astype(BF16)), (low, 1.0 - low)


def head_probs(q2, k2, lanes, mask):
    s = jnp.where(mask, nt(q2 * lanes, k2) * 0.125, masked_value)
    top = jnp.max(s, axis=-1, keepdims=True)
    e = jnp.exp(s - top)
    total = jnp.sum(e, axis=-1, keepdims=True)
    return e, top, total


def head_grad(q2, k2, v2, gc2, lanes, p):
    gp = nt(gc2 * lanes, v2)
    row_dot = jnp.sum(p * gp, axis=-1, keepdims=True)
    ds = (p * (gp - row_dot)).astype(BF16)
    return nn(ds, k2) * 0.125, tn(ds, q2) * 0.125, tn(p.astype(BF16), gc2)


class Fetched:
    def __init__(self, ref, copies):
        self.ref, self.copies, self.shape = ref, copies, getattr(ref, "shape", None)

    def wait(self, k=None):
        for c in self.copies if k is None else [self.copies[k]]:
            c.wait()
        return self.ref


def whole(shape):
    return shape, lambda src, dst, sc: [(src, dst)]


def kernel_call(body, outs, args, smem=(), hbm=None, flops=0, scratch=(), limit=12, loose=()):
    hbm = hbm or {}
    specs = []
    n_bytes = 0
    for i, a in enumerate(args):
        n_bytes += a.size * a.dtype.itemsize
        space = pl.ANY if i in loose else pltpu.HBM if i in hbm else pltpu.SMEM if i in smem else pltpu.VMEM
        specs.append(pl.BlockSpec(memory_space=space))
    shapes = [jax.ShapeDtypeStruct(s, d) for s, d in outs]
    out_specs = [pl.BlockSpec(memory_space=pltpu.VMEM) for _ in outs]
    args = [pltpu.with_memory_space_constraint(a, pltpu.HBM) if i in hbm and i not in loose else a for i, a in enumerate(args)]
    n_in, n_out, n_scratch = len(args), len(outs), len(scratch)
    extra = []
    own = [i for i, (shape, _) in hbm.items() if shape is not None]
    for i in own:
        extra.append(pltpu.VMEM(hbm[i][0], args[i].dtype))
    n_chunks = {}
    for i, (shape, chunks) in hbm.items():
        n_chunks[i] = getattr(chunks, "count", 1)
        extra.append(pltpu.SemaphoreType.DMA((n_chunks[i],)))

    def run(*refs):
        ins = list(refs[:n_in])
        rest = refs[n_in + n_out + n_scratch :]
        sc = ins[0]
        for j, (i, (_, chunks)) in enumerate(hbm.items()):
            dst = rest[own.index(i)] if i in own else refs[n_in + n_out :]
            sem = rest[len(own) + j]
            copies = [
                pltpu.make_async_copy(a, b, sem.at[k]) for k, (a, b) in enumerate(chunks(ins[i], dst, sc))
            ]
            for c in copies:
                c.start()
            ins[i] = Fetched(dst, copies)
        body(*ins, *refs[n_in : n_in + n_out + n_scratch])

    return pl.pallas_call(
        run,
        out_shape=shapes,
        in_specs=specs,
        out_specs=out_specs,
        scratch_shapes=list(scratch) + extra,
        compiler_params=pltpu.CompilerParams(vmem_limit_bytes=limit << 20),
        cost_estimate=pl.CostEstimate(
            flops=int(flops * COST), transcendentals=0, bytes_accessed=int(n_bytes * COST)
        ),
        name=body.func.__name__ if hasattr(body, "func") else body.__name__,
    )(*args)


def chunked(count, make):
    def chunks(src, dst, sc):
        return [make(src, dst, sc, k) for k in range(count)]

    chunks.count = count
    return chunks


def gathered(own_args, shared_args, rows, start=2):
    spec = {}
    for i, at in own_args:
        spec[i] = (None, chunked(1, lambda src, dst, sc, k, at=at: (src, dst[at].at[pl.ds(0, 2 * rows), :])))
    for j, i in enumerate(shared_args):

        def make(src, dst, sc, k, j=j):
            width = dst[0].shape[1]
            return src.at[:, pl.ds(k * width, width)], dst[k].at[pl.ds((start + j) * rows, rows), :]

        spec[i] = (None, chunked(2, make))
    return spec


def by_row(count):
    return chunked(count, lambda src, dst, sc, k: (src.at[k], dst.at[k]))


def tiles(count, axis):
    def make(src, dst, sc, k):
        at = pl.ds(k * TILE, TILE)
        return (src.at[at, :], dst.at[at, :]) if axis == 0 else (src.at[:, at], dst.at[:, at])

    return chunked(count, make)


def columns(n, axis):
    def chunks(src, dst, sc):
        at = pl.ds(pl.multiple_of(sc[2] * n, n), n)
        if axis == 0:
            return [(src.at[at, :], dst)]
        return [(src.at[(slice(None),) * (len(src.shape) - 1) + (at,)], dst)]

    return chunks


def route_kernel(n_dp, route, lens, tokens, cotangent, msg, pick_out):
    rows, width = tokens.shape
    row = jnp.broadcast_to(f(route.wait()[...]), (rows, rows))
    col = row.T
    group = float(2 * rows)
    dest_r = jnp.floor(row / group)
    dest_c = jnp.floor(col / group)
    before = iota((rows, rows), 0) < iota((rows, rows), 1)
    same = jnp.where(before, (dest_r == dest_c).astype(F32), 0.0)
    rank = dest_r[0:1] * (rows // n_dp) + jnp.sum(same, axis=0, keepdims=True)
    pick = (jnp.broadcast_to(rank, (rows, rows)) == f(iota((rows, rows), 0))).astype(F32)
    place = row - jnp.floor(row / float(rows)) * float(rows)
    ids = jnp.sum(pick * place, axis=1, keepdims=True)
    lane = iota((rows, PAD), 1)
    extra = jnp.where(lane == 0, ids, 0.0)
    lens = f(lens.wait()[...])
    for i in range(4):
        extra = jnp.where(lane == i + 1, lens[:, i : i + 1], extra)
    pick_b = pick.astype(BF16)
    pick_out[...] = pick_b
    msg[:, :width] = nn(pick_b, tokens.wait()[...]).astype(BF16)
    msg[:, 2 * width :] = extra.astype(BF16)
    msg[:, width : 2 * width] = nn(pick_b, cotangent.wait()[...]).astype(BF16)


def ends_of(sc):
    e = [sc[4]]
    for i in range(1, 4):
        e.append(e[-1] + sc[4 + i])
    return e


def attn_kernel(
    sc, mine, other, vecs, w_qkv, qv_bias, w_out, x_out, normed_out, qkv_out, lse_out, top_out, part_out, ctx_out
):
    rows = mine.shape[0]
    width = w_out.shape[1]
    cols = w_out.shape[0]
    for i, half in enumerate((mine, other)):
        put = place_matrix(f(half[:, 2 * width : 2 * width + 1]))
        x = tn(put, half[:, :width])
        s = slice(i * rows, (i + 1) * rows)
        x_out[s, :] = x.astype(BF16)
        xhat, _ = norm_stats(x)
        normed_out[s, :] = (xhat * vecs[0:1, :] + vecs[1:2, :]).astype(BF16)
    normed = normed_out[...]
    qv_bias = qv_bias.wait()
    for c in range(3):
        y = nn(normed, w_qkv.wait(c)[c])
        if c == 0:
            y = y + f(qv_bias[0:1, :])
        if c == 2:
            y = y + f(qv_bias[1:2, :])
        qkv_out[:, c * cols : (c + 1) * cols] = y.astype(BF16)
    mask, live = pair_mask(ends_of(sc), sc[0], rows)
    lanes_b, lanes_f = half_lanes()
    lane = iota((1, PAD), 1)
    lse = jnp.zeros((2 * rows, PAD), F32)
    for pair in range(cols // PAD):
        s = slice(pair * PAD, (pair + 1) * PAD)
        q2 = qkv_out[:, s]
        k2 = qkv_out[:, slice(cols + pair * PAD, cols + (pair + 1) * PAD)]
        v2 = qkv_out[:, slice(2 * cols + pair * PAD, 2 * cols + (pair + 1) * PAD)]
        out = jnp.zeros((2 * rows, PAD), F32)
        for i in range(2):
            e, top, total = head_probs(q2, k2, lanes_b[i], mask)
            probs = (e * (1.0 / total)).astype(BF16)
            out = out + nn(probs, v2) * lanes_f[i]
            h = 2 * pair + i
            lse = jnp.where(lane == h, top + jnp.log(total), lse)
            best = jnp.max(jnp.where(live, top, masked_value), axis=0, keepdims=True)
            top_out[h : h + 1, :] = jnp.broadcast_to(best, (1, PAD))
        ctx_out[:, s] = out.astype(BF16)
    lse_out[...] = lse
    part_out[...] = nn(ctx_out[...], w_out.wait()[...]).astype(BF16)


def middle_kernel(x, part, recv, vecs, mine, other, middle_out, mid_out, cot_out, msg_out):
    rows, width = msg_out.shape[0], x.shape[1]
    for i, half in enumerate((mine, other)):
        s = slice(i * rows, (i + 1) * rows)
        o = slice((1 - i) * rows, (2 - i) * rows)
        put = place_matrix(f(half[:, 2 * width : 2 * width + 1]))
        cot = tn(put, half[:, width : 2 * width]).astype(BF16)
        cot_out[s, :] = cot
        middle = f(x[s, :]) + (f(part[s, :]) + f(recv[o, :])) + vecs[2:3, :]
        middle_out[s, :] = middle
        mhat, _ = norm_stats(middle)
        mid = (mhat * vecs[3:4, :] + vecs[4:5, :]).astype(BF16)
        mid_out[s, :] = mid
        if i == 0:
            msg_out[:, :width] = mid
            msg_out[:, width:] = cot


TILE = 1024


def mlp_kernel(mid, cot, vecs, up, down, gmid_out, mine_out, other_out, sums_out, acc, acc_y):
    width, hidden = up.shape
    rows = mine_out.shape[0]
    per_row = width // TILE
    for t in range(hidden // TILE):
        s = slice(t * TILE, (t + 1) * TILE)
        bias = vecs[6 + t // per_row : 7 + t // per_row, (t % per_row) * TILE : (t % per_row + 1) * TILE]
        act, slope = gelu_parts(nn(mid[...], up.wait(t)[:, s]) + bias)
        gpre = (nt(cot[...], down.wait(t)[s, :]) * slope).astype(BF16)
        sums_out[:, s] = jnp.sum(f(gpre), axis=0, keepdims=True)
        g = nt(gpre, up.ref[:, s])
        y = nn(act.astype(BF16), down.ref[s, :])
        if t == 0:
            acc[...] = g
            acc_y[...] = y
        else:
            acc[...] += g
            acc_y[...] += y
    gmid_out[...] = acc[...].astype(BF16)
    mine_out[...] = acc_y[:rows, :]
    other_out[...] = acc_y[rows:, :].astype(BF16)


def gmid_kernel(part, recv, middle, cot, normed, vecs, gmid_out, gattn_out, sums_out, msg_out):
    rows, width = gmid_out.shape
    msg_out[:, width:] = normed[:rows, :]
    for i in range(2):
        s = slice(i * rows, (i + 1) * rows)
        o = slice((1 - i) * rows, (2 - i) * rows)
        g = f(part[s, :]) + f(recv[o, :])
        mhat, inv = norm_stats(middle[s, :])
        c = f(cot[s, :])
        gm = c + norm_grad(mhat, inv, vecs[3:4, :], g)
        gattn = gm.astype(BF16)
        gattn_out[s, :] = gattn
        if i == 0:
            gmid_out[...] = gm
            msg_out[:, :width] = gattn
            sums_out[0:1, :] = jnp.sum(gm, axis=0, keepdims=True)
            sums_out[1:2, :] = jnp.sum(g * mhat, axis=0, keepdims=True)
            sums_out[2:3, :] = jnp.sum(g, axis=0, keepdims=True)
            sums_out[3:4, :] = jnp.sum(c, axis=0, keepdims=True)
            sums_out[4:8, :] = jnp.zeros((4, sums_out.shape[1]), F32)


def attn_grad_kernel(sc, gattn, w_out, qkv, lse, w_qkv, mine_out, other_out, sums_out, gqkv):
    rows = gattn.shape[0] // 2
    cols = w_out.shape[0]
    mask, _ = pair_mask(ends_of(sc), sc[0], rows)
    gctx = nt(gattn[...], w_out.wait()[...]).astype(BF16)
    lanes_b, lanes_f = half_lanes()
    for pair in range(cols // PAD):
        cut = [slice(c * cols + pair * PAD, c * cols + (pair + 1) * PAD) for c in range(3)]
        q2, k2, v2 = (qkv[:, c] for c in cut)
        gc2 = gctx[:, pair * PAD : (pair + 1) * PAD]
        total = None
        for i in range(2):
            h = 2 * pair + i
            s = jnp.where(mask, nt(q2 * lanes_b[i], k2) * 0.125, masked_value)
            p = jnp.exp(s - lse[:, h : h + 1])
            g3 = [g * lanes_f[i] for g in head_grad(q2, k2, v2, gc2, lanes_b[i], p)]
            total = g3 if total is None else [a + b for a, b in zip(total, g3)]
        for c in range(3):
            g = total[c].astype(BF16)
            gqkv[:, cut[c]] = g
            sums_out[c : c + 1, pair * PAD : (pair + 1) * PAD] = jnp.sum(f(g), axis=0, keepdims=True)
    y = sum(nt(gqkv[:, c * cols : (c + 1) * cols], w_qkv.wait(c)[c]) for c in range(3))
    mine_out[...] = y[:rows]
    other_out[...] = y[rows:].astype(BF16)


def last_kernel(part, recv, x, gmid, middle, y_mine, y_other, vecs, ids, msg_out, sums_out):
    rows, width = part.shape
    put = place_matrix(f(ids[:, 2 * width : 2 * width + 1]))
    res = middle[:rows, :] + (y_mine[...] + f(y_other[...])) + vecs[5:6, :]
    msg_out[:, :width] = nn(put, res.astype(BF16)).astype(BF16)
    g = part[...] + f(recv[...])
    xhat, inv = norm_stats(f(x[:rows, :]))
    grad = (gmid[...] + norm_grad(xhat, inv, vecs[0:1, :], g)).astype(BF16)
    sums_out[0:1, :] = jnp.sum(g * xhat, axis=0, keepdims=True)
    sums_out[1:2, :] = jnp.sum(g, axis=0, keepdims=True)
    msg_out[:, width:] = nn(put, grad).astype(BF16)


def restore_kernel(pick, msg, out, grad):
    width = out.shape[1]
    y = tn(pick[...], msg[...]).astype(BF16)
    out[...] = y[:, :width]
    grad[...] = y[:, width:]


def clip_kernel(w, factor, out):
    for c in range(2):
        out[:, c, :] = (f(w[c]) * factor[...]).astype(BF16)


def run_lengths(bits, block):
    return {b: block << i for i, b in enumerate(sorted(bits))}


def split_rows(src, run, mine, send_out, keep_out, at):
    n = src.shape[0]
    for j in range(n // (2 * run)):
        k = pl.multiple_of(2 * run * j + mine * run, run)
        s = pl.multiple_of(2 * run * j + (1 - mine) * run, run)
        dst = slice(j * run, (j + 1) * run)
        keep_out[dst, at] = src[pl.ds(k, run), :]
        send_out[dst, at] = src[pl.ds(s, run), :].astype(BF16)


def mlp_weights_kernel(
    n_bits, bit, sc, mid, cot, m1, m2, m3, o1, o2, o3, vecs, up, down,
    send_down, keep_down, send_up, keep_up, mids, cots, grad,
):
    for x in (mid, cot, m1, m2, m3, o1, o2, o3):
        x.wait()
    q_hidden = down.shape[0]
    per_row = mids.shape[1] // q_hidden
    bias = jnp.zeros((1, q_hidden), F32)
    for k in range(4):
        part = vecs[6 + k // per_row : 7 + k // per_row, (k % per_row) * q_hidden : (k % per_row + 1) * q_hidden]
        bias = jnp.where(sc[2] == k, part, bias)
    mine = (sc[1] >> bit) & 1
    run = (mids.shape[1] >> n_bits) << bit
    act, slope = gelu_parts(nn(mids[...], up.wait()[...]) + bias)
    every = slice(None)
    grad[...] = tn(cots[...], act.astype(BF16))
    split_rows(grad, run, mine, send_down, keep_down, every)
    gpre = (nt(cots[...], down.wait()[...]) * slope).astype(BF16)
    grad[...] = tn(mids[...], gpre)
    split_rows(grad, run, mine, send_up, keep_up, every)


def attn_quarter(n_dp, masks, sc, ids, qv_bias, w_qkv, w_out, gattns, norms, ctx, gqkv):
    group = norms.shape[0] // len(masks)
    rows = group // 2
    me = sc[1]
    norm4 = norms[...]
    w_qkv, qv_bias = w_qkv.wait(), qv_bias.wait()
    q4 = (nn(norm4, w_qkv[0]) + f(qv_bias[0:1, :])).astype(BF16)
    k4 = nn(norm4, w_qkv[1]).astype(BF16)
    v4 = (nn(norm4, w_qkv[2]) + f(qv_bias[1:2, :])).astype(BF16)
    gc4 = nt(gattns[...], w_out.wait()[...]).astype(BF16)
    lanes_b, lanes_f = half_lanes()
    table = f(ids[:, 2 * norms.shape[1] :])
    from_dp = iota((rows, 1), 0) // (rows // n_dp)
    first = iota((rows, 1), 0) == from_dp * (rows // n_dp)
    for g, bits in enumerate(masks):
        chosen = jnp.where((from_dp == (me ^ bits)) & first, table, 0.0)
        lens = jnp.sum(chosen, axis=0, keepdims=True)
        ends = [lens[:, 1:2]]
        for i in range(2, 5):
            ends.append(ends[-1] + lens[:, i : i + 1])
        mask, _ = pair_mask([e.astype(I32) for e in ends], sc[0], rows)
        s = slice(g * group, (g + 1) * group)
        q2, k2, v2, gc2 = q4[s], k4[s], v4[s], gc4[s]
        out = jnp.zeros((group, PAD), F32)
        total = None
        for i in range(2):
            e, _, denom = head_probs(q2, k2, lanes_b[i], mask)
            p = e * (1.0 / denom)
            out = out + nn(p.astype(BF16), v2) * lanes_f[i]
            g3 = [x * lanes_f[i] for x in head_grad(q2, k2, v2, gc2, lanes_b[i], p)]
            total = g3 if total is None else [a + b for a, b in zip(total, g3)]
        ctx[s, :] = out.astype(BF16)
        for c in range(3):
            gqkv[s, c * PAD : (c + 1) * PAD] = total[c].astype(BF16)


def attn_first_kernel(
    n_dp, masks, sc, ids, nrm, ga, m1, m2, o1, o2, qv_bias, w_qkv, w_out, grad, gattns, norms, ctx, gqkv
):
    for x in (ga, nrm, m1, m2, o1, o2):
        x.wait()
    attn_quarter(n_dp, masks, sc, ids, qv_bias, w_qkv, w_out, gattns, norms, ctx, gqkv)
    grad[:, : 3 * PAD] = tn(norms[...], gqkv[...])
    grad[:, 3 * PAD :] = tn(gattns[...], ctx[...])


def attn_weights_kernel(
    n_bits, bit, n_dp, masks, sc, ids, base, m3, o3, qv_bias, w_qkv, w_out,
    send_out, keep_out, gattns, norms, ctx, gqkv, grad,
):
    m3.wait()
    o3.wait()
    run = (norms.shape[1] >> n_bits) << bit
    attn_quarter(n_dp, masks, sc, ids, qv_bias, w_qkv, w_out, gattns, norms, ctx, gqkv)
    grad[:, : 3 * PAD] = base[:, : 3 * PAD] + tn(norms[...], gqkv[...])
    grad[:, 3 * PAD :] = base[:, 3 * PAD :] + tn(gattns[...], ctx[...])
    split_rows(grad, run, (sc[1] >> bit) & 1, send_out, keep_out, slice(None))


def step_kernel(bit, run, sc, keep, recv, send_out, keep_out, cur):
    cur[...] = keep[...] + f(recv[...])
    split_rows(cur, run, (sc[1] >> bit) & 1, send_out, keep_out, slice(None))


def pieces_kernel(n_pairs, sc, *refs):
    pairs, (own, p1, p2, p3), cur = refs[: 2 * n_pairs], refs[2 * n_pairs : -1], refs[-1]
    n = own.shape[0]
    w = pairs[0].shape[1]
    for i in range(n_pairs):
        cur[:, i * w : (i + 1) * w] = pairs[2 * i][...] + f(pairs[2 * i + 1][...])
    q = sc[2]
    for j, out in enumerate((own, p1, p2, p3)):
        out[...] = cur[pl.ds(pl.multiple_of((q ^ j) * n, n), n), :].astype(out.dtype)


def join_mlp_kernel(sc, own, p1, p2, p3, out):
    w = own.shape[1]
    for j, p in enumerate((own, p1, p2, p3)):
        out[:, pl.ds(pl.multiple_of((sc[2] ^ j) * w, w), w)] = f(p[...])


def join_attn_kernel(sc, own, p1, p2, p3, qkv_out, out_out):
    w = own.shape[1] // 4
    for j, p in enumerate((own, p1, p2, p3)):
        at = pl.ds(pl.multiple_of((sc[2] ^ j) * w, w), w)
        for c in range(3):
            qkv_out[c, :, at] = f(p[:, c * w : (c + 1) * w])
        out_out[:, at] = f(p[:, 3 * w :])


def after(x, *deps):
    return lax.optimization_barrier((x, *deps))[0]


def local(
    tokens,
    cotangent,
    route,
    lengths,
    clip_tau,
    attn_norm_gain,
    attn_norm_bias,
    qkv_weight,
    qv_bias,
    out_weight,
    out_bias,
    mlp_norm_gain,
    mlp_norm_bias,
    up_weight,
    up_bias,
    down_weight,
    down_bias,
):
    n_dp = lax.axis_size("dp")
    n_bits = n_dp.bit_length() - 1
    rs_bits = [b for b in range(n_bits) if b not in AG_BITS]
    masks = [1 << AG_BITS[0], 1 << AG_BITS[1], (1 << AG_BITS[0]) | (1 << AG_BITS[1])]
    me = lax.axis_index("dp")
    core = lax.axis_index("tensor")
    rows, width = tokens.shape
    group = 2 * rows
    cols = qkv_weight.shape[2]
    hidden = up_weight.shape[1]
    q_cols = cols // 4
    q_hidden = hidden // 4
    quarter = ((me >> AG_BITS[0]) & 1) + 2 * ((me >> AG_BITS[1]) & 1)
    sc = jnp.concatenate([jnp.stack([core, me, quarter, core]).astype(I32), lengths[0]])

    def swap(x):
        return lax.ppermute(x, "tensor", [(0, 1), (1, 0)])

    def hop(x, mask):
        return lax.ppermute(x, "dp", [(i, i ^ mask) for i in range(n_dp)])

    def exchange(x):
        return lax.all_to_all(x, "dp", split_axis=0, concat_axis=0, tiled=True)

    def share(own):
        got = [hop(own[:rows], m) for m in masks]
        return got + [swap(g) for g in got]

    w_qkv = jnp.transpose(qkv_weight, (1, 0, 2))
    vecs = jnp.concatenate(
        [attn_norm_gain, attn_norm_bias, out_bias, mlp_norm_gain, mlp_norm_bias, down_bias, up_bias]
    ).astype(F32).reshape(-1, width)

    msg, pick = kernel_call(
        functools.partial(route_kernel, n_dp),
        [((rows, 2 * width + PAD), BF16), ((rows, rows), BF16)],
        [route.reshape(1, rows), lengths, tokens, cotangent],
        hbm={0: whole((1, rows)), 1: whole(lengths.shape), 2: whole(tokens.shape), 3: whole(tokens.shape)},
        flops=4 * rows * rows * width,
    )
    got = after(exchange(msg), vecs, sc)
    other = swap(got)
    x, normed, qkv, lse, tops, part = kernel_call(
        attn_kernel,
        [
            ((group, width), BF16),
            ((group, width), BF16),
            ((group, 3 * cols), BF16),
            ((group, PAD), F32),
            ((cols // HD, PAD), F32),
            ((group, width), BF16),
        ],
        [sc, got, other, vecs, w_qkv, qv_bias, out_weight],
        smem=(0,),
        hbm={4: (w_qkv.shape, by_row(3)), 5: whole(qv_bias.shape), 6: whole(out_weight.shape)},
        flops=2 * group * width * 4 * cols * 3,
        scratch=[pltpu.VMEM((group, cols), BF16)],
        limit=20,
    )
    middle, mid, cot, msg_mlp = kernel_call(
        middle_kernel,
        [((group, width), F32), ((group, width), BF16), ((group, width), BF16), ((rows, 2 * width), BF16)],
        [x, part, swap(part), vecs, got, other],
        flops=1 << 28,
    )
    m1, m2 = (hop(msg_mlp, m) for m in masks[:2])
    gmid_part, mlp_mine, mlp_other, up_sums = kernel_call(
        mlp_kernel,
        [((group, width), BF16), ((rows, width), F32), ((rows, width), BF16), ((1, hidden), F32)],
        [mid, cot, vecs, up_weight, down_weight],
        hbm={3: (up_weight.shape, tiles(hidden // TILE, 1)), 4: (down_weight.shape, tiles(hidden // TILE, 0))},
        flops=2 * group * width * hidden * 4,
        scratch=[pltpu.VMEM((group, width), F32), pltpu.VMEM((group, width), F32)],
        limit=24,
    )
    gmid_part, m1, m2 = lax.optimization_barrier((gmid_part, m1, m2))
    m3 = hop(m2, masks[0])
    o1, o2 = swap(m1), swap(m2)
    gmid_recv = swap(gmid_part)
    gmid, gattn, mid_sums, msg_attn = kernel_call(
        gmid_kernel,
        [((rows, width), F32), ((group, width), BF16), ((8, width), F32), ((rows, 2 * width), BF16)],
        [gmid_part, gmid_recv, middle, cot, normed, vecs],
        flops=1 << 28,
    )
    gn_mine, gn_other, qkv_sums = kernel_call(
        attn_grad_kernel,
        [((rows, width), F32), ((rows, width), BF16), ((3, cols), F32)],
        [sc, gattn, out_weight, qkv, lse, w_qkv],
        smem=(0,),
        hbm={2: whole(out_weight.shape), 5: (w_qkv.shape, by_row(3))},
        flops=2 * group * width * 4 * cols * 3,
        scratch=[pltpu.VMEM((group, 3 * cols), BF16)],
        limit=20,
    )
    gn_other, m3, o1, o2 = lax.optimization_barrier((gn_other, m3, o1, o2))
    gn_recv = swap(gn_other)
    msg_attn = after(msg_attn, gn_other)
    a1, a2 = (hop(msg_attn, m) for m in masks[:2])
    mlp_shared = [m1, m2, m3, o1, o2, swap(m3)]
    back, norm_sums = kernel_call(
        last_kernel,
        [((rows, 2 * width), BF16), ((2, width), F32)],
        [gn_mine, gn_recv, x, gmid, middle, mlp_mine, swap(mlp_other), vecs, got],
        flops=1 << 28,
    )

    n_vec = 6 * width
    sums = jnp.concatenate(
        [
            norm_sums.reshape(-1),
            mid_sums[:4].reshape(-1),
            qkv_sums[0],
            qkv_sums[2],
            up_sums.reshape(-1),
        ]
    )
    n_sum = sums.size
    msg = jnp.concatenate([sums, jnp.pad(tops[:, 0], (0, PAD - tops.shape[0]))]).reshape(-1, PAD)
    is_top = iota(msg.shape, 0) == n_sum // PAD

    def combine(msg, *came):
        return functools.reduce(lambda a, b: jnp.where(is_top, jnp.maximum(a, b), a + b), (msg, *came))

    near = [1 << b for b in rs_bits[:2]]
    came = [hop(msg, m) for m in [near[0] | near[1]] + near]
    later = [b for b in range(n_bits) if b not in rs_bits[:2]]
    restored = exchange(back)

    block = width // n_dp
    first = rs_bits[0]
    def step(i, recv, keep):
        n, w = keep.shape
        left = [b for b in range(n_bits) if b not in rs_bits[:i]]
        run = run_lengths(left, block)[rs_bits[i]]
        return kernel_call(
            functools.partial(step_kernel, rs_bits[i], run),
            [((n // 2, w), BF16), ((n // 2, w), F32)],
            [sc, keep, recv],
            smem=(0,),
            flops=1 << 26,
            scratch=[pltpu.VMEM((n, w), F32)],
        )

    half = ((width // 2, q_hidden), BF16), ((width // 2, q_hidden), F32)
    send_down, keep_down, send_up, keep_up = kernel_call(
        functools.partial(mlp_weights_kernel, n_bits, first),
        [half[0], half[1], half[0], half[1]],
        [sc, after(mid, norm_sums), cot] + mlp_shared + [vecs, up_weight, down_weight],
        smem=(0,),
        hbm={
            **gathered([(1, 0), (2, 1)], [3, 6, 4, 7, 5, 8], rows),
            10: ((width, q_hidden), columns(q_hidden, 1)),
            11: ((q_hidden, width), columns(q_hidden, 0)),
        },
        limit=28,
        flops=2 * 4 * group * width * q_hidden * 4,
        scratch=[
            pltpu.VMEM((4 * group, width), BF16),
            pltpu.VMEM((4 * group, width), BF16),
            pltpu.VMEM((width, q_hidden), F32),
        ],
    )
    send_down, send_up, a1, a2, restored, *came = lax.optimization_barrier(
        (send_down, send_up, a1, a2, restored, *came)
    )
    msg = combine(msg, *came)
    a3 = hop(a1, masks[1])
    b1, b2 = swap(a1), swap(a2)
    recv_down = hop(send_down, 1 << first)

    def attn_scratch(n):
        return [
            pltpu.VMEM((n * group, width), BF16),
            pltpu.VMEM((n * group, width), BF16),
            pltpu.VMEM((n * group, q_cols), BF16),
            pltpu.VMEM((n * group, 3 * q_cols), BF16),
        ]

    def quarter_weights(i):
        return {
            i: ((2, q_cols), columns(q_cols, 1)),
            i + 1: ((3, width, q_cols), columns(q_cols, 1)),
            i + 2: ((q_cols, width), columns(q_cols, 0)),
        }

    (part_attn,) = kernel_call(
        functools.partial(attn_first_kernel, n_dp, [0] + masks[:2]),
        [((width, 4 * q_cols), F32)],
        [sc, got, normed, gattn, a1, a2, b1, b2, qv_bias, w_qkv, out_weight],
        smem=(0,),
        hbm={**gathered([(2, 1), (3, 0)], [4, 6, 5, 7], rows), **quarter_weights(8)},
        limit=24,
        loose=(6, 7),
        flops=2 * 3 * group * width * q_cols * 12,
        scratch=attn_scratch(3),
    )
    a3, recv_down, part_attn = lax.optimization_barrier((a3, recv_down, part_attn))

    def hand_out(*pairs):
        n, w = pairs[0][0].shape
        w *= len(pairs)
        pieces = kernel_call(
            functools.partial(pieces_kernel, len(pairs)),
            [((block, w), F32)] + [((block, w), BF16)] * 3,
            [sc] + [a for pair in pairs for a in pair],
            smem=(0,),
            flops=1 << 26,
            scratch=[pltpu.VMEM((n, w), F32)],
        )
        far_first = [hop(p, m) for p, m in zip(pieces[:0:-1], masks[::-1])]
        return [pieces[0]] + far_first[::-1]

    def clip(msg):
        threshold = clip_tau[0].astype(F32)
        head_factor = jnp.sqrt(threshold / jnp.maximum(msg[-1, : tops.shape[0]], threshold))
        column_factor = jnp.repeat(head_factor, HD)
        clipped_qk = pl.pallas_call(
            clip_kernel,
            grid=(4,),
            out_shape=jax.ShapeDtypeStruct((width, 2, cols), BF16),
            in_specs=[
                pl.BlockSpec((2, width // 4, cols), lambda i: (0, i, 0)),
                pl.BlockSpec((1, cols), lambda i: (0, 0)),
            ],
            out_specs=pl.BlockSpec((width // 4, 2, cols), lambda i: (i, 0, 0)),
            name="clip_kernel",
        )(w_qkv, column_factor.reshape(1, cols))
        return clipped_qk, head_factor, column_factor

    def join_mlp(pieces):
        return kernel_call(join_mlp_kernel, [((block, hidden), F32)], [sc] + pieces, smem=(0,))[0]

    n_steps = len(rs_bits)
    recvs = {0: recv_down}
    sends = {1: send_up}
    keeps = {0: keep_down, 1: keep_up}
    for t in range(1, n_steps + 2):
        active = [i for i in range(3) if 0 <= t - i < n_steps]
        gate = ()
        for i in active:
            if t > i:
                sends[i], keeps[i] = step(t - i, recvs[i], keeps[i])
                gate = (sends[i],)
        for i in active:
            recvs[i] = hop(after(sends[i], *gate), 1 << rs_bits[t - i])
        extra = []
        if t <= n_steps:
            msg = after(msg, *gate)
            came = hop(msg, 1 << later[t - 1])
        if t == 1:
            send_attn, keep_attn = kernel_call(
                functools.partial(attn_weights_kernel, n_bits, first, n_dp, masks[2:]),
                [((width // 2, 4 * q_cols), BF16), ((width // 2, 4 * q_cols), F32)],
                [sc, got, part_attn, a3, swap(a3), qv_bias, w_qkv, out_weight],
                smem=(0,),
                hbm={**gathered([], [3, 4], rows, 0), **quarter_weights(5)},
                limit=20,
                loose=(4,),
                flops=2 * group * width * q_cols * 12,
                scratch=attn_scratch(1) + [pltpu.VMEM((width, 4 * q_cols), F32)],
            )
            sends[2], keeps[2] = send_attn, keep_attn
            out_tokens, grad_tokens = kernel_call(
                restore_kernel,
                [((rows, width), BF16)] * 2,
                [pick, after(restored, *gate)],
                flops=1 << 27,
            )
            extra = [out_tokens, grad_tokens, sends[2]]
        if t >= n_steps:
            mlp_pieces = hand_out((after(keeps[t - n_steps], *gate), recvs[t - n_steps]))
            extra = mlp_pieces[1:]
        if t == n_steps + 1:
            clipped_qk, head_factor, column_factor = clip(msg)
            extra = extra + [clipped_qk, grad_down]
        done = lax.optimization_barrier([recvs[i] for i in active] + [came] + extra)
        recvs.update(zip(active, done))
        if t <= n_steps:
            msg = combine(msg, done[len(active)])
        if t == 1:
            out_tokens, grad_tokens, sends[2] = done[-3:]
        if t == n_steps + 1:
            mlp_pieces[1:], clipped_qk, grad_down = done[-5:-2], done[-2], done[-1]
            grad_up = join_mlp(mlp_pieces)
        if t == n_steps:
            mlp_pieces[1:] = done[-3:]
            grad_down = join_mlp(mlp_pieces)
    attn_pieces = hand_out((keeps[2], recvs[2]))
    msg = after(msg, attn_pieces[0])
    grad_up, *attn_pieces[1:] = lax.optimization_barrier((grad_up, *attn_pieces[1:]))
    grad_down = grad_down.T
    grad_qkv, grad_out = kernel_call(
        join_attn_kernel, [((3, block, cols), F32), ((block, cols), F32)], [sc] + attn_pieces, smem=(0,)
    )
    grad_qkv = jnp.transpose(grad_qkv, (1, 0, 2))
    grad_out = grad_out.T

    theirs = swap(msg).reshape(-1)
    msg = msg.reshape(-1)
    vector_sum = (msg[:n_vec] + theirs[:n_vec]).reshape(6, width)
    own, oth = msg[n_vec:n_sum], theirs[n_vec:n_sum]
    one = jnp.where(core == 0, own, oth)
    two = jnp.where(core == 0, oth, own)
    qv_sum = jnp.stack(
        [
            jnp.concatenate([one[:cols], two[:cols]]),
            jnp.concatenate([one[cols : 2 * cols], two[cols : 2 * cols]]),
        ]
    )
    up_sum = jnp.concatenate([one[2 * cols :], two[2 * cols :]])

    clipped_q_bias = (f(qv_bias[0]) * column_factor).astype(BF16)
    return (
        out_tokens,
        grad_tokens,
        grad_qkv,
        grad_out,
        grad_up,
        grad_down,
        qv_sum,
        up_sum,
        vector_sum,
        head_factor,
        clipped_qk,
        clipped_q_bias,
    )

def solution(mesh):
    placed = (
        P(("dp", "tensor"), None),
        P(("dp", "tensor"), None),
        P(("dp", "tensor")),
        P("dp", None),
        P(),
        P(),
        P(),
        P(None, None, "tensor"),
        P(None, "tensor"),
        P("tensor", None),
        P(),
        P(),
        P(),
        P(None, "tensor"),
        P("tensor"),
        P("tensor", None),
        P(),
    )
    return jax.shard_map(
        local,
        mesh=mesh,
        in_specs=placed,
        out_specs=(
            P(("dp", "tensor"), None),
            P(("dp", "tensor"), None),
            P("dp", None, "tensor"),
            P("tensor", "dp"),
            P("dp", "tensor"),
            P("tensor", "dp"),
            P(),
            P(),
            P(),
            P("tensor"),
            P(None, None, "tensor"),
            P("tensor"),
        ),
        check_vma=False,
    )
```

```python
import functools
import jax
import jax.numpy as jnp
from jax import lax
from jax.experimental import pallas as pl
from jax.experimental.pallas import tpu as pltpu
from jax.sharding import PartitionSpec as P

HD = 64
AG_BITS = (0, 2)
PAD = 128
COST = 1

epsilon = 1e-05
masked_value = -1e30
gelu_coef = 0.7978845608028654
F32 = jnp.float32
BF16 = jnp.bfloat16
I32 = jnp.int32


def f(x):
    return x.astype(F32)


def dot(a, b, ca, cb):
    return lax.dot_general(a, b, (((ca,), (cb,)), ((), ())), preferred_element_type=F32)


def nn(a, b):
    return dot(a, b, 1, 0)


def nt(a, b):
    return dot(a, b, 1, 1)


def tn(a, b):
    return dot(a, b, 0, 0)


def norm_stats(values):
    row_mean = jnp.mean(values, axis=-1, keepdims=True)
    centered = values - row_mean
    variance = jnp.mean(centered * centered, axis=-1, keepdims=True)
    inv = lax.rsqrt(variance + epsilon)
    return centered * inv, inv


def norm_grad(xhat, inv, gain, grad):
    scaled = grad * gain
    a = jnp.mean(scaled, axis=-1, keepdims=True)
    b = jnp.mean(scaled * xhat, axis=-1, keepdims=True)
    return inv * (scaled - a - xhat * b)


def gelu_parts(p):
    p2 = p * p
    th = jnp.tanh(gelu_coef * (p + 0.044715 * p2 * p))
    half = 0.5 * (1.0 + th)
    slope = half + 0.5 * p * (1.0 - th * th) * (gelu_coef * (1.0 + 3.0 * 0.044715 * p2))
    return p * half, slope


def iota(shape, axis):
    return lax.broadcasted_iota(I32, shape, axis)


def place_matrix(ids):
    rows = ids.shape[0]
    return (ids == f(iota((rows, rows), 1))).astype(BF16)


def pair_mask(ends, core, rows):
    group = 2 * rows
    pos_r = (iota((group, 1), 0) + core * rows) & (group - 1)
    pos_c = (iota((1, group), 1) + core * rows) & (group - 1)
    sid_r = sum((pos_r >= e).astype(I32) for e in ends)
    sid_c = sum((pos_c >= e).astype(I32) for e in ends)
    sid_r = jnp.where(pos_r < ends[-1], sid_r, -1)
    same = (sid_r == sid_c).astype(I32) * (pos_c <= pos_r).astype(I32)
    diagonal = (pos_r == pos_c).astype(I32)
    return (same + diagonal) > 0, sid_r >= 0


def half_lanes():
    lane = iota((1, PAD), 1)
    low = (lane < HD).astype(F32)
    return (low.astype(BF16), (1.0 - low).astype(BF16)), (low, 1.0 - low)


def head_probs(q2, k2, lanes, mask):
    s = jnp.where(mask, nt(q2 * lanes, k2) * 0.125, masked_value)
    top = jnp.max(s, axis=-1, keepdims=True)
    e = jnp.exp(s - top)
    total = jnp.sum(e, axis=-1, keepdims=True)
    return e, top, total


def head_grad(q2, k2, v2, gc2, lanes, p):
    gp = nt(gc2 * lanes, v2)
    row_dot = jnp.sum(p * gp, axis=-1, keepdims=True)
    ds = (p * (gp - row_dot)).astype(BF16)
    return nn(ds, k2) * 0.125, tn(ds, q2) * 0.125, tn(p.astype(BF16), gc2)


class Fetched:
    def __init__(self, ref, copies):
        self.ref, self.copies, self.shape = ref, copies, getattr(ref, "shape", None)

    def wait(self, k=None):
        for c in self.copies if k is None else [self.copies[k]]:
            c.wait()
        return self.ref


def whole(shape):
    return shape, lambda src, dst, sc: [(src, dst)]


def kernel_call(body, outs, args, smem=(), hbm=None, flops=0, scratch=(), limit=12, loose=()):
    hbm = hbm or {}
    specs = []
    n_bytes = 0
    for i, a in enumerate(args):
        n_bytes += a.size * a.dtype.itemsize
        space = pl.ANY if i in loose else pltpu.HBM if i in hbm else pltpu.SMEM if i in smem else pltpu.VMEM
        specs.append(pl.BlockSpec(memory_space=space))
    shapes = [jax.ShapeDtypeStruct(s, d) for s, d in outs]
    out_specs = [pl.BlockSpec(memory_space=pltpu.VMEM) for _ in outs]
    args = [pltpu.with_memory_space_constraint(a, pltpu.HBM) if i in hbm and i not in loose else a for i, a in enumerate(args)]
    n_in, n_out, n_scratch = len(args), len(outs), len(scratch)
    extra = []
    own = [i for i, (shape, _) in hbm.items() if shape is not None]
    for i in own:
        extra.append(pltpu.VMEM(hbm[i][0], args[i].dtype))
    n_chunks = {}
    for i, (shape, chunks) in hbm.items():
        n_chunks[i] = getattr(chunks, "count", 1)
        extra.append(pltpu.SemaphoreType.DMA((n_chunks[i],)))

    def run(*refs):
        ins = list(refs[:n_in])
        rest = refs[n_in + n_out + n_scratch :]
        sc = ins[0]
        for j, (i, (_, chunks)) in enumerate(hbm.items()):
            dst = rest[own.index(i)] if i in own else refs[n_in + n_out :]
            sem = rest[len(own) + j]
            copies = [
                pltpu.make_async_copy(a, b, sem.at[k]) for k, (a, b) in enumerate(chunks(ins[i], dst, sc))
            ]
            for c in copies:
                c.start()
            ins[i] = Fetched(dst, copies)
        body(*ins, *refs[n_in : n_in + n_out + n_scratch])

    return pl.pallas_call(
        run,
        out_shape=shapes,
        in_specs=specs,
        out_specs=out_specs,
        scratch_shapes=list(scratch) + extra,
        compiler_params=pltpu.CompilerParams(vmem_limit_bytes=limit << 20),
        cost_estimate=pl.CostEstimate(
            flops=int(flops * COST), transcendentals=0, bytes_accessed=int(n_bytes * COST)
        ),
        name=body.func.__name__ if hasattr(body, "func") else body.__name__,
    )(*args)


def chunked(count, make):
    def chunks(src, dst, sc):
        return [make(src, dst, sc, k) for k in range(count)]

    chunks.count = count
    return chunks


def gathered(own_args, shared_args, rows, start=2):
    spec = {}
    for i, at in own_args:
        spec[i] = (None, chunked(1, lambda src, dst, sc, k, at=at: (src, dst[at].at[pl.ds(0, 2 * rows), :])))
    for j, i in enumerate(shared_args):

        def make(src, dst, sc, k, j=j):
            width = dst[0].shape[1]
            return src.at[:, pl.ds(k * width, width)], dst[k].at[pl.ds((start + j) * rows, rows), :]

        spec[i] = (None, chunked(2, make))
    return spec


def by_row(count):
    return chunked(count, lambda src, dst, sc, k: (src.at[k], dst.at[k]))


def tiles(count, axis):
    def make(src, dst, sc, k):
        at = pl.ds(k * TILE, TILE)
        return (src.at[at, :], dst.at[at, :]) if axis == 0 else (src.at[:, at], dst.at[:, at])

    return chunked(count, make)


def columns(n, axis):
    def chunks(src, dst, sc):
        at = pl.ds(pl.multiple_of(sc[2] * n, n), n)
        if axis == 0:
            return [(src.at[at, :], dst)]
        return [(src.at[(slice(None),) * (len(src.shape) - 1) + (at,)], dst)]

    return chunks


def route_kernel(n_dp, route, lens, tokens, cotangent, msg, pick_out):
    rows, width = tokens.shape
    row = jnp.broadcast_to(f(route.wait()[...]), (rows, rows))
    col = row.T
    group = float(2 * rows)
    dest_r = jnp.floor(row / group)
    dest_c = jnp.floor(col / group)
    before = iota((rows, rows), 0) < iota((rows, rows), 1)
    same = jnp.where(before, (dest_r == dest_c).astype(F32), 0.0)
    rank = dest_r[0:1] * (rows // n_dp) + jnp.sum(same, axis=0, keepdims=True)
    pick = (jnp.broadcast_to(rank, (rows, rows)) == f(iota((rows, rows), 0))).astype(F32)
    place = row - jnp.floor(row / float(rows)) * float(rows)
    ids = jnp.sum(pick * place, axis=1, keepdims=True)
    lane = iota((rows, PAD), 1)
    extra = jnp.where(lane == 0, ids, 0.0)
    lens = f(lens.wait()[...])
    for i in range(4):
        extra = jnp.where(lane == i + 1, lens[:, i : i + 1], extra)
    pick_b = pick.astype(BF16)
    pick_out[...] = pick_b
    msg[:, :width] = nn(pick_b, tokens.wait()[...]).astype(BF16)
    msg[:, 2 * width :] = extra.astype(BF16)
    msg[:, width : 2 * width] = nn(pick_b, cotangent.wait()[...]).astype(BF16)


def ends_of(sc):
    e = [sc[4]]
    for i in range(1, 4):
        e.append(e[-1] + sc[4 + i])
    return e


def attn_kernel(
    sc, mine, other, vecs, w_qkv, qv_bias, w_out, x_out, normed_out, qkv_out, lse_out, top_out, part_out, ctx_out
):
    rows = mine.shape[0]
    width = w_out.shape[1]
    cols = w_out.shape[0]
    for i, half in enumerate((mine, other)):
        put = place_matrix(f(half[:, 2 * width : 2 * width + 1]))
        x = tn(put, half[:, :width])
        s = slice(i * rows, (i + 1) * rows)
        x_out[s, :] = x.astype(BF16)
        xhat, _ = norm_stats(x)
        normed_out[s, :] = (xhat * vecs[0:1, :] + vecs[1:2, :]).astype(BF16)
    normed = normed_out[...]
    qv_bias = qv_bias.wait()
    for c in range(3):
        y = nn(normed, w_qkv.wait(c)[c])
        if c == 0:
            y = y + f(qv_bias[0:1, :])
        if c == 2:
            y = y + f(qv_bias[1:2, :])
        qkv_out[:, c * cols : (c + 1) * cols] = y.astype(BF16)
    mask, live = pair_mask(ends_of(sc), sc[0], rows)
    lanes_b, lanes_f = half_lanes()
    lane = iota((1, PAD), 1)
    lse = jnp.zeros((2 * rows, PAD), F32)
    for pair in range(cols // PAD):
        s = slice(pair * PAD, (pair + 1) * PAD)
        q2 = qkv_out[:, s]
        k2 = qkv_out[:, slice(cols + pair * PAD, cols + (pair + 1) * PAD)]
        v2 = qkv_out[:, slice(2 * cols + pair * PAD, 2 * cols + (pair + 1) * PAD)]
        out = jnp.zeros((2 * rows, PAD), F32)
        for i in range(2):
            e, top, total = head_probs(q2, k2, lanes_b[i], mask)
            probs = (e * (1.0 / total)).astype(BF16)
            out = out + nn(probs, v2) * lanes_f[i]
            h = 2 * pair + i
            lse = jnp.where(lane == h, top + jnp.log(total), lse)
            best = jnp.max(jnp.where(live, top, masked_value), axis=0, keepdims=True)
            top_out[h : h + 1, :] = jnp.broadcast_to(best, (1, PAD))
        ctx_out[:, s] = out.astype(BF16)
    lse_out[...] = lse
    part_out[...] = nn(ctx_out[...], w_out.wait()[...]).astype(BF16)


def middle_kernel(x, part, recv, vecs, mine, other, middle_out, mid_out, cot_out, msg_out):
    rows, width = msg_out.shape[0], x.shape[1]
    for i, half in enumerate((mine, other)):
        s = slice(i * rows, (i + 1) * rows)
        o = slice((1 - i) * rows, (2 - i) * rows)
        put = place_matrix(f(half[:, 2 * width : 2 * width + 1]))
        cot = tn(put, half[:, width : 2 * width]).astype(BF16)
        cot_out[s, :] = cot
        middle = f(x[s, :]) + (f(part[s, :]) + f(recv[o, :])) + vecs[2:3, :]
        middle_out[s, :] = middle
        mhat, _ = norm_stats(middle)
        mid = (mhat * vecs[3:4, :] + vecs[4:5, :]).astype(BF16)
        mid_out[s, :] = mid
        if i == 0:
            msg_out[:, :width] = mid
            msg_out[:, width:] = cot


TILE = 1024


def mlp_kernel(mid, cot, vecs, up, down, gmid_out, mine_out, other_out, sums_out, acc, acc_y):
    width, hidden = up.shape
    rows = mine_out.shape[0]
    per_row = width // TILE
    for t in range(hidden // TILE):
        s = slice(t * TILE, (t + 1) * TILE)
        bias = vecs[6 + t // per_row : 7 + t // per_row, (t % per_row) * TILE : (t % per_row + 1) * TILE]
        act, slope = gelu_parts(nn(mid[...], up.wait(t)[:, s]) + bias)
        gpre = (nt(cot[...], down.wait(t)[s, :]) * slope).astype(BF16)
        sums_out[:, s] = jnp.sum(f(gpre), axis=0, keepdims=True)
        g = nt(gpre, up.ref[:, s])
        y = nn(act.astype(BF16), down.ref[s, :])
        if t == 0:
            acc[...] = g
            acc_y[...] = y
        else:
            acc[...] += g
            acc_y[...] += y
    gmid_out[...] = acc[...].astype(BF16)
    mine_out[...] = acc_y[:rows, :]
    other_out[...] = acc_y[rows:, :].astype(BF16)


def gmid_kernel(part, recv, middle, cot, normed, vecs, gmid_out, gattn_out, sums_out, msg_out):
    rows, width = gmid_out.shape
    msg_out[:, width:] = normed[:rows, :]
    for i in range(2):
        s = slice(i * rows, (i + 1) * rows)
        o = slice((1 - i) * rows, (2 - i) * rows)
        g = f(part[s, :]) + f(recv[o, :])
        mhat, inv = norm_stats(middle[s, :])
        c = f(cot[s, :])
        gm = c + norm_grad(mhat, inv, vecs[3:4, :], g)
        gattn = gm.astype(BF16)
        gattn_out[s, :] = gattn
        if i == 0:
            gmid_out[...] = gm
            msg_out[:, :width] = gattn
            sums_out[0:1, :] = jnp.sum(gm, axis=0, keepdims=True)
            sums_out[1:2, :] = jnp.sum(g * mhat, axis=0, keepdims=True)
            sums_out[2:3, :] = jnp.sum(g, axis=0, keepdims=True)
            sums_out[3:4, :] = jnp.sum(c, axis=0, keepdims=True)
            sums_out[4:8, :] = jnp.zeros((4, sums_out.shape[1]), F32)


def attn_grad_kernel(sc, gattn, w_out, qkv, lse, w_qkv, mine_out, other_out, sums_out, gqkv):
    rows = gattn.shape[0] // 2
    cols = w_out.shape[0]
    mask, _ = pair_mask(ends_of(sc), sc[0], rows)
    gctx = nt(gattn[...], w_out.wait()[...]).astype(BF16)
    lanes_b, lanes_f = half_lanes()
    for pair in range(cols // PAD):
        cut = [slice(c * cols + pair * PAD, c * cols + (pair + 1) * PAD) for c in range(3)]
        q2, k2, v2 = (qkv[:, c] for c in cut)
        gc2 = gctx[:, pair * PAD : (pair + 1) * PAD]
        total = None
        for i in range(2):
            h = 2 * pair + i
            s = jnp.where(mask, nt(q2 * lanes_b[i], k2) * 0.125, masked_value)
            p = jnp.exp(s - lse[:, h : h + 1])
            g3 = [g * lanes_f[i] for g in head_grad(q2, k2, v2, gc2, lanes_b[i], p)]
            total = g3 if total is None else [a + b for a, b in zip(total, g3)]
        for c in range(3):
            g = total[c].astype(BF16)
            gqkv[:, cut[c]] = g
            sums_out[c : c + 1, pair * PAD : (pair + 1) * PAD] = jnp.sum(f(g), axis=0, keepdims=True)
    y = sum(nt(gqkv[:, c * cols : (c + 1) * cols], w_qkv.wait(c)[c]) for c in range(3))
    mine_out[...] = y[:rows]
    other_out[...] = y[rows:].astype(BF16)


def last_kernel(part, recv, x, gmid, middle, y_mine, y_other, vecs, ids, msg_out, sums_out):
    rows, width = part.shape
    put = place_matrix(f(ids[:, 2 * width : 2 * width + 1]))
    res = middle[:rows, :] + (y_mine[...] + f(y_other[...])) + vecs[5:6, :]
    msg_out[:, :width] = nn(put, res.astype(BF16)).astype(BF16)
    g = part[...] + f(recv[...])
    xhat, inv = norm_stats(f(x[:rows, :]))
    grad = (gmid[...] + norm_grad(xhat, inv, vecs[0:1, :], g)).astype(BF16)
    sums_out[0:1, :] = jnp.sum(g * xhat, axis=0, keepdims=True)
    sums_out[1:2, :] = jnp.sum(g, axis=0, keepdims=True)
    msg_out[:, width:] = nn(put, grad).astype(BF16)


def restore_kernel(pick, msg, out, grad):
    width = out.shape[1]
    y = tn(pick[...], msg[...]).astype(BF16)
    out[...] = y[:, :width]
    grad[...] = y[:, width:]


def clip_kernel(w, factor, out):
    for c in range(2):
        out[:, c, :] = (f(w[c]) * factor[...]).astype(BF16)


def run_lengths(bits, block):
    return {b: block << i for i, b in enumerate(sorted(bits))}


def split_rows(src, run, mine, send_out, keep_out, at):
    n = src.shape[0]
    for j in range(n // (2 * run)):
        k = pl.multiple_of(2 * run * j + mine * run, run)
        s = pl.multiple_of(2 * run * j + (1 - mine) * run, run)
        dst = slice(j * run, (j + 1) * run)
        keep_out[dst, at] = src[pl.ds(k, run), :]
        send_out[dst, at] = src[pl.ds(s, run), :].astype(BF16)


def mlp_weights_kernel(
    n_bits, bit, sc, mid, cot, m1, m2, m3, o1, o2, o3, vecs, up, down,
    send_down, keep_down, send_up, keep_up, mids, cots, grad,
):
    for x in (mid, cot, m1, m2, m3, o1, o2, o3):
        x.wait()
    q_hidden = down.shape[0]
    per_row = mids.shape[1] // q_hidden
    bias = jnp.zeros((1, q_hidden), F32)
    for k in range(4):
        part = vecs[6 + k // per_row : 7 + k // per_row, (k % per_row) * q_hidden : (k % per_row + 1) * q_hidden]
        bias = jnp.where(sc[2] == k, part, bias)
    mine = (sc[1] >> bit) & 1
    run = (mids.shape[1] >> n_bits) << bit
    act, slope = gelu_parts(nn(mids[...], up.wait()[...]) + bias)
    every = slice(None)
    grad[...] = tn(cots[...], act.astype(BF16))
    split_rows(grad, run, mine, send_down, keep_down, every)
    gpre = (nt(cots[...], down.wait()[...]) * slope).astype(BF16)
    grad[...] = tn(mids[...], gpre)
    split_rows(grad, run, mine, send_up, keep_up, every)


def attn_quarter(n_dp, masks, sc, ids, qv_bias, w_qkv, w_out, gattns, norms, ctx, gqkv):
    group = norms.shape[0] // len(masks)
    rows = group // 2
    me = sc[1]
    norm4 = norms[...]
    w_qkv, qv_bias = w_qkv.wait(), qv_bias.wait()
    q4 = (nn(norm4, w_qkv[0]) + f(qv_bias[0:1, :])).astype(BF16)
    k4 = nn(norm4, w_qkv[1]).astype(BF16)
    v4 = (nn(norm4, w_qkv[2]) + f(qv_bias[1:2, :])).astype(BF16)
    gc4 = nt(gattns[...], w_out.wait()[...]).astype(BF16)
    lanes_b, lanes_f = half_lanes()
    table = f(ids[:, 2 * norms.shape[1] :])
    from_dp = iota((rows, 1), 0) // (rows // n_dp)
    first = iota((rows, 1), 0) == from_dp * (rows // n_dp)
    for g, bits in enumerate(masks):
        chosen = jnp.where((from_dp == (me ^ bits)) & first, table, 0.0)
        lens = jnp.sum(chosen, axis=0, keepdims=True)
        ends = [lens[:, 1:2]]
        for i in range(2, 5):
            ends.append(ends[-1] + lens[:, i : i + 1])
        mask, _ = pair_mask([e.astype(I32) for e in ends], sc[0], rows)
        s = slice(g * group, (g + 1) * group)
        q2, k2, v2, gc2 = q4[s], k4[s], v4[s], gc4[s]
        out = jnp.zeros((group, PAD), F32)
        total = None
        for i in range(2):
            e, _, denom = head_probs(q2, k2, lanes_b[i], mask)
            p = e * (1.0 / denom)
            out = out + nn(p.astype(BF16), v2) * lanes_f[i]
            g3 = [x * lanes_f[i] for x in head_grad(q2, k2, v2, gc2, lanes_b[i], p)]
            total = g3 if total is None else [a + b for a, b in zip(total, g3)]
        ctx[s, :] = out.astype(BF16)
        for c in range(3):
            gqkv[s, c * PAD : (c + 1) * PAD] = total[c].astype(BF16)


def attn_first_kernel(
    n_dp, masks, sc, ids, nrm, ga, m1, m2, o1, o2, qv_bias, w_qkv, w_out, grad, gattns, norms, ctx, gqkv
):
    for x in (ga, nrm, m1, m2, o1, o2):
        x.wait()
    attn_quarter(n_dp, masks, sc, ids, qv_bias, w_qkv, w_out, gattns, norms, ctx, gqkv)
    grad[:, : 3 * PAD] = tn(norms[...], gqkv[...])
    grad[:, 3 * PAD :] = tn(gattns[...], ctx[...])


def attn_weights_kernel(
    n_bits, bit, n_dp, masks, sc, ids, base, m3, o3, qv_bias, w_qkv, w_out,
    send_out, keep_out, gattns, norms, ctx, gqkv, grad,
):
    m3.wait()
    o3.wait()
    run = (norms.shape[1] >> n_bits) << bit
    attn_quarter(n_dp, masks, sc, ids, qv_bias, w_qkv, w_out, gattns, norms, ctx, gqkv)
    grad[:, : 3 * PAD] = base[:, : 3 * PAD] + tn(norms[...], gqkv[...])
    grad[:, 3 * PAD :] = base[:, 3 * PAD :] + tn(gattns[...], ctx[...])
    split_rows(grad, run, (sc[1] >> bit) & 1, send_out, keep_out, slice(None))


def step_kernel(bit, run, sc, keep, recv, send_out, keep_out, cur):
    cur[...] = keep[...] + f(recv[...])
    split_rows(cur, run, (sc[1] >> bit) & 1, send_out, keep_out, slice(None))


def pieces_kernel(n_pairs, sc, *refs):
    pairs, (own, p1, p2, p3), cur = refs[: 2 * n_pairs], refs[2 * n_pairs : -1], refs[-1]
    n = own.shape[0]
    w = pairs[0].shape[1]
    for i in range(n_pairs):
        cur[:, i * w : (i + 1) * w] = pairs[2 * i][...] + f(pairs[2 * i + 1][...])
    q = sc[2]
    for j, out in enumerate((own, p1, p2, p3)):
        out[...] = cur[pl.ds(pl.multiple_of((q ^ j) * n, n), n), :].astype(out.dtype)


def join_mlp_kernel(sc, own, p1, p2, p3, out):
    w = own.shape[1]
    for j, p in enumerate((own, p1, p2, p3)):
        out[:, pl.ds(pl.multiple_of((sc[2] ^ j) * w, w), w)] = f(p[...])


def join_attn_kernel(sc, own, p1, p2, p3, qkv_out, out_out):
    w = own.shape[1] // 4
    for j, p in enumerate((own, p1, p2, p3)):
        at = pl.ds(pl.multiple_of((sc[2] ^ j) * w, w), w)
        for c in range(3):
            qkv_out[c, :, at] = f(p[:, c * w : (c + 1) * w])
        out_out[:, at] = f(p[:, 3 * w :])


def after(x, *deps):
    return lax.optimization_barrier((x, *deps))[0]


def local(
    tokens,
    cotangent,
    route,
    lengths,
    clip_tau,
    attn_norm_gain,
    attn_norm_bias,
    qkv_weight,
    qv_bias,
    out_weight,
    out_bias,
    mlp_norm_gain,
    mlp_norm_bias,
    up_weight,
    up_bias,
    down_weight,
    down_bias,
):
    n_dp = lax.axis_size("dp")
    n_bits = n_dp.bit_length() - 1
    rs_bits = [b for b in range(n_bits) if b not in AG_BITS]
    masks = [1 << AG_BITS[0], 1 << AG_BITS[1], (1 << AG_BITS[0]) | (1 << AG_BITS[1])]
    me = lax.axis_index("dp")
    core = lax.axis_index("tensor")
    rows, width = tokens.shape
    group = 2 * rows
    cols = qkv_weight.shape[2]
    hidden = up_weight.shape[1]
    q_cols = cols // 4
    q_hidden = hidden // 4
    quarter = ((me >> AG_BITS[0]) & 1) + 2 * ((me >> AG_BITS[1]) & 1)
    sc = jnp.concatenate([jnp.stack([core, me, quarter, core]).astype(I32), lengths[0]])

    def swap(x):
        return lax.ppermute(x, "tensor", [(0, 1), (1, 0)])

    def hop(x, mask):
        return lax.ppermute(x, "dp", [(i, i ^ mask) for i in range(n_dp)])

    def exchange(x):
        return lax.all_to_all(x, "dp", split_axis=0, concat_axis=0, tiled=True)

    def share(own):
        got = [hop(own[:rows], m) for m in masks]
        return got + [swap(g) for g in got]

    w_qkv = jnp.transpose(qkv_weight, (1, 0, 2))
    vecs = jnp.concatenate(
        [attn_norm_gain, attn_norm_bias, out_bias, mlp_norm_gain, mlp_norm_bias, down_bias, up_bias]
    ).astype(F32).reshape(-1, width)

    msg, pick = kernel_call(
        functools.partial(route_kernel, n_dp),
        [((rows, 2 * width + PAD), BF16), ((rows, rows), BF16)],
        [route.reshape(1, rows), lengths, tokens, cotangent],
        hbm={0: whole((1, rows)), 1: whole(lengths.shape), 2: whole(tokens.shape), 3: whole(tokens.shape)},
        flops=4 * rows * rows * width,
    )
    got = after(exchange(msg), vecs, sc)
    other = swap(got)
    x, normed, qkv, lse, tops, part = kernel_call(
        attn_kernel,
        [
            ((group, width), BF16),
            ((group, width), BF16),
            ((group, 3 * cols), BF16),
            ((group, PAD), F32),
            ((cols // HD, PAD), F32),
            ((group, width), BF16),
        ],
        [sc, got, other, vecs, w_qkv, qv_bias, out_weight],
        smem=(0,),
        hbm={4: (w_qkv.shape, by_row(3)), 5: whole(qv_bias.shape), 6: whole(out_weight.shape)},
        flops=2 * group * width * 4 * cols * 3,
        scratch=[pltpu.VMEM((group, cols), BF16)],
        limit=20,
    )
    middle, mid, cot, msg_mlp = kernel_call(
        middle_kernel,
        [((group, width), F32), ((group, width), BF16), ((group, width), BF16), ((rows, 2 * width), BF16)],
        [x, part, swap(part), vecs, got, other],
        flops=1 << 28,
    )
    m1, m2 = (hop(msg_mlp, m) for m in masks[:2])
    gmid_part, mlp_mine, mlp_other, up_sums = kernel_call(
        mlp_kernel,
        [((group, width), BF16), ((rows, width), F32), ((rows, width), BF16), ((1, hidden), F32)],
        [mid, cot, vecs, up_weight, down_weight],
        hbm={3: (up_weight.shape, tiles(hidden // TILE, 1)), 4: (down_weight.shape, tiles(hidden // TILE, 0))},
        flops=2 * group * width * hidden * 4,
        scratch=[pltpu.VMEM((group, width), F32), pltpu.VMEM((group, width), F32)],
        limit=24,
    )
    gmid_part, m1, m2 = lax.optimization_barrier((gmid_part, m1, m2))
    m3 = hop(m2, masks[0])
    o1, o2 = swap(m1), swap(m2)
    gmid_recv = swap(gmid_part)
    gmid, gattn, mid_sums, msg_attn = kernel_call(
        gmid_kernel,
        [((rows, width), F32), ((group, width), BF16), ((8, width), F32), ((rows, 2 * width), BF16)],
        [gmid_part, gmid_recv, middle, cot, normed, vecs],
        flops=1 << 28,
    )
    gn_mine, gn_other, qkv_sums = kernel_call(
        attn_grad_kernel,
        [((rows, width), F32), ((rows, width), BF16), ((3, cols), F32)],
        [sc, gattn, out_weight, qkv, lse, w_qkv],
        smem=(0,),
        hbm={2: whole(out_weight.shape), 5: (w_qkv.shape, by_row(3))},
        flops=2 * group * width * 4 * cols * 3,
        scratch=[pltpu.VMEM((group, 3 * cols), BF16)],
        limit=20,
    )
    gn_other, m3, o1, o2 = lax.optimization_barrier((gn_other, m3, o1, o2))
    gn_recv = swap(gn_other)
    msg_attn = after(msg_attn, gn_other)
    a1, a2 = (hop(msg_attn, m) for m in masks[:2])
    mlp_shared = [m1, m2, m3, o1, o2, swap(m3)]
    back, norm_sums = kernel_call(
        last_kernel,
        [((rows, 2 * width), BF16), ((2, width), F32)],
        [gn_mine, gn_recv, x, gmid, middle, mlp_mine, swap(mlp_other), vecs, got],
        flops=1 << 28,
    )

    n_vec = 6 * width
    sums = jnp.concatenate(
        [
            norm_sums.reshape(-1),
            mid_sums[:4].reshape(-1),
            qkv_sums[0],
            qkv_sums[2],
            up_sums.reshape(-1),
        ]
    )
    n_sum = sums.size
    msg = jnp.concatenate([sums, jnp.pad(tops[:, 0], (0, PAD - tops.shape[0]))]).reshape(-1, PAD)
    is_top = iota(msg.shape, 0) == n_sum // PAD

    def combine(msg, *came):
        return functools.reduce(lambda a, b: jnp.where(is_top, jnp.maximum(a, b), a + b), (msg, *came))

    near = [1 << b for b in rs_bits[:2]]
    came = [hop(msg, m) for m in [near[0] | near[1]] + near]
    later = [b for b in range(n_bits) if b not in rs_bits[:2]]
    restored = exchange(back)

    block = width // n_dp
    first = rs_bits[0]
    def step(i, recv, keep):
        n, w = keep.shape
        left = [b for b in range(n_bits) if b not in rs_bits[:i]]
        run = run_lengths(left, block)[rs_bits[i]]
        return kernel_call(
            functools.partial(step_kernel, rs_bits[i], run),
            [((n // 2, w), BF16), ((n // 2, w), F32)],
            [sc, keep, recv],
            smem=(0,),
            flops=1 << 26,
            scratch=[pltpu.VMEM((n, w), F32)],
        )

    half = ((width // 2, q_hidden), BF16), ((width // 2, q_hidden), F32)
    send_down, keep_down, send_up, keep_up = kernel_call(
        functools.partial(mlp_weights_kernel, n_bits, first),
        [half[0], half[1], half[0], half[1]],
        [sc, after(mid, norm_sums), cot] + mlp_shared + [vecs, up_weight, down_weight],
        smem=(0,),
        hbm={
            **gathered([(1, 0), (2, 1)], [3, 6, 4, 7, 5, 8], rows),
            10: ((width, q_hidden), columns(q_hidden, 1)),
            11: ((q_hidden, width), columns(q_hidden, 0)),
        },
        limit=28,
        flops=2 * 4 * group * width * q_hidden * 4,
        scratch=[
            pltpu.VMEM((4 * group, width), BF16),
            pltpu.VMEM((4 * group, width), BF16),
            pltpu.VMEM((width, q_hidden), F32),
        ],
    )
    send_down, send_up, a1, a2, restored, *came = lax.optimization_barrier(
        (send_down, send_up, a1, a2, restored, *came)
    )
    msg = combine(msg, *came)
    a3 = hop(a1, masks[1])
    b1, b2 = swap(a1), swap(a2)
    recv_down = hop(send_down, 1 << first)

    def attn_scratch(n):
        return [
            pltpu.VMEM((n * group, width), BF16),
            pltpu.VMEM((n * group, width), BF16),
            pltpu.VMEM((n * group, q_cols), BF16),
            pltpu.VMEM((n * group, 3 * q_cols), BF16),
        ]

    def quarter_weights(i):
        return {
            i: ((2, q_cols), columns(q_cols, 1)),
            i + 1: ((3, width, q_cols), columns(q_cols, 1)),
            i + 2: ((q_cols, width), columns(q_cols, 0)),
        }

    (part_attn,) = kernel_call(
        functools.partial(attn_first_kernel, n_dp, [0] + masks[:2]),
        [((width, 4 * q_cols), F32)],
        [sc, got, normed, gattn, a1, a2, b1, b2, qv_bias, w_qkv, out_weight],
        smem=(0,),
        hbm={**gathered([(2, 1), (3, 0)], [4, 6, 5, 7], rows), **quarter_weights(8)},
        limit=24,
        loose=(6, 7),
        flops=2 * 3 * group * width * q_cols * 12,
        scratch=attn_scratch(3),
    )
    a3, recv_down, part_attn = lax.optimization_barrier((a3, recv_down, part_attn))

    def hand_out(*pairs):
        n, w = pairs[0][0].shape
        w *= len(pairs)
        pieces = kernel_call(
            functools.partial(pieces_kernel, len(pairs)),
            [((block, w), F32)] + [((block, w), BF16)] * 3,
            [sc] + [a for pair in pairs for a in pair],
            smem=(0,),
            flops=1 << 26,
            scratch=[pltpu.VMEM((n, w), F32)],
        )
        far_first = [hop(p, m) for p, m in zip(pieces[:0:-1], masks[::-1])]
        return [pieces[0]] + far_first[::-1]

    def clip(msg):
        threshold = clip_tau[0].astype(F32)
        head_factor = jnp.sqrt(threshold / jnp.maximum(msg[-1, : tops.shape[0]], threshold))
        column_factor = jnp.repeat(head_factor, HD)
        clipped_qk = pl.pallas_call(
            clip_kernel,
            grid=(4,),
            out_shape=jax.ShapeDtypeStruct((width, 2, cols), BF16),
            in_specs=[
                pl.BlockSpec((2, width // 4, cols), lambda i: (0, i, 0)),
                pl.BlockSpec((1, cols), lambda i: (0, 0)),
            ],
            out_specs=pl.BlockSpec((width // 4, 2, cols), lambda i: (i, 0, 0)),
            name="clip_kernel",
        )(w_qkv, column_factor.reshape(1, cols))
        return clipped_qk, head_factor, column_factor

    def join_mlp(pieces):
        return kernel_call(join_mlp_kernel, [((block, hidden), F32)], [sc] + pieces, smem=(0,))[0]

    n_steps = len(rs_bits)
    recvs = {0: recv_down}
    sends = {1: send_up}
    keeps = {0: keep_down, 1: keep_up}
    for t in range(1, n_steps + 2):
        active = [i for i in range(3) if 0 <= t - i < n_steps]
        gate = ()
        for i in active:
            if t > i:
                sends[i], keeps[i] = step(t - i, recvs[i], keeps[i])
                gate = (sends[i],)
        for i in active:
            recvs[i] = hop(after(sends[i], *gate), 1 << rs_bits[t - i])
        extra = []
        if t <= n_steps:
            msg = after(msg, *gate)
            came = hop(msg, 1 << later[t - 1])
        if t == 1:
            send_attn, keep_attn = kernel_call(
                functools.partial(attn_weights_kernel, n_bits, first, n_dp, masks[2:]),
                [((width // 2, 4 * q_cols), BF16), ((width // 2, 4 * q_cols), F32)],
                [sc, got, part_attn, a3, swap(a3), qv_bias, w_qkv, out_weight],
                smem=(0,),
                hbm={**gathered([], [3, 4], rows, 0), **quarter_weights(5)},
                limit=20,
                loose=(4,),
                flops=2 * group * width * q_cols * 12,
                scratch=attn_scratch(1) + [pltpu.VMEM((width, 4 * q_cols), F32)],
            )
            sends[2], keeps[2] = send_attn, keep_attn
            out_tokens, grad_tokens = kernel_call(
                restore_kernel,
                [((rows, width), BF16)] * 2,
                [pick, after(restored, *gate)],
                flops=1 << 27,
            )
            extra = [out_tokens, grad_tokens, sends[2]]
        if t >= n_steps:
            mlp_pieces = hand_out((after(keeps[t - n_steps], *gate), recvs[t - n_steps]))
            extra = mlp_pieces[1:]
        if t == n_steps + 1:
            clipped_qk, head_factor, column_factor = clip(msg)
            extra = [extra[0], clipped_qk, grad_down]
        done = lax.optimization_barrier([recvs[i] for i in active] + [came] + extra)
        recvs.update(zip(active, done))
        if t <= n_steps:
            msg = combine(msg, done[len(active)])
        if t == 1:
            out_tokens, grad_tokens, sends[2] = done[-3:]
        if t == n_steps + 1:
            mlp_pieces[1], clipped_qk, grad_down = done[-3:]
            grad_up = join_mlp(mlp_pieces)
        if t == n_steps:
            mlp_pieces[1:] = done[-3:]
            grad_down = join_mlp(mlp_pieces)
    attn_pieces = hand_out((keeps[2], recvs[2]))
    msg = after(msg, attn_pieces[0])
    grad_up, *attn_pieces[1:] = lax.optimization_barrier((grad_up, *attn_pieces[1:]))
    grad_down = grad_down.T
    grad_qkv, grad_out = kernel_call(
        join_attn_kernel, [((3, block, cols), F32), ((block, cols), F32)], [sc] + attn_pieces, smem=(0,)
    )
    grad_qkv = jnp.transpose(grad_qkv, (1, 0, 2))
    grad_out = grad_out.T

    theirs = swap(msg).reshape(-1)
    msg = msg.reshape(-1)
    vector_sum = (msg[:n_vec] + theirs[:n_vec]).reshape(6, width)
    own, oth = msg[n_vec:n_sum], theirs[n_vec:n_sum]
    one = jnp.where(core == 0, own, oth)
    two = jnp.where(core == 0, oth, own)
    qv_sum = jnp.stack(
        [
            jnp.concatenate([one[:cols], two[:cols]]),
            jnp.concatenate([one[cols : 2 * cols], two[cols : 2 * cols]]),
        ]
    )
    up_sum = jnp.concatenate([one[2 * cols :], two[2 * cols :]])

    clipped_q_bias = (f(qv_bias[0]) * column_factor).astype(BF16)
    return (
        out_tokens,
        grad_tokens,
        grad_qkv,
        grad_out,
        grad_up,
        grad_down,
        qv_sum,
        up_sum,
        vector_sum,
        head_factor,
        clipped_qk,
        clipped_q_bias,
    )

def solution(mesh):
    placed = (
        P(("dp", "tensor"), None),
        P(("dp", "tensor"), None),
        P(("dp", "tensor")),
        P("dp", None),
        P(),
        P(),
        P(),
        P(None, None, "tensor"),
        P(None, "tensor"),
        P("tensor", None),
        P(),
        P(),
        P(),
        P(None, "tensor"),
        P("tensor"),
        P("tensor", None),
        P(),
    )
    return jax.shard_map(
        local,
        mesh=mesh,
        in_specs=placed,
        out_specs=(
            P(("dp", "tensor"), None),
            P(("dp", "tensor"), None),
            P("dp", None, "tensor"),
            P("tensor", "dp"),
            P("dp", "tensor"),
            P("tensor", "dp"),
            P(),
            P(),
            P(),
            P("tensor"),
            P(None, None, "tensor"),
            P("tensor"),
        ),
        check_vma=False,
    )
```
